32 devices in a mesh: fsdp: 16 (over z, y, core), dp: 2 (over x).
Axes of the slice: x: 2, y: 2, z: 4, core: 2. Of those that a mesh axis runs over, the one named last changes fastest.
Arguments:
- tokens: bfloat16 [32, 256, 1152], P(('fsdp', 'dp')), may hold values from -12 to 12, as said below
- cond: bfloat16 [32, 1152], P(('fsdp', 'dp')), may hold values from -6 to 6
- segment_ids: int32 [32, 256], P(('fsdp', 'dp')), may hold values from 0 to 7, as said below
- ada_weight: bfloat16 [1152, 6912], P('fsdp'), may hold values from -0.1875 to 0.1875
- ada_bias: bfloat16 [6912], P('fsdp'), may hold values from -1 to 1
- qkv_weight: bfloat16 [1152, 3456], P('fsdp'), may hold values from -0.1875 to 0.1875
- qv_bias: bfloat16 [2304], P('fsdp'), may hold values from -1 to 1
- proj_weight: bfloat16 [1152, 1152], P('fsdp'), may hold values from -0.75 to 0.75
- proj_bias: bfloat16 [1152], P('fsdp'), may hold values from -1 to 1
- fc1_weight: bfloat16 [1152, 4608], P('fsdp'), may hold values from -0.1875 to 0.1875
- fc1_bias: bfloat16 [4608], P('fsdp'), may hold values from -1 to 1
- fc2_weight: bfloat16 [4608, 1152], P('fsdp'), may hold values from -0.09375 to 0.09375
- fc2_bias: bfloat16 [1152], P('fsdp'), may hold values from -1 to 1
- out_grad: bfloat16 [32, 256, 1152], P(('fsdp', 'dp')), may hold values from -6 to 6
Outputs:
- output: bfloat16 [32, 256, 1152], P(('fsdp', 'dp'))
- tokens_grad: bfloat16 [32, 256, 1152], P(('fsdp', 'dp'))
- ada_weight_grad: float32 [1152, 6912], P('fsdp')
- ada_bias_grad: float32 [6912], P('fsdp')
- qkv_weight_grad: float32 [1152, 3456], P('fsdp')
- qv_bias_grad: float32 [2304], P('fsdp')
- proj_weight_grad: float32 [1152, 1152], P('fsdp')
- proj_bias_grad: float32 [1152], P('fsdp')
- fc1_weight_grad: float32 [1152, 4608], P('fsdp')
- fc1_bias_grad: float32 [4608], P('fsdp')
- fc2_weight_grad: float32 [4608, 1152], P('fsdp')
- fc2_bias_grad: float32 [1152], P('fsdp')
The draws below stay inside these ranges and needn't reach their ends.
Inputs may be any that keep to these rules, and one draw needn't show every extreme that they name: `segment_ids`: each row holds whole images one after another, numbered from 0 in order: eight images of 32 tokens, or two of 128 tokens, or one of 128 tokens among four of 32 tokens. Some row holds eight images and some row holds two. `tokens`: token features.
All inputs are finite; a program needn't handle non-finite values.
Results may differ from the reference program's by a relative error of at most 0.02.
The reference program's roundings to bfloat16 on the way count: a program that leaves them out, or rounds other values in their place, can miss the bound.
Values may be sent and summed in bfloat16 or wider, within the bound.
A program may use at most 384 MiB of HBM per device.

```python
import math
import jax
import jax.numpy as jnp
from jax import lax

D = 1152
HEADS = 16
HEAD_DIM = 72
FF = 4608
SEQ = 256
ROWS = 32


def draw_tokens(key, part):
    key_scale, key_value = jax.random.split(key, 2)
    scales = jnp.exp(jax.random.uniform(key_scale, (ROWS, SEQ, 1), jnp.float32, jnp.log(0.3), jnp.log(3.0)))
    values_drawn = jax.random.normal(key_value, (ROWS, SEQ, D), jnp.float32)
    values_drawn = jnp.clip(values_drawn, -4.0, 4.0)
    return (values_drawn * scales).astype(jnp.bfloat16)


def draw_segment_ids(key, part):
    key_large, key_spot, key_pick = jax.random.split(jax.random.fold_in(key, 17), 3)
    large_count = jax.random.randint(key_large, (ROWS,), 0, 3)
    picked = jax.random.permutation(key_pick, ROWS)
    large_count = large_count.at[picked[0]].set(0).at[picked[1]].set(2)
    spots = jax.random.randint(key_spot, (ROWS,), 0, 5)[:, None]
    units = jnp.arange(8, dtype=jnp.int32)[None, :]
    single = jnp.where(units < spots, units, jnp.where(units < spots + 4, spots, units - 3))
    counts = large_count[:, None]
    unit_ids = jnp.where(counts == 0, units, jnp.where(counts == 2, units // 4, single))
    return jnp.repeat(unit_ids, SEQ // 8, axis=1).astype(jnp.int32)


def shard_levels(own_key, extent, shards, smallest, high):
    gain = 1.0
    for axis_at, blocks in shards:
        heights = jax.random.uniform(jax.random.fold_in(jax.random.fold_in(own_key, 6), axis_at), (blocks,), jnp.float32, smallest / len(shards), high / len(shards))
        gain = gain * jnp.repeat(jnp.exp(heights), extent[axis_at] // blocks).reshape((-1,) + (1,) * (len(extent) - 1 - axis_at))
    return gain


def noise(key, shape, deviation, bound, cuts=(), kind=jnp.bfloat16):
    entries = jax.random.normal(key, shape, jnp.float32) * deviation
    if len(cuts) > 0:
        entries = shard_levels(key, shape, cuts, -0.22, 0.18) * entries
    return jnp.clip(entries, min=-bound, max=bound).astype(kind)


def setup_inputs(seed: int = 0) -> dict:
    splits = jax.random.split(jax.random.key(seed), 15)
    tokens = draw_tokens(jax.random.fold_in(splits[14], 71), 0)
    cond = noise(splits[1], (ROWS, D), 1.0, 6.0, ((0, 32),))
    segment_ids = draw_segment_ids(jax.random.fold_in(splits[14], 71), 0)
    ada_weight = noise(splits[3], (D, 6 * D), D ** -0.5, 0.1875, ((0, 16),))
    ada_bias = noise(splits[4], (6 * D,), 0.2, 1.0, ((0, 16),))
    qkv_weight = noise(splits[5], (D, 3 * D), D ** -0.5, 0.1875, ((0, 16),))
    qv_bias = noise(splits[6], (2 * D,), 0.2, 1.0, ((0, 16),))
    proj_weight = noise(splits[7], (D, D), (D // 16) ** -0.5, 0.75, ((0, 16),))
    proj_bias = noise(splits[8], (D,), 0.2, 1.0, ((0, 16),))
    fc1_weight = noise(splits[9], (D, FF), D ** -0.5, 0.1875, ((0, 16),))
    fc1_bias = noise(splits[10], (FF,), 0.2, 1.0, ((0, 16),))
    fc2_weight = noise(splits[11], (FF, D), FF ** -0.5, 0.09375, ((0, 16),))
    fc2_bias = noise(splits[12], (D,), 0.2, 1.0, ((0, 16),))
    out_grad = noise(splits[13], (ROWS, SEQ, D), 1.0, 6.0, ((0, 32),))
    return {"tokens": tokens, "cond": cond, "segment_ids": segment_ids, "ada_weight": ada_weight, "ada_bias": ada_bias, "qkv_weight": qkv_weight, "qv_bias": qv_bias, "proj_weight": proj_weight, "proj_bias": proj_bias, "fc1_weight": fc1_weight, "fc1_bias": fc1_bias, "fc2_weight": fc2_weight, "fc2_bias": fc2_bias, "out_grad": out_grad}


@jax.custom_vjp
def low(v):
    return lax.optimization_barrier(v.astype(jnp.bfloat16)).astype(jnp.float32)

@jax.custom_vjp
def low_back(v):
    return v

def low_keep(v):
    return (low(v), None)

def low_pass(kept, grad):
    return (grad,)

def back_keep(v):
    return (v, None)

def back_low(kept, grad):
    return (low(grad),)
low.defvjp(low_keep, low_pass)
low_back.defvjp(back_keep, back_low)
highest = lax.Precision.HIGHEST
root_half = 0.7978845608028654

def product(left, right):
    return jnp.matmul(left, right, precision=highest)

def layer_norm(stream):
    centre = lax.optimization_barrier(jnp.mean(stream, axis=-1, keepdims=True))
    centred = stream - centre
    spread = lax.optimization_barrier(jnp.mean(centred * centred, axis=-1, keepdims=True))
    return centred * lax.rsqrt(spread + 1e-06)

def gelu_tanh(stream):
    return 0.5 * stream * (1.0 + jnp.tanh(root_half * (stream + 0.044715 * stream * stream * stream)))

def block_forward(stream, cond_rows, segments, ada_w, ada_b, qkv_w, qv_b, proj_w, proj_b, fc1_w, fc1_b, fc2_w, fc2_b):
    group_size, seq_len, model_width = stream.shape
    head_scale = HEAD_DIM ** (-0.5)
    cond_act = low(cond_rows / (1.0 + jnp.exp(-cond_rows)))
    modulation = low_back(product(cond_act, ada_w) + ada_b)
    pieces = [modulation[:, None, section * model_width:(section + 1) * model_width] for section in range(6)]
    shift_one, scale_one, gate_one, shift_two, scale_two, gate_two = pieces
    hidden_one = low(layer_norm(stream) * (1.0 + scale_one) + shift_one)
    zero_bias = jnp.zeros((model_width,), jnp.float32)
    qkv_bias = jnp.concatenate([qv_b[:model_width], zero_bias, qv_b[model_width:]])
    projected = low(low_back(product(hidden_one, qkv_w) + qkv_bias))
    shaped = projected.reshape(group_size, seq_len, 3, HEADS, HEAD_DIM)
    queries = shaped[:, :, 0]
    keys_all = shaped[:, :, 1]
    values_all = shaped[:, :, 2]
    scores = low_back(jnp.einsum('gqhd,gkhd->ghqk', queries, keys_all, precision=highest) * head_scale)
    same_doc = segments[:, None, :, None] == segments[:, None, None, :]
    scores = jnp.where(same_doc, scores, -1e+30)
    top_score = lax.optimization_barrier(jnp.max(scores, axis=-1, keepdims=True))
    exp_scores = jnp.exp(scores - top_score)
    probabilities = low(exp_scores / lax.optimization_barrier(jnp.sum(exp_scores, axis=-1, keepdims=True)))
    mixed_heads = jnp.einsum('ghqk,gkhd->gqhd', probabilities, values_all, precision=highest)
    mixed_heads = low(low_back(mixed_heads.reshape(group_size, seq_len, model_width)))
    branch_one = low_back(product(mixed_heads, proj_w) + proj_b)
    resid_one = stream + gate_one * branch_one
    hidden_two = low(layer_norm(resid_one) * (1.0 + scale_two) + shift_two)
    pre_act = low_back(product(hidden_two, fc1_w) + fc1_b)
    active = low(gelu_tanh(pre_act))
    branch_two = low_back(product(active, fc2_w) + fc2_b)
    return resid_one + gate_two * branch_two

def reference(tokens, cond, segment_ids, ada_weight, ada_bias, qkv_weight, qv_bias, proj_weight, proj_bias, fc1_weight, fc1_bias, fc2_weight, fc2_bias, out_grad):
    group_size = math.gcd(ROWS, max(1, 4096 // SEQ))
    steps_count = ROWS // group_size
    params = tuple((array_in.astype(jnp.float32) for array_in in (ada_weight, ada_bias, qkv_weight, qv_bias, proj_weight, proj_bias, fc1_weight, fc1_bias, fc2_weight, fc2_bias)))

    def grouped(array_in):
        return array_in.reshape((steps_count, group_size) + array_in.shape[1:])

    def one_group(totals, inputs_group):
        stream, cond_rows, segments, cotangent = inputs_group

        def apply_block(stream_in, *weights_in):
            return block_forward(stream_in, cond_rows, segments, *weights_in)
        result, pullback = jax.vjp(apply_block, stream, *params)
        gradients = pullback(cotangent)
        updated = tuple((running + increment for running, increment in zip(totals, gradients[1:])))
        return (updated, (result.astype(jnp.bfloat16), gradients[0].astype(jnp.bfloat16)))
    zero_start = tuple((jnp.zeros_like(array_in) for array_in in params))
    sweep_in = (grouped(tokens.astype(jnp.float32)), grouped(cond.astype(jnp.float32)), grouped(segment_ids), grouped(out_grad.astype(jnp.float32)))
    totals, (outputs, input_grads) = lax.scan(one_group, zero_start, sweep_in)
    return (outputs.reshape(ROWS, SEQ, D), input_grads.reshape(ROWS, SEQ, D), totals[0], totals[1], totals[2], totals[3], totals[4], totals[5], totals[6], totals[7], totals[8], totals[9])
```

```python
import jax
import jax.numpy as jnp
from jax import lax
from jax.sharding import PartitionSpec as P

HEADS = 16
HEAD_DIM = 72


root_half = 0.7978845608028654
norm_eps = 1e-06
masked_score = -1e30


def gelu_tanh(stream):
    return (
        0.5 * stream * (1.0 + jnp.tanh(root_half * (stream + 0.044715 * stream * stream * stream)))
    )


def gelu_slope(stream):
    tanh_inner = jnp.tanh(root_half * (stream + 0.044715 * stream * stream * stream))
    return 0.5 * (1.0 + tanh_inner) + 0.5 * stream * (1.0 - tanh_inner * tanh_inner) * root_half * (
        1.0 + 3.0 * 0.044715 * stream * stream
    )


def normalize(stream):
    centre = jnp.mean(stream, axis=-1, keepdims=True)
    centred = stream - centre
    inv_std = lax.rsqrt(jnp.mean(centred * centred, axis=-1, keepdims=True) + norm_eps)
    return (centred * inv_std, inv_std)


def normalize_back(incoming, normed, inv_std):
    return inv_std * (
        incoming
        - jnp.mean(incoming, axis=-1, keepdims=True)
        - normed * jnp.mean(incoming * normed, axis=-1, keepdims=True)
    )


def head_scores(projected, same_doc, head_index, model_width):
    query_part = lax.dynamic_slice_in_dim(projected, head_index * HEAD_DIM, HEAD_DIM, 1)
    key_part = lax.dynamic_slice_in_dim(projected, model_width + head_index * HEAD_DIM, HEAD_DIM, 1)
    value_part = lax.dynamic_slice_in_dim(
        projected, 2 * model_width + head_index * HEAD_DIM, HEAD_DIM, 1
    )
    raw_scores = jnp.einsum(
        "qd,kd->qk", query_part, key_part, preferred_element_type=jnp.float32
    ) * HEAD_DIM ** (-0.5)
    return (jnp.where(same_doc, raw_scores, masked_score), query_part, key_part, value_part)


def merge_heads(stacked, model_width):
    return jnp.transpose(stacked, (1, 0, 2)).reshape(stacked.shape[1], model_width)


def attend_row(projected, segments_row, model_width):
    same_doc = segments_row[:, None] == segments_row[None, :]

    def one_head(head_index):
        scores, query_part, key_part, value_part = head_scores(
            projected, same_doc, head_index, model_width
        )
        top_score = jnp.max(scores, axis=-1, keepdims=True)
        exp_scores = jnp.exp(scores - top_score)
        denominator = jnp.sum(exp_scores, axis=-1, keepdims=True)
        probabilities = (exp_scores / denominator).astype(jnp.bfloat16)
        mixed_heads = jnp.dot(probabilities, value_part, preferred_element_type=jnp.float32)
        return (mixed_heads, (top_score + jnp.log(denominator))[:, 0])

    mixed_heads, log_total = lax.map(one_head, jnp.arange(HEADS))
    return (merge_heads(mixed_heads, model_width).astype(jnp.bfloat16), log_total)


def attend_back(projected, segments_row, log_total, d_mixed, model_width):
    same_doc = segments_row[:, None] == segments_row[None, :]
    head_scale = HEAD_DIM ** (-0.5)

    def one_head(head_index):
        scores, query_part, key_part, value_part = head_scores(
            projected, same_doc, head_index, model_width
        )
        d_head = lax.dynamic_slice_in_dim(d_mixed, head_index * HEAD_DIM, HEAD_DIM, 1)
        lse_row = lax.dynamic_index_in_dim(log_total, head_index, 0, keepdims=False)
        probabilities = jnp.exp(scores - lse_row[:, None])
        prob_low = probabilities.astype(jnp.bfloat16)
        d_probs = jnp.einsum("qd,kd->qk", d_head, value_part, preferred_element_type=jnp.float32)
        d_value = jnp.einsum("qk,qd->kd", prob_low, d_head, preferred_element_type=jnp.float32)
        d_scores = (
            probabilities * (d_probs - jnp.sum(d_probs * probabilities, axis=-1, keepdims=True))
        ).astype(jnp.bfloat16)
        d_query = (
            jnp.einsum("qk,kd->qd", d_scores, key_part, preferred_element_type=jnp.float32)
            * head_scale
        )
        d_key = (
            jnp.einsum("qk,qd->kd", d_scores, query_part, preferred_element_type=jnp.float32)
            * head_scale
        )
        return (d_query, d_key, d_value)

    d_query, d_key, d_value = lax.map(one_head, jnp.arange(HEADS))
    merged = [
        merge_heads(d_query, model_width),
        merge_heads(d_key, model_width),
        merge_heads(d_value, model_width),
    ]
    return jnp.concatenate(merged, axis=-1).astype(jnp.bfloat16)


def on_device(
    tokens,
    cond,
    segment_ids,
    ada_weight,
    ada_bias,
    qkv_weight,
    qv_bias,
    proj_weight,
    proj_bias,
    fc1_weight,
    fc1_bias,
    fc2_weight,
    fc2_bias,
    out_grad,
):
    row_count, seq_len, model_width = tokens.shape
    ff_width = fc1_weight.shape[1]
    stream = tokens.astype(jnp.float32)
    cond_float = cond.astype(jnp.float32)
    cond_act = (cond_float / (1.0 + jnp.exp(-cond_float))).astype(jnp.bfloat16)
    fsdp_at, dp_at = lax.axis_index("fsdp"), lax.axis_index("dp")
    dp_size = lax.axis_size("dp")
    slice_width, bias_width = ada_weight.shape[0], ada_bias.shape[0]
    act_all = lax.all_gather(cond_act, ("fsdp", "dp"), axis=0, tiled=True)
    act_mine = lax.dynamic_slice_in_dim(act_all, fsdp_at * slice_width, slice_width, 1)
    partial = jnp.dot(act_mine, ada_weight, preferred_element_type=jnp.float32)
    bias_row = lax.dynamic_update_slice_in_dim(
        jnp.zeros((6 * model_width,), jnp.float32),
        ada_bias.astype(jnp.float32),
        fsdp_at * bias_width,
        0,
    )
    partial = (partial + bias_row).reshape(-1, dp_size, row_count, 6 * model_width)
    partial = lax.dynamic_index_in_dim(partial, dp_at, 1, keepdims=False)
    modulation = lax.psum_scatter(
        partial.reshape(-1, 6 * model_width), "fsdp", scatter_dimension=0, tiled=True
    )
    pieces = [
        modulation[:, None, section * model_width : (section + 1) * model_width]
        for section in range(6)
    ]
    shift_one, scale_one, gate_one, shift_two, scale_two, gate_two = pieces
    qkv_full, qv_bias_full, proj_full, proj_bias_full = (
        lax.all_gather(qkv_weight, "fsdp", axis=0, tiled=True),
        lax.all_gather(qv_bias, "fsdp", axis=0, tiled=True),
        lax.all_gather(proj_weight, "fsdp", axis=0, tiled=True),
        lax.all_gather(proj_bias, "fsdp", axis=0, tiled=True),
    )
    normed_one, inv_one = normalize(stream)
    hidden_one = (normed_one * (1.0 + scale_one) + shift_one).astype(jnp.bfloat16)
    qv_float = qv_bias_full.astype(jnp.float32)
    qkv_bias = jnp.concatenate(
        [qv_float[:model_width], jnp.zeros((model_width,), jnp.float32), qv_float[model_width:]]
    )
    projected = (
        jnp.dot(hidden_one, qkv_full, preferred_element_type=jnp.float32) + qkv_bias
    ).astype(jnp.bfloat16)

    def row_forward(row_items):
        return attend_row(row_items[0], row_items[1], model_width)

    mixed_rows, log_total = lax.map(row_forward, (projected, segment_ids))
    branch_one = jnp.dot(
        mixed_rows, proj_full, preferred_element_type=jnp.float32
    ) + proj_bias_full.astype(jnp.float32)
    resid_one = stream + gate_one * branch_one
    fc1_full, fc1_bias_full, fc2_full, fc2_bias_full = (
        lax.all_gather(fc1_weight, "fsdp", axis=0, tiled=True),
        lax.all_gather(fc1_bias, "fsdp", axis=0, tiled=True),
        lax.all_gather(fc2_weight, "fsdp", axis=0, tiled=True),
        lax.all_gather(fc2_bias, "fsdp", axis=0, tiled=True),
    )
    normed_two, inv_two = normalize(resid_one)
    hidden_two = (normed_two * (1.0 + scale_two) + shift_two).astype(jnp.bfloat16)
    pre_act = jnp.dot(
        hidden_two, fc1_full, preferred_element_type=jnp.float32
    ) + fc1_bias_full.astype(jnp.float32)
    active = gelu_tanh(pre_act).astype(jnp.bfloat16)
    branch_two = jnp.dot(
        active, fc2_full, preferred_element_type=jnp.float32
    ) + fc2_bias_full.astype(jnp.float32)
    output = (resid_one + gate_two * branch_two).astype(jnp.bfloat16)
    d_out = out_grad.astype(jnp.float32)
    fc1_back, fc2_back = (
        lax.all_gather(fc1_weight, "fsdp", axis=0, tiled=True),
        lax.all_gather(fc2_weight, "fsdp", axis=0, tiled=True),
    )
    d_gate_two = jnp.sum(d_out * branch_two, axis=1)
    d_branch_two = (d_out * gate_two).astype(jnp.bfloat16)
    fc2_shard = lax.psum_scatter(
        jnp.einsum("rsf,rsd->fd", active, d_branch_two, preferred_element_type=jnp.float32).astype(
            jnp.bfloat16
        ),
        "fsdp",
        scatter_dimension=0,
        tiled=True,
    )
    grad_fc2_bias = jnp.sum(d_branch_two.astype(jnp.float32), axis=(0, 1))
    d_active = jnp.einsum("rsd,fd->rsf", d_branch_two, fc2_back, preferred_element_type=jnp.float32)
    d_pre = (d_active * gelu_slope(pre_act)).astype(jnp.bfloat16)
    grad_fc1_bias = jnp.sum(d_pre.astype(jnp.float32), axis=(0, 1))
    d_hidden_two = jnp.einsum("rsf,ef->rse", d_pre, fc1_back, preferred_element_type=jnp.float32)
    d_scale_two = jnp.sum(d_hidden_two * normed_two, axis=1)
    d_shift_two = jnp.sum(d_hidden_two, axis=1)
    d_resid = d_out + normalize_back(d_hidden_two * (1.0 + scale_two), normed_two, inv_two)
    qkv_back, proj_back = (
        lax.all_gather(qkv_weight, "fsdp", axis=0, tiled=True),
        lax.all_gather(proj_weight, "fsdp", axis=0, tiled=True),
    )
    d_gate_one = jnp.sum(d_resid * branch_one, axis=1)
    d_branch_one = (d_resid * gate_one).astype(jnp.bfloat16)
    grad_proj_bias = jnp.sum(d_branch_one.astype(jnp.float32), axis=(0, 1))
    d_mixed = jnp.einsum(
        "rsd,ed->rse", d_branch_one, proj_back, preferred_element_type=jnp.float32
    ).astype(jnp.bfloat16)

    def row_backward(row_items):
        return attend_back(row_items[0], row_items[1], row_items[2], row_items[3], model_width)

    d_projected = lax.map(row_backward, (projected, segment_ids, log_total, d_mixed))
    d_proj_float = d_projected.astype(jnp.float32)
    grad_qv_bias = jnp.concatenate(
        [
            jnp.sum(d_proj_float[..., :model_width], axis=(0, 1)),
            jnp.sum(d_proj_float[..., 2 * model_width :], axis=(0, 1)),
        ]
    )
    d_hidden_one = jnp.einsum(
        "rsf,ef->rse", d_projected, qkv_back, preferred_element_type=jnp.float32
    )
    d_scale_one = jnp.sum(d_hidden_one * normed_one, axis=1)
    d_shift_one = jnp.sum(d_hidden_one, axis=1)
    tokens_grad = (
        d_resid + normalize_back(d_hidden_one * (1.0 + scale_one), normed_one, inv_one)
    ).astype(jnp.bfloat16)
    d_modulation = jnp.concatenate(
        [d_shift_one, d_scale_one, d_gate_one, d_shift_two, d_scale_two, d_gate_two], axis=-1
    ).astype(jnp.bfloat16)
    d_mod_all = lax.all_gather(d_modulation, ("fsdp", "dp"), axis=0, tiled=True)
    grad_ada = jnp.einsum("rd,re->de", act_mine, d_mod_all, preferred_element_type=jnp.float32)
    grad_ada_bias = jnp.sum(
        lax.dynamic_slice_in_dim(d_mod_all, fsdp_at * bias_width, bias_width, 1).astype(jnp.float32),
        axis=0,
    )

    def owners(term):
        return lax.psum_scatter(
            term.astype(jnp.bfloat16), "fsdp", scatter_dimension=0, tiled=True
        )

    qkv_shard = owners(
        jnp.einsum("rse,rsf->ef", hidden_one, d_projected, preferred_element_type=jnp.float32)
    )
    proj_shard = owners(
        jnp.einsum("rse,rsd->ed", mixed_rows, d_branch_one, preferred_element_type=jnp.float32)
    )
    fc1_shard = owners(
        jnp.einsum("rse,rsf->ef", hidden_two, d_pre, preferred_element_type=jnp.float32)
    )
    bias_shards = (
        None,
        lax.psum_scatter(
            grad_qv_bias.astype(jnp.bfloat16), "fsdp", scatter_dimension=0, tiled=True
        ).astype(jnp.float32),
        lax.psum_scatter(
            grad_proj_bias.astype(jnp.bfloat16), "fsdp", scatter_dimension=0, tiled=True
        ).astype(jnp.float32),
        lax.psum_scatter(
            grad_fc1_bias.astype(jnp.bfloat16), "fsdp", scatter_dimension=0, tiled=True
        ).astype(jnp.float32),
        lax.psum_scatter(
            grad_fc2_bias.astype(jnp.bfloat16), "fsdp", scatter_dimension=0, tiled=True
        ).astype(jnp.float32),
    )
    summed = (
        grad_ada,
        grad_ada_bias,
        lax.psum(qkv_shard.astype(jnp.bfloat16), "dp").astype(jnp.float32),
        lax.psum(bias_shards[1].astype(jnp.bfloat16), "dp").astype(jnp.float32),
        lax.psum(proj_shard.astype(jnp.bfloat16), "dp").astype(jnp.float32),
        lax.psum(bias_shards[2].astype(jnp.bfloat16), "dp").astype(jnp.float32),
        lax.psum(fc1_shard.astype(jnp.bfloat16), "dp").astype(jnp.float32),
        lax.psum(bias_shards[3].astype(jnp.bfloat16), "dp").astype(jnp.float32),
        lax.psum(fc2_shard, "dp").astype(jnp.float32),
        lax.psum(bias_shards[4].astype(jnp.bfloat16), "dp").astype(jnp.float32),
    )
    return (
        output,
        tokens_grad,
        summed[0],
        summed[1],
        summed[2],
        summed[3],
        summed[4],
        summed[5],
        summed[6],
        summed[7],
        summed[8],
        summed[9],
    )


def solution(mesh):
    in_specs = (
        P(("fsdp", "dp"), None, None),
        P(("fsdp", "dp"), None),
        P(("fsdp", "dp"), None),
        P("fsdp", None),
        P("fsdp"),
        P("fsdp", None),
        P("fsdp"),
        P("fsdp", None),
        P("fsdp"),
        P("fsdp", None),
        P("fsdp"),
        P("fsdp", None),
        P("fsdp"),
        P(("fsdp", "dp"), None, None),
    )
    out_specs = (
        P(("fsdp", "dp"), None, None),
        P(("fsdp", "dp"), None, None),
        P("fsdp", None),
        P("fsdp"),
        P("fsdp", None),
        P("fsdp"),
        P("fsdp", None),
        P("fsdp"),
        P("fsdp", None),
        P("fsdp"),
        P("fsdp", None),
        P("fsdp"),
    )
    return jax.shard_map(
        on_device, mesh=mesh, in_specs=in_specs, out_specs=out_specs, check_vma=False
    )
```

```python
import functools

import jax
import jax.numpy as jnp
from jax import lax
from jax.experimental import pallas as pl
from jax.experimental.pallas import tpu as pltpu
from jax.sharding import PartitionSpec as P

HEADS = 16
HEAD_DIM = 72


root_half = 0.7978845608028654
norm_eps = 1e-06
masked_score = -1e30


def gelu_tanh(stream):
    return (
        0.5 * stream * (1.0 + jnp.tanh(root_half * (stream + 0.044715 * stream * stream * stream)))
    )


def gelu_slope(stream):
    tanh_inner = jnp.tanh(root_half * (stream + 0.044715 * stream * stream * stream))
    return 0.5 * (1.0 + tanh_inner) + 0.5 * stream * (1.0 - tanh_inner * tanh_inner) * root_half * (
        1.0 + 3.0 * 0.044715 * stream * stream
    )


def normalize(stream):
    centre = jnp.mean(stream, axis=-1, keepdims=True)
    centred = stream - centre
    inv_std = lax.rsqrt(jnp.mean(centred * centred, axis=-1, keepdims=True) + norm_eps)
    return (centred * inv_std, inv_std)


def normalize_back(incoming, normed, inv_std):
    return inv_std * (
        incoming
        - jnp.mean(incoming, axis=-1, keepdims=True)
        - normed * jnp.mean(incoming * normed, axis=-1, keepdims=True)
    )


def head_scores(projected, same_doc, head_index, model_width):
    query_part = lax.dynamic_slice_in_dim(projected, head_index * HEAD_DIM, HEAD_DIM, 1)
    key_part = lax.dynamic_slice_in_dim(projected, model_width + head_index * HEAD_DIM, HEAD_DIM, 1)
    value_part = lax.dynamic_slice_in_dim(
        projected, 2 * model_width + head_index * HEAD_DIM, HEAD_DIM, 1
    )
    raw_scores = jnp.einsum(
        "qd,kd->qk", query_part, key_part, preferred_element_type=jnp.float32
    ) * HEAD_DIM ** (-0.5)
    return (jnp.where(same_doc, raw_scores, masked_score), query_part, key_part, value_part)


def merge_heads(stacked, model_width):
    return jnp.transpose(stacked, (1, 0, 2)).reshape(stacked.shape[1], model_width)


def attend_row(projected, segments_row, model_width):
    same_doc = segments_row[:, None] == segments_row[None, :]

    def one_head(head_index):
        scores, query_part, key_part, value_part = head_scores(
            projected, same_doc, head_index, model_width
        )
        top_score = jnp.max(scores, axis=-1, keepdims=True)
        exp_scores = jnp.exp(scores - top_score)
        denominator = jnp.sum(exp_scores, axis=-1, keepdims=True)
        probabilities = (exp_scores / denominator).astype(jnp.bfloat16)
        mixed_heads = jnp.dot(probabilities, value_part, preferred_element_type=jnp.float32)
        return (mixed_heads, (top_score + jnp.log(denominator))[:, 0])

    mixed_heads, log_total = lax.map(one_head, jnp.arange(HEADS))
    return (merge_heads(mixed_heads, model_width).astype(jnp.bfloat16), log_total)


def attend_back(projected, segments_row, log_total, d_mixed, model_width):
    same_doc = segments_row[:, None] == segments_row[None, :]
    head_scale = HEAD_DIM ** (-0.5)

    def one_head(head_index):
        scores, query_part, key_part, value_part = head_scores(
            projected, same_doc, head_index, model_width
        )
        d_head = lax.dynamic_slice_in_dim(d_mixed, head_index * HEAD_DIM, HEAD_DIM, 1)
        lse_row = lax.dynamic_index_in_dim(log_total, head_index, 0, keepdims=False)
        probabilities = jnp.exp(scores - lse_row[:, None])
        prob_low = probabilities.astype(jnp.bfloat16)
        d_probs = jnp.einsum("qd,kd->qk", d_head, value_part, preferred_element_type=jnp.float32)
        d_value = jnp.einsum("qk,qd->kd", prob_low, d_head, preferred_element_type=jnp.float32)
        d_scores = (
            probabilities * (d_probs - jnp.sum(d_probs * probabilities, axis=-1, keepdims=True))
        ).astype(jnp.bfloat16)
        d_query = (
            jnp.einsum("qk,kd->qd", d_scores, key_part, preferred_element_type=jnp.float32)
            * head_scale
        )
        d_key = (
            jnp.einsum("qk,qd->kd", d_scores, query_part, preferred_element_type=jnp.float32)
            * head_scale
        )
        return (d_query, d_key, d_value)

    d_query, d_key, d_value = lax.map(one_head, jnp.arange(HEADS))
    merged = [
        merge_heads(d_query, model_width),
        merge_heads(d_key, model_width),
        merge_heads(d_value, model_width),
    ]
    return jnp.concatenate(merged, axis=-1).astype(jnp.bfloat16)


def general_form(
    tokens,
    cond,
    segment_ids,
    ada_weight,
    ada_bias,
    qkv_weight,
    qv_bias,
    proj_weight,
    proj_bias,
    fc1_weight,
    fc1_bias,
    fc2_weight,
    fc2_bias,
    out_grad,
):
    row_count, seq_len, model_width = tokens.shape
    ff_width = fc1_weight.shape[1]
    stream = tokens.astype(jnp.float32)
    cond_float = cond.astype(jnp.float32)
    cond_act = (cond_float / (1.0 + jnp.exp(-cond_float))).astype(jnp.bfloat16)
    fsdp_at, dp_at = lax.axis_index("fsdp"), lax.axis_index("dp")
    dp_size = lax.axis_size("dp")
    slice_width, bias_width = ada_weight.shape[0], ada_bias.shape[0]
    act_all = lax.all_gather(cond_act, ("fsdp", "dp"), axis=0, tiled=True)
    act_mine = lax.dynamic_slice_in_dim(act_all, fsdp_at * slice_width, slice_width, 1)
    partial = jnp.dot(act_mine, ada_weight, preferred_element_type=jnp.float32)
    bias_row = lax.dynamic_update_slice_in_dim(
        jnp.zeros((6 * model_width,), jnp.float32),
        ada_bias.astype(jnp.float32),
        fsdp_at * bias_width,
        0,
    )
    partial = (partial + bias_row).reshape(-1, dp_size, row_count, 6 * model_width)
    partial = lax.dynamic_index_in_dim(partial, dp_at, 1, keepdims=False)
    modulation = lax.psum_scatter(
        partial.reshape(-1, 6 * model_width), "fsdp", scatter_dimension=0, tiled=True
    )
    pieces = [
        modulation[:, None, section * model_width : (section + 1) * model_width]
        for section in range(6)
    ]
    shift_one, scale_one, gate_one, shift_two, scale_two, gate_two = pieces
    qkv_full, qv_bias_full, proj_full, proj_bias_full = (
        lax.all_gather(qkv_weight, "fsdp", axis=0, tiled=True),
        lax.all_gather(qv_bias, "fsdp", axis=0, tiled=True),
        lax.all_gather(proj_weight, "fsdp", axis=0, tiled=True),
        lax.all_gather(proj_bias, "fsdp", axis=0, tiled=True),
    )
    normed_one, inv_one = normalize(stream)
    hidden_one = (normed_one * (1.0 + scale_one) + shift_one).astype(jnp.bfloat16)
    qv_float = qv_bias_full.astype(jnp.float32)
    qkv_bias = jnp.concatenate(
        [qv_float[:model_width], jnp.zeros((model_width,), jnp.float32), qv_float[model_width:]]
    )
    projected = (
        jnp.dot(hidden_one, qkv_full, preferred_element_type=jnp.float32) + qkv_bias
    ).astype(jnp.bfloat16)

    def row_forward(row_items):
        return attend_row(row_items[0], row_items[1], model_width)

    mixed_rows, log_total = lax.map(row_forward, (projected, segment_ids))
    branch_one = jnp.dot(
        mixed_rows, proj_full, preferred_element_type=jnp.float32
    ) + proj_bias_full.astype(jnp.float32)
    resid_one = stream + gate_one * branch_one
    fc1_full, fc1_bias_full, fc2_full, fc2_bias_full = (
        lax.all_gather(fc1_weight, "fsdp", axis=0, tiled=True),
        lax.all_gather(fc1_bias, "fsdp", axis=0, tiled=True),
        lax.all_gather(fc2_weight, "fsdp", axis=0, tiled=True),
        lax.all_gather(fc2_bias, "fsdp", axis=0, tiled=True),
    )
    normed_two, inv_two = normalize(resid_one)
    hidden_two = (normed_two * (1.0 + scale_two) + shift_two).astype(jnp.bfloat16)
    pre_act = jnp.dot(
        hidden_two, fc1_full, preferred_element_type=jnp.float32
    ) + fc1_bias_full.astype(jnp.float32)
    active = gelu_tanh(pre_act).astype(jnp.bfloat16)
    branch_two = jnp.dot(
        active, fc2_full, preferred_element_type=jnp.float32
    ) + fc2_bias_full.astype(jnp.float32)
    output = (resid_one + gate_two * branch_two).astype(jnp.bfloat16)
    d_out = out_grad.astype(jnp.float32)
    fc1_back, fc2_back = (
        lax.all_gather(fc1_weight, "fsdp", axis=0, tiled=True),
        lax.all_gather(fc2_weight, "fsdp", axis=0, tiled=True),
    )
    d_gate_two = jnp.sum(d_out * branch_two, axis=1)
    d_branch_two = (d_out * gate_two).astype(jnp.bfloat16)
    fc2_shard = lax.psum_scatter(
        jnp.einsum("rsf,rsd->fd", active, d_branch_two, preferred_element_type=jnp.float32).astype(
            jnp.bfloat16
        ),
        "fsdp",
        scatter_dimension=0,
        tiled=True,
    )
    grad_fc2_bias = jnp.sum(d_branch_two.astype(jnp.float32), axis=(0, 1))
    d_active = jnp.einsum("rsd,fd->rsf", d_branch_two, fc2_back, preferred_element_type=jnp.float32)
    d_pre = (d_active * gelu_slope(pre_act)).astype(jnp.bfloat16)
    grad_fc1_bias = jnp.sum(d_pre.astype(jnp.float32), axis=(0, 1))
    d_hidden_two = jnp.einsum("rsf,ef->rse", d_pre, fc1_back, preferred_element_type=jnp.float32)
    d_scale_two = jnp.sum(d_hidden_two * normed_two, axis=1)
    d_shift_two = jnp.sum(d_hidden_two, axis=1)
    d_resid = d_out + normalize_back(d_hidden_two * (1.0 + scale_two), normed_two, inv_two)
    qkv_back, proj_back = (
        lax.all_gather(qkv_weight, "fsdp", axis=0, tiled=True),
        lax.all_gather(proj_weight, "fsdp", axis=0, tiled=True),
    )
    d_gate_one = jnp.sum(d_resid * branch_one, axis=1)
    d_branch_one = (d_resid * gate_one).astype(jnp.bfloat16)
    grad_proj_bias = jnp.sum(d_branch_one.astype(jnp.float32), axis=(0, 1))
    d_mixed = jnp.einsum(
        "rsd,ed->rse", d_branch_one, proj_back, preferred_element_type=jnp.float32
    ).astype(jnp.bfloat16)

    def row_backward(row_items):
        return attend_back(row_items[0], row_items[1], row_items[2], row_items[3], model_width)

    d_projected = lax.map(row_backward, (projected, segment_ids, log_total, d_mixed))
    d_proj_float = d_projected.astype(jnp.float32)
    grad_qv_bias = jnp.concatenate(
        [
            jnp.sum(d_proj_float[..., :model_width], axis=(0, 1)),
            jnp.sum(d_proj_float[..., 2 * model_width :], axis=(0, 1)),
        ]
    )
    d_hidden_one = jnp.einsum(
        "rsf,ef->rse", d_projected, qkv_back, preferred_element_type=jnp.float32
    )
    d_scale_one = jnp.sum(d_hidden_one * normed_one, axis=1)
    d_shift_one = jnp.sum(d_hidden_one, axis=1)
    tokens_grad = (
        d_resid + normalize_back(d_hidden_one * (1.0 + scale_one), normed_one, inv_one)
    ).astype(jnp.bfloat16)
    d_modulation = jnp.concatenate(
        [d_shift_one, d_scale_one, d_gate_one, d_shift_two, d_scale_two, d_gate_two], axis=-1
    ).astype(jnp.bfloat16)
    d_mod_all = lax.all_gather(d_modulation, ("fsdp", "dp"), axis=0, tiled=True)
    grad_ada = jnp.einsum("rd,re->de", act_mine, d_mod_all, preferred_element_type=jnp.float32)
    grad_ada_bias = jnp.sum(
        lax.dynamic_slice_in_dim(d_mod_all, fsdp_at * bias_width, bias_width, 1).astype(jnp.float32),
        axis=0,
    )

    def owners(term):
        return lax.psum_scatter(
            term.astype(jnp.bfloat16), "fsdp", scatter_dimension=0, tiled=True
        )

    qkv_shard = owners(
        jnp.einsum("rse,rsf->ef", hidden_one, d_projected, preferred_element_type=jnp.float32)
    )
    proj_shard = owners(
        jnp.einsum("rse,rsd->ed", mixed_rows, d_branch_one, preferred_element_type=jnp.float32)
    )
    fc1_shard = owners(
        jnp.einsum("rse,rsf->ef", hidden_two, d_pre, preferred_element_type=jnp.float32)
    )
    bias_shards = (
        None,
        lax.psum_scatter(
            grad_qv_bias.astype(jnp.bfloat16), "fsdp", scatter_dimension=0, tiled=True
        ).astype(jnp.float32),
        lax.psum_scatter(
            grad_proj_bias.astype(jnp.bfloat16), "fsdp", scatter_dimension=0, tiled=True
        ).astype(jnp.float32),
        lax.psum_scatter(
            grad_fc1_bias.astype(jnp.bfloat16), "fsdp", scatter_dimension=0, tiled=True
        ).astype(jnp.float32),
        lax.psum_scatter(
            grad_fc2_bias.astype(jnp.bfloat16), "fsdp", scatter_dimension=0, tiled=True
        ).astype(jnp.float32),
    )
    summed = (
        grad_ada,
        grad_ada_bias,
        lax.psum(qkv_shard.astype(jnp.bfloat16), "dp").astype(jnp.float32),
        lax.psum(bias_shards[1].astype(jnp.bfloat16), "dp").astype(jnp.float32),
        lax.psum(proj_shard.astype(jnp.bfloat16), "dp").astype(jnp.float32),
        lax.psum(bias_shards[2].astype(jnp.bfloat16), "dp").astype(jnp.float32),
        lax.psum(fc1_shard.astype(jnp.bfloat16), "dp").astype(jnp.float32),
        lax.psum(bias_shards[3].astype(jnp.bfloat16), "dp").astype(jnp.float32),
        lax.psum(fc2_shard, "dp").astype(jnp.float32),
        lax.psum(bias_shards[4].astype(jnp.bfloat16), "dp").astype(jnp.float32),
    )
    return (
        output,
        tokens_grad,
        summed[0],
        summed[1],
        summed[2],
        summed[3],
        summed[4],
        summed[5],
        summed[6],
        summed[7],
        summed[8],
        summed[9],
    )


MESH_ID = pl.DeviceIdType.MESH
f32 = jnp.float32
bf16 = jnp.bfloat16

SEQ = 256
WIDTH = 1152
HIDDEN = 4608
PART = 1152
QKV = 864
PAD = 128
LOCAL = 4


def dot_nn(left, right):
    return lax.dot_general(left, right, (((1,), (0,)), ((), ())), preferred_element_type=f32)


def dot_nt(left, right):
    return lax.dot_general(left, right, (((1,), (1,)), ((), ())), preferred_element_type=f32)


def dot_tn(left, right):
    return lax.dot_general(left, right, (((0,), (0,)), ((), ())), preferred_element_type=f32)


def iota(shape, axis):
    return lax.broadcasted_iota(jnp.int32, shape, axis)


def whole_part(value, divisor):
    return jnp.floor((value + 0.5) * (1.0 / divisor))


class Ids:
    def __init__(self):
        self.used = 0

    def take(self, count):
        start = self.used
        self.used += count
        return start


IDS = Ids()
IDS.small_y, IDS.small_z, IDS.small_c = IDS.take(1), IDS.take(6), IDS.take(1)
IDS.small_x, IDS.small_d = IDS.take(1), IDS.take(1)
IDS.mod_c, IDS.mod_y, IDS.mod_z = IDS.take(1), IDS.take(1), IDS.take(3)
IDS.core = [IDS.take(1) for _ in range(3)]
IDS.z = [IDS.take(3) for _ in range(4)]
IDS.y = [IDS.take(4) for _ in range(4)]
IDS.h1, IDS.h2, IDS.d2, IDS.d1 = IDS.take(3), IDS.take(3), IDS.take(3), IDS.take(3)
IDS.r1, IDS.r2, IDS.r3, IDS.r4 = IDS.take(3), IDS.take(3), IDS.take(3), IDS.take(3)
IDS.gy = [IDS.take(4) for _ in range(4)]
IDS.gz = [IDS.take(3) for _ in range(4)]
IDS.gf = [IDS.take(3) for _ in range(4)]
IDS.end_y, IDS.end_z, IDS.end_x, IDS.end_c = IDS.take(1), IDS.take(6), IDS.take(1), IDS.take(1)
ID_COUNT = IDS.used

SCRATCH = (
    ((32, 8, 384), f32),
    ((16, 8, WIDTH), f32),
    ((8, 8, WIDTH), f32),
    ((4, 8, WIDTH), f32),
    ((3, 8, WIDTH), f32),
    ((8, WIDTH), f32),
    ((72, QKV), bf16),
    ((72, PART), bf16),
    ((72, WIDTH), bf16),
    ((72, QKV), bf16),
    ((72, PART), bf16),
    ((72, WIDTH), bf16),
    ((WIDTH, QKV), bf16),
    ((WIDTH, PART), bf16),
    ((PART, WIDTH), bf16),
    ((4, 72, WIDTH), bf16),
    ((288, WIDTH), bf16),
    ((1024, WIDTH), bf16),
    ((1024, WIDTH), bf16),
    ((1024, WIDTH), bf16),
    ((1024, 12 * PAD), bf16),
    ((16, SEQ, SEQ), bf16),
    ((1024, 288), bf16),
    ((1024, PART), bf16),
    ((1024, PART), bf16),
    ((1024, QKV), bf16),
    ((3, SEQ, WIDTH), bf16),
    ((3, SEQ, WIDTH), bf16),
    ((SEQ, WIDTH), bf16),
    ((SEQ, WIDTH), bf16),
    ((SEQ, WIDTH), bf16),
    ((SEQ, WIDTH), f32),
    ((SEQ, WIDTH), f32),
    ((SEQ, WIDTH), f32),
    ((SEQ, WIDTH), f32),
    ((16, WIDTH), f32),
    ((8, WIDTH), f32),
    ((WIDTH, QKV), bf16),
    ((WIDTH, PART), bf16),
    ((PART, WIDTH), bf16),
    ((4, 72, WIDTH), bf16),
    ((4, 144, QKV), bf16),
    ((4, 144, PART), bf16),
    ((4, 144, WIDTH), bf16),
    ((4, 72, WIDTH), bf16),
    ((3, 144, QKV), bf16),
    ((3, 144, PART), bf16),
    ((3, 144, WIDTH), bf16),
    ((3, 72, WIDTH), bf16),
    ((72, QKV), bf16),
    ((72, PART), bf16),
    ((72, WIDTH), bf16),
    ((72, QKV), bf16),
    ((72, PART), bf16),
    ((72, WIDTH), bf16),
    ((4, 72, QKV), bf16),
    ((4, 72, PART), bf16),
    ((4, 72, WIDTH), bf16),
    ((72, WIDTH), bf16),
    ((32, 16, WIDTH), bf16),
)


def block_kernel(
    tok, og, small, ada, adab, wqkv, wproj, wfc1, wfc2, out,
    tgrad, oada, oqkv, oproj, ofc1, ofc2, osum, S, modp, modc,
    mody, modz, mod, own_qkv, own_fc1, own_fc2, xr_qkv, xr_fc1, xr_fc2, G_qkv,
    G_fc1, G_fc2, G_proj, W_proj, H1, H2, D2, qp, P, mixed,
    active, slope, dprj, rrA, rrB, sA, sB, sX, keep, own,
    b1, resid, acc, bias, g_qkv, g_fc1, g_fc2, g_proj, yr_qkv, yr_fc1,
    yr_fc2, yr_proj, zr_qkv, zr_fc1, zr_fc2, zr_proj, fa_qkv, fa_fc1, fa_fc2, fb_qkv,
    fb_fc1, fb_fc2, fr_qkv, fr_fc1, fr_fc2, p_out, E, snd, rcv, loc,
):
    own_w, xr_w, G_w = (own_qkv, own_fc1, own_fc2), (xr_qkv, xr_fc1, xr_fc2), (G_qkv, G_fc1, G_fc2)
    w_in, w_out = (wqkv, wfc1, wfc2), (oqkv, ofc1, ofc2)
    yr_w, zr_w = (yr_qkv, yr_fc1, yr_fc2), (zr_qkv, zr_fc1, zr_fc2)
    fa_w, fb_w, fr_w = (fa_qkv, fa_fc1, fa_fc2), (fb_qkv, fb_fc1, fb_fc2), (fr_qkv, fr_fc1, fr_fc2)
    f = lax.axis_index("fsdp")
    x = lax.axis_index("dp")
    z = lax.div(f, 4)
    y = lax.rem(lax.div(f, 2), 2)
    c = lax.rem(f, 2)
    q = 2 * x + c
    qp_, qx_, qd_ = 2 * x + 1 - c, 2 * (1 - x) + c, 2 * (1 - x) + 1 - c

    def dev(zz, yy, cc, xx):
        return ((zz * 2 + yy) * 2 + cc, xx)

    mate, xnb, diag, ynb = dev(z, y, 1 - c, x), dev(z, y, c, 1 - x), dev(z, y, 1 - c, 1 - x), dev(z, 1 - y, c, x)

    def z_to(k):
        return lax.rem(z + k, 4)

    def z_from(k):
        return lax.rem(z + 4 - k, 4)

    def znb(k):
        return dev(z_to(k), y, c, x)

    def rc(src, dst, ident, to):
        return pltpu.make_async_remote_copy(
            src_ref=src, dst_ref=dst, send_sem=snd.at[ident], recv_sem=rcv.at[ident],
            device_id=to, device_id_type=MESH_ID,
        )

    pending = []

    def send(src, dst, ident, to):
        rc(src, dst, ident, to).start()
        pending.append((src, ident, to))

    def got(dst, ident):
        rc(dst, dst, ident, mate).wait_recv()

    def sent(src, ident):
        rc(src, src, ident, mate).wait_send()

    def settle(first):
        keep_on = []
        for item in pending:
            if item[1] in first:
                sent(item[0], item[1])
            else:
                keep_on.append(item)
        pending[:] = keep_on

    barrier = pltpu.get_barrier_semaphore()
    neighbours = [mate, xnb, diag, ynb, znb(1), znb(2), znb(3)]
    for to in neighbours:
        pl.semaphore_signal(barrier, inc=1, device_id=to, device_id_type=MESH_ID)
    pl.semaphore_wait(barrier, len(neighbours))


    def slot_of(cc, xx, yy, zz):
        return ((cc * 2 + xx) * 2 + yy) * 4 + zz

    my_slot = slot_of(c, x, y, z)
    send(small, S.at[my_slot], IDS.small_y, ynb)
    kinds = (0, 1, 2)
    for kind in kinds:
        send(w_in[kind].at[qp_], xr_w[kind], IDS.core[kind], mate)
    own_copies = []
    for at, kind in enumerate(kinds):
        own_copies.append(pltpu.make_async_copy(w_in[kind].at[q], own_w[kind], loc.at[at]))
        own_copies[-1].start()
    S[my_slot] = small[...]
    acc[...] = jnp.zeros((16, WIDTH), f32)
    in_column = y == x
    proj_copy = pltpu.make_async_copy(wproj, G_proj.at[z], loc.at[3])

    def chip_rows(zz, yy):
        return pl.ds(pl.multiple_of((2 * zz + yy) * 144, 16), 144)

    def assemble(kind, at):
        own_copies[at].wait()
        got(xr_w[kind], IDS.core[kind])
        mine = own_w[kind][...].astype(f32)
        other = xr_w[kind][...].astype(f32)
        low = jnp.where(c == 0, mine, other)
        high = jnp.where(c == 0, other, mine)
        G = G_w[kind]
        G[chip_rows(z, y), :] = jnp.concatenate([low, high], axis=0).astype(bf16)
        part = G.at[chip_rows(z, y), :]
        send(part, part, IDS.y[kind], ynb)
        for k in (2, 1, 3):
            send(part, part, IDS.z[kind] + k - 1, znb(k))

    def near(j):
        if j == 0:
            return jnp.where(z == 0, 3, 1)
        if j == 1:
            return jnp.where((z == 1) | (z == 2), 3, 2)
        return jnp.where(z == 0, 1, jnp.where(z == 3, 3, 2))

    def forward(kind, j):
        k = near(j)
        source = lax.rem(z + 4 - k, 4)
        part = G_w[kind].at[chip_rows(source, y), :]
        got(part, IDS.z[kind] + k - 1)
        send(part, part, IDS.y[kind] + 1 + j, ynb)

    def arrived(kind):
        other = 1 - y
        got(G_w[kind].at[chip_rows(z, other), :], IDS.y[kind])
        for j in range(3):
            source = lax.rem(z + 4 - near(j), 4)
            got(G_w[kind].at[chip_rows(source, other), :], IDS.y[kind] + 1 + j)

    def proj_first():
        @pl.when(in_column)
        def _():
            proj_copy.start()
            for k in (2, 1, 3):
                rc(wproj, G_proj.at[z], IDS.z[3] + k - 1, znb(k)).start()
            rc(wproj, G_proj.at[z], IDS.y[3], ynb).start()

    def proj_forward(j):
        @pl.when(in_column)
        def _():
            k = near(j)
            part = G_proj.at[lax.rem(z + 4 - k, 4)]
            got(part, IDS.z[3] + k - 1)
            rc(part, part, IDS.y[3] + 1 + j, ynb).start()

    def proj_arrived():
        @pl.when(in_column)
        def _():
            proj_copy.wait()
            for k in (1, 2, 3):
                sent(wproj, IDS.z[3] + k - 1)
            sent(wproj, IDS.y[3])
            for j in range(3):
                sent(G_proj.at[lax.rem(z + 4 - near(j), 4)], IDS.y[3] + 1 + j)

        @pl.when(jnp.logical_not(in_column))
        def _():
            got(G_proj.at[z], IDS.y[3])
            for j in range(3):
                got(G_proj.at[lax.rem(z + 4 - near(j), 4)], IDS.y[3] + 1 + j)

        W_proj[...] = jnp.concatenate(
            [G_proj[head].astype(f32) for head in range(LOCAL)], axis=0
        ).astype(bf16)

    assemble(0, 0)

    got(S.at[slot_of(c, x, 1 - y, z)], IDS.small_y)
    for k in (2, 1, 3):
        for yy in range(2):
            part = S.at[slot_of(c, x, yy, z)]
            send(part, part, IDS.small_z + 2 * (k - 1) + yy, znb(k))
    proj_first()
    assemble(1, 1)
    for k in (1, 2, 3):
        for yy in range(2):
            got(S.at[slot_of(c, x, yy, z_from(k))], IDS.small_z + 2 * (k - 1) + yy)
    eight = lambda cc, xx: S.at[pl.ds((cc * 2 + xx) * 8, 8)]
    send(eight(c, x), eight(c, x), IDS.small_c, mate)
    send(eight(c, x), eight(c, x), IDS.small_x, xnb)

    def pick_columns(rows):
        total = None
        for piece in range(3):
            kk = iota((384, PAD), 0) + piece * 384
            jj = iota((384, PAD), 1)
            chosen = ((kk == 72 * f + jj) & (jj < 72)).astype(f32).astype(bf16)
            term = dot_nn(rows(piece), chosen)
            total = term if total is None else total + term
        return total.astype(bf16)

    got(eight(1 - c, x), IDS.small_c)
    act = pick_columns(
        lambda piece: jnp.concatenate(
            [S[pl.ds((cc * 2 + x) * 8, 8), piece, :] for cc in range(2)], axis=0
        ).astype(bf16)
    )[:, :72]
    for section in range(6):
        modp[:, section, :] = dot_nn(
            act, ada[:, section * WIDTH : (section + 1) * WIDTH]
        ) + adab[section : section + 1, :]
    for section in (6, 7):
        modp[:, section, :] = jnp.zeros((16, WIDTH), f32)
    assemble(2, 2)
    theirs, ours = modp.at[pl.ds((1 - c) * 8, 8)], modp.at[pl.ds(c * 8, 8)]
    send(theirs, modc, IDS.mod_c, mate)
    got(modc, IDS.mod_c)
    for at in range(8):
        ours[at] += modc[at]
    send(modp.at[pl.ds(c * 8 + (1 - y) * 4, 4)], mody, IDS.mod_y, ynb)
    got(mody, IDS.mod_y)
    base = c * 8 + y * 4
    for at in range(4):
        modp[base + at] += mody[at]
    for k in (2, 1, 3):
        send(modp.at[base + z_to(k)], modz.at[k - 1], IDS.mod_z + k - 1, znb(k))
    forward(0, 0)
    got(eight(c, 1 - x), IDS.small_x)
    send(eight(c, 1 - x), eight(c, 1 - x), IDS.small_d, mate)

    def place(row, width, lane_of, owner_of):
        kk = iota((384, width), 1).astype(f32)
        jj = iota((384, width), 0).astype(f32)
        chosen = (jj == lane_of(kk)).astype(f32).astype(bf16)
        spread = dot_nn(row.astype(bf16), chosen)
        at = iota((16, width), 0)
        slot_f = ((lax.rem(at, 4) * 2 + lax.rem(lax.div(at, 4), 2)) * 2 + lax.div(at, 8)).astype(f32)
        mine = slot_f == owner_of(iota((16, width), 1).astype(f32))
        return jnp.sum(jnp.where(mine, spread, 0.0), axis=0, keepdims=True)

    def plane(piece):
        return jnp.concatenate([S[pl.ds((cc * 2 + x) * 8, 8), piece, :] for cc in range(2)], axis=0)

    def mod72(kk):
        return kk - 72.0 * whole_part(kk, 72)

    by72 = lambda kk: whole_part(kk, 72)
    qf, xf, cf = q.astype(f32), x.astype(f32), c.astype(f32)
    row3, row4 = plane(3), plane(4)
    bias[0:1, :] = place(row3, WIDTH, lambda kk: 144.0 + mod72(kk), by72)
    bias[1:2, :] = place(row3, WIDTH, lambda kk: 216.0 + mod72(kk), by72)
    bias[2:3, :] = place(row4, WIDTH, lambda kk: 72.0 * qf + mod72(kk), by72)

    def qkv_owner(kk):
        third = whole_part(kk, 288)
        head = whole_part(kk - 288.0 * third, 72)
        owner = 2.0 * head + xf + 4.0 * third
        return jnp.where((third == 1.0) | (third > 2.5), -1.0, owner)

    bias[3:4, :] = place(row3, WIDTH, lambda kk: 72.0 * cf + mod72(kk), qkv_owner)

    for k in (1, 2, 3):
        got(modz.at[k - 1], IDS.mod_z + k - 1)
    mod[...] = modp[base + z] + modz[0] + modz[1] + modz[2]

    def row_of(section):
        return mod[section : section + 1, :]

    def slot_rows(slot):
        return pl.ds(pl.multiple_of(slot * SEQ, SEQ), SEQ)

    TILE = 64

    def tiles(body):
        def step(at, carry):
            body(pl.multiple_of(at * TILE, TILE))
            return carry

        lax.fori_loop(0, SEQ // TILE, step, 0)


    def norm_one(at):
        normed, _ = normalize(tok[pl.ds(at, TILE), :].astype(f32))
        H1[pl.ds(pl.multiple_of(q * SEQ + at, TILE), TILE), :] = (
            normed * (1.0 + row_of(1)) + row_of(0)
        ).astype(bf16)

    tiles(norm_one)

    def spread_start(buf, ident):
        part = buf.at[slot_rows(q), :]
        send(part, part, ident, mate)
        send(part, part, ident + 1, xnb)

    def spread_mid(buf, ident):
        part = buf.at[slot_rows(qx_), :]
        got(part, ident + 1)
        send(part, part, ident + 2, mate)

    def spread_mate(buf, ident):
        got(buf.at[slot_rows(qp_), :], ident)

    def spread_end(buf, ident):
        got(buf.at[slot_rows(qd_), :], ident + 2)

    spread_start(H1, IDS.h1)

    def add_row(at, value):
        acc[at : at + 1, :] += jnp.sum(value, axis=0, keepdims=True)

    def out_gate(at):
        low = (og[pl.ds(at, TILE), :].astype(f32) * row_of(5)).astype(bf16)
        D2[pl.ds(pl.multiple_of(q * SEQ + at, TILE), TILE), :] = low
        add_row(6, low.astype(f32))

    tiles(out_gate)
    forward(0, 1)
    spread_mate(H1, IDS.h1)
    forward(0, 2)
    spread_mid(H1, IDS.h1)
    arrived(0)


    def project(slot):
        rows = slot_rows(slot)
        value = (dot_nn(H1[rows, :], G_qkv[...]) + bias[3:4, :QKV]).astype(bf16)
        blank = jnp.zeros((SEQ, PAD - HEAD_DIM), bf16)
        for at in range(12):
            qp[rows, at * PAD : (at + 1) * PAD] = jnp.concatenate(
                [value[:, at * HEAD_DIM : (at + 1) * HEAD_DIM], blank], axis=1
            )

    def attend(slot):
        rows = slot_rows(slot)
        where_seg = slot_of(lax.rem(slot, 2), lax.div(slot, 2), y, z)
        seg = S[where_seg, 5:6, :SEQ]
        seg_column = jnp.transpose(jnp.broadcast_to(seg, (8, SEQ)))[:, :1]
        same = seg_column == seg
        pieces = []
        for head in range(LOCAL):
            query = qp[rows, head * PAD : (head + 1) * PAD]
            key = qp[rows, (LOCAL + head) * PAD : (LOCAL + head + 1) * PAD]
            value = qp[rows, (2 * LOCAL + head) * PAD : (2 * LOCAL + head + 1) * PAD]
            scores = jnp.where(same, dot_nt(query, key) * HEAD_DIM ** (-0.5), masked_score)
            exp_scores = jnp.exp(scores - jnp.max(scores, axis=1, keepdims=True))
            probs = (exp_scores / jnp.sum(exp_scores, axis=1, keepdims=True)).astype(bf16)
            P[slot * LOCAL + head] = probs
            pieces.append(dot_nn(probs, value).astype(bf16)[:, :HEAD_DIM])
        mixed[rows, :] = jnp.concatenate(pieces, axis=1)

    def pair(body, group):
        def step(at, carry):
            body(2 * group + lax.rem(c + at, 2))
            return carry

        lax.fori_loop(0, 2, step, 0)

    got(eight(1 - c, 1 - x), IDS.small_d)
    pair(project, x)
    pair(attend, x)
    proj_forward(0)
    proj_forward(1)
    proj_forward(2)
    spread_end(H1, IDS.h1)
    spread_start(D2, IDS.d2)
    pair(project, 1 - x)
    pair(attend, 1 - x)


    def reduce_rows(partial, rr, ident, between=None):
        sA[...] = partial(qd_).astype(bf16)
        send(sA, rr.at[0], ident, mate)
        keep[...] = partial(qx_)
        sB[...] = partial(qp_).astype(bf16)
        got(rr.at[0], ident)
        sX[...] = (keep[...] + rr[0].astype(f32)).astype(bf16)
        send(sX, rr.at[2], ident + 2, xnb)
        send(sB, rr.at[1], ident + 1, mate)
        own[...] = partial(q)
        if between is not None:
            between()
        got(rr.at[1], ident + 1)
        got(rr.at[2], ident + 2)
        settle((ident, ident + 1, ident + 2))

    def total_rows(rr, at):
        rows = pl.ds(at, TILE)
        return own[rows, :] + rr[1, rows, :].astype(f32) + rr[2, rows, :].astype(f32)

    proj_arrived()
    forward(1, 0)

    def after_one():
        forward(1, 1)
        spread_mate(D2, IDS.d2)

    reduce_rows(lambda slot: dot_nn(mixed[slot_rows(slot), :], W_proj[...]), rrA, IDS.r1, after_one)


    def norm_two(at):
        rows = pl.ds(at, TILE)
        branch = total_rows(rrA, at) + bias[0:1, :]
        b1[rows, :] = branch
        stream = tok[rows, :].astype(f32) + row_of(2) * branch
        resid[rows, :] = stream
        normed, _ = normalize(stream)
        H2[pl.ds(pl.multiple_of(q * SEQ + at, TILE), TILE), :] = (
            normed * (1.0 + row_of(4)) + row_of(3)
        ).astype(bf16)

    tiles(norm_two)
    spread_start(H2, IDS.h2)
    spread_mid(D2, IDS.d2)
    forward(1, 2)
    spread_mate(H2, IDS.h2)
    arrived(1)

    CHUNK = 384

    def first_layer(slot):
        rows = slot_rows(slot)
        for at in range(0, PART, CHUNK):
            pre = dot_nn(H2[rows, :], G_fc1[:, at : at + CHUNK]) + bias[2:3, at : at + CHUNK]
            square = pre * pre
            bend = jnp.tanh(root_half * (pre + 0.044715 * square * pre))
            active[rows, at : at + CHUNK] = (0.5 * pre * (1.0 + bend)).astype(bf16)
            slope[rows, at : at + CHUNK] = (
                0.5 * (1.0 + bend)
                + 0.5 * pre * (1.0 - bend * bend) * root_half * (1.0 + 3.0 * 0.044715 * square)
            ).astype(bf16)

    pair(first_layer, x)
    forward(2, 0)
    spread_mid(H2, IDS.h2)
    spread_end(H2, IDS.h2)
    pair(first_layer, 1 - x)
    forward(2, 1)
    spread_end(D2, IDS.d2)

    def cross(left, right, dest, width):
        for at in range(0, width, CHUNK):
            dest[at : at + CHUNK, :] = dot_tn(left[:, at : at + CHUNK], right[...]).astype(bf16)

    cross(active, D2, g_fc2, PART)
    forward(2, 2)

    def grad_start(kind, grads):
        for zz in range(4):
            send(
                grads.at[chip_rows(zz, 1 - y), :], yr_w[kind].at[zz], IDS.gy[kind] + zz, ynb
            )

    def add_block(grads, rows_at, extra):
        def step(at, carry):
            rows = pl.ds(pl.multiple_of(rows_at + at * 48, 16), 48)
            grads[rows, :] = (
                grads[rows, :].astype(f32) + extra[pl.ds(pl.multiple_of(at * 48, 16), 48), :].astype(f32)
            ).astype(bf16)
            return carry

        lax.fori_loop(0, 3, step, 0)

    def grad_mid(kind, grads, k):
        zz = z_to(k)
        got(yr_w[kind].at[zz], IDS.gy[kind] + zz)
        add_block(grads, (2 * zz + y) * 144, yr_w[kind].at[zz])
        send(
            grads.at[chip_rows(zz, y), :], zr_w[kind].at[k - 1], IDS.gz[kind] + k - 1, znb(k)
        )

    def grad_end(kind, grads):
        got(yr_w[kind].at[z], IDS.gy[kind] + z)
        for k in (1, 2, 3):
            got(zr_w[kind].at[k - 1], IDS.gz[kind] + k - 1)
        width = grads.shape[1]
        A, B, fr = fa_w[kind], fb_w[kind], fr_w[kind]
        for at in range(0, width, CHUNK):
            cols = slice(at, min(at + CHUNK, width))
            total = grads[chip_rows(z, y), cols].astype(f32) + yr_w[kind][z, :, cols].astype(f32)
            for k in range(3):
                total = total + zr_w[kind][k, :, cols].astype(f32)
            low, high = total[:72], total[72:]
            mine = jnp.where(c == 0, low, high).astype(bf16)
            A[:, cols] = mine
            B[:, cols] = jnp.where(c == 0, high, low).astype(bf16)
            fr[q, :, cols] = mine
        send(B, fr.at[q], IDS.gf[kind], mate)
        send(A, fr.at[q], IDS.gf[kind] + 1, xnb)
        send(B, fr.at[q], IDS.gf[kind] + 2, diag)

    out_copies = []

    def grad_out(kind, at):
        fr = fr_w[kind]
        for step, source in enumerate((qp_, qx_, qd_)):
            got(fr.at[source], IDS.gf[kind] + step)
        copy = pltpu.make_async_copy(fr, w_out[kind], loc.at[at])
        copy.start()
        out_copies.append(copy)

    grad_start(2, g_fc2)
    arrived(2)

    def back_hidden(slot):
        rows = slot_rows(slot)
        for at in range(0, PART, CHUNK):
            low = (
                dot_nt(D2[rows, :], G_fc2[at : at + CHUNK, :])
                * slope[rows, at : at + CHUNK].astype(f32)
            ).astype(bf16)
            slope[rows, at : at + CHUNK] = low
            acc[8:9, at : at + CHUNK] += jnp.sum(low.astype(f32), axis=0, keepdims=True)

    pair(back_hidden, x)
    pair(back_hidden, 1 - x)
    d_pre = slope
    settle(tuple(IDS.d2 + step for step in range(3)))
    D1 = D2
    reduce_rows(lambda slot: dot_nt(d_pre[slot_rows(slot), :], G_fc1[...]), rrA, IDS.r3,
                lambda: cross(H2, d_pre, g_fc1, WIDTH))
    grad_start(1, g_fc1)

    def back_two(at):
        rows = pl.ds(at, TILE)
        d_hidden = total_rows(rrA, at)
        normed, inv = normalize(resid[rows, :])
        add_row(3, d_hidden)
        add_row(4, d_hidden * normed)
        d_resid = og[rows, :].astype(f32) + normalize_back(d_hidden * (1.0 + row_of(4)), normed, inv)
        add_row(2, d_resid * b1[rows, :])
        low = (d_resid * row_of(2)).astype(bf16)
        add_row(7, low.astype(f32))
        D1[pl.ds(pl.multiple_of(q * SEQ + at, TILE), TILE), :] = low
        b1[rows, :] = d_resid

    tiles(back_two)
    spread_start(D1, IDS.d1)

    reduce_rows(lambda slot: dot_nn(active[slot_rows(slot), :], G_fc2[...]), rrB, IDS.r2)

    def finish_forward(at):
        rows = pl.ds(at, TILE)
        branch = total_rows(rrB, at) + bias[1:2, :]
        out[rows, :] = (resid[rows, :] + row_of(5) * branch).astype(bf16)
        add_row(5, og[rows, :].astype(f32) * branch)

    grad_mid(2, g_fc2, 2)
    grad_mid(2, g_fc2, 1)
    spread_mate(D1, IDS.d1)
    spread_mid(D1, IDS.d1)
    grad_mid(2, g_fc2, 3)


    def attend_backward(slot):
        rows = slot_rows(slot)
        d_mix = dot_nt(D1[rows, :], W_proj[...]).astype(bf16)
        blank = jnp.zeros((SEQ, PAD - HEAD_DIM), bf16)
        scale = HEAD_DIM ** (-0.5)
        d_query, d_key, d_value = [], [], []
        for head in range(LOCAL):
            query = qp[rows, head * PAD : (head + 1) * PAD]
            key = qp[rows, (LOCAL + head) * PAD : (LOCAL + head + 1) * PAD]
            value = qp[rows, (2 * LOCAL + head) * PAD : (2 * LOCAL + head + 1) * PAD]
            d_head = jnp.concatenate([d_mix[:, head * HEAD_DIM : (head + 1) * HEAD_DIM], blank], axis=1)
            probs = P[slot * LOCAL + head]
            d_probs = dot_nt(d_head, value)
            d_value.append(dot_tn(probs, d_head).astype(bf16)[:, :HEAD_DIM])
            wide = probs.astype(f32)
            d_scores = (wide * (d_probs - jnp.sum(d_probs * wide, axis=1, keepdims=True))).astype(bf16)
            d_query.append((dot_nn(d_scores, key) * scale).astype(bf16)[:, :HEAD_DIM])
            d_key.append((dot_tn(d_scores, query) * scale).astype(bf16)[:, :HEAD_DIM])
        value = jnp.concatenate(d_query + d_key + d_value, axis=1)
        dprj[rows, :] = value
        acc[9:10, :QKV] += jnp.sum(value.astype(f32), axis=0, keepdims=True)

    pair(attend_backward, x)
    spread_end(D1, IDS.d1)
    pair(attend_backward, 1 - x)
    cross(H1, dprj, g_qkv, WIDTH)
    proj_grads = dot_tn(mixed[...], D1[...])
    for head in range(LOCAL):
        g_proj[head] = proj_grads[head * 72 : (head + 1) * 72].astype(bf16)

    @pl.when(jnp.logical_not(in_column))
    def _():
        for head in range(LOCAL):
            rc(g_proj.at[head], yr_proj.at[head], IDS.gy[3] + head, ynb).start()

    grad_start(0, g_qkv)
    grad_mid(1, g_fc1, 2)
    grad_mid(1, g_fc1, 1)
    grad_mid(1, g_fc1, 3)
    tiles(finish_forward)

    reduce_rows(lambda slot: dot_nt(dprj[slot_rows(slot), :], G_qkv[...]), rrA, IDS.r4,
                lambda: grad_end(2, g_fc2))

    def back_one(at):
        rows = pl.ds(at, TILE)
        d_hidden = total_rows(rrA, at)
        normed, inv = normalize(tok[rows, :].astype(f32))
        add_row(0, d_hidden)
        add_row(1, d_hidden * normed)
        tgrad[rows, :] = (
            b1[rows, :] + normalize_back(d_hidden * (1.0 + row_of(1)), normed, inv)
        ).astype(bf16)

    tiles(back_one)

    E[my_slot] = acc[...].astype(bf16)
    send(E.at[my_slot], E.at[my_slot], IDS.end_y, ynb)

    @pl.when(in_column)
    def _():
        for k in (2, 1, 3):
            zz = z_to(k)
            got(yr_proj.at[zz], IDS.gy[3] + zz)
            g_proj[zz] = (g_proj[zz].astype(f32) + yr_proj[zz].astype(f32)).astype(bf16)
            rc(g_proj.at[zz], zr_proj.at[k - 1], IDS.gz[3] + k - 1, znb(k)).start()

    got(E.at[slot_of(c, x, 1 - y, z)], IDS.end_y)
    for k in (2, 1, 3):
        for yy in range(2):
            part = E.at[slot_of(c, x, yy, z)]
            send(part, part, IDS.end_z + 2 * (k - 1) + yy, znb(k))
    grad_mid(0, g_qkv, 2)
    grad_mid(0, g_qkv, 1)
    grad_mid(0, g_qkv, 3)
    for k in (1, 2, 3):
        for yy in range(2):
            got(E.at[slot_of(c, x, yy, z_from(k))], IDS.end_z + 2 * (k - 1) + yy)
    group = lambda cc, xx: E.at[pl.ds((cc * 2 + xx) * 8, 8)]
    send(group(c, x), group(c, x), IDS.end_x, xnb)
    grad_end(1, g_fc1)

    @pl.when(in_column)
    def _():
        got(yr_proj.at[z], IDS.gy[3] + z)
        total = g_proj[z].astype(f32) + yr_proj[z].astype(f32)
        for k in (1, 2, 3):
            got(zr_proj.at[k - 1], IDS.gz[3] + k - 1)
            total = total + zr_proj[k - 1].astype(f32)
        p_out[...] = total.astype(bf16)
        rc(p_out, p_out, IDS.gf[3], xnb).start()

    got(group(c, 1 - x), IDS.end_x)
    send(E.at[pl.ds(c * 16, 16)], E.at[pl.ds(c * 16, 16)], IDS.end_c, mate)
    grad_out(2, 0)

    @pl.when(jnp.logical_not(in_column))
    def _():
        got(p_out, IDS.gf[3])

    copy = pltpu.make_async_copy(p_out, oproj, loc.at[3])
    copy.start()
    out_copies.append(copy)
    got(E.at[pl.ds((1 - c) * 16, 16)], IDS.end_c)

    act_all = pick_columns(lambda piece: S[:, piece, :].astype(bf16))[:, :72]
    for section in range(6):
        rows = E[:, section, :]
        stage = (keep, own)[section // 3].at[(section % 3) * 72 : (section % 3 + 1) * 72, :]
        stage[...] = dot_tn(act_all, rows)
        copy = pltpu.make_async_copy(
            stage, oada.at[:, section * WIDTH : (section + 1) * WIDTH], loc.at[4 + section]
        )
        copy.start()
        out_copies.append(copy)
        osum[section : section + 1, :] = jnp.sum(rows.astype(f32), axis=0, keepdims=True)
    for section in (6, 7):
        osum[section : section + 1, :] = jnp.sum(E[:, section, :].astype(f32), axis=0, keepdims=True)
    for section in (8, 9):
        for quarter in range(4):
            start = ((quarter % 2) * 2 + quarter // 2) * 8
            at = 8 + 4 * (section - 8) + quarter
            osum[at : at + 1, :] = jnp.sum(
                E[start : start + 8, section, :].astype(f32), axis=0, keepdims=True
            )
    grad_out(1, 1)
    grad_end(0, g_qkv)
    grad_out(0, 2)
    for copy in out_copies:
        copy.wait()
    for src, ident, _ in pending:
        sent(src, ident)

    @pl.when(in_column)
    def _():
        for k in (1, 2, 3):
            sent(p_out, IDS.gz[3] + k - 1)
        sent(p_out, IDS.gf[3])

    @pl.when(jnp.logical_not(in_column))
    def _():
        for head in range(LOCAL):
            sent(p_out, IDS.gy[3] + head)


def one_kernel(
    tokens,
    cond,
    segment_ids,
    ada_weight,
    ada_bias,
    qkv_weight,
    qv_bias,
    proj_weight,
    proj_bias,
    fc1_weight,
    fc1_bias,
    fc2_weight,
    fc2_bias,
    out_grad,
):
    fsdp_at = lax.axis_index("fsdp")
    cond_float = cond[0].astype(f32)
    cond_act = (cond_float / (1.0 + jnp.exp(-cond_float))).astype(bf16).astype(f32)
    blank = lambda count: jnp.zeros((count,), f32)
    small = jnp.concatenate(
        [
            cond_act,
            qv_bias.astype(f32),
            proj_bias.astype(f32),
            fc2_bias.astype(f32),
            blank(96),
            fc1_bias.astype(f32),
            blank(96),
            segment_ids[0].astype(f32),
            blank(128 + 768),
        ]
    ).reshape(8, 384)
    adab = lax.dynamic_update_slice_in_dim(
        blank(8 * WIDTH), ada_bias.astype(f32), fsdp_at * 432, 0
    ).reshape(8, WIDTH)
    wqkv = qkv_weight.reshape(72, 3, 4, 4, 72).transpose(3, 0, 1, 2, 4).reshape(4, 72, QKV)
    wfc1 = fc1_weight.reshape(72, 16, 4, 72).transpose(2, 0, 1, 3).reshape(4, 72, PART)
    wfc2 = fc2_weight.reshape(4, 72, WIDTH)
    vmem = pl.BlockSpec(memory_space=pltpu.VMEM)
    anywhere = pl.BlockSpec(memory_space=pl.ANY)
    shape = jax.ShapeDtypeStruct
    scratch = [pltpu.VMEM(dims, kind) for dims, kind in SCRATCH]
    out, tgrad, oada, oqkv, oproj, ofc1, ofc2, osum = pl.pallas_call(
        block_kernel,
        out_shape=(
            shape((SEQ, WIDTH), bf16),
            shape((SEQ, WIDTH), bf16),
            shape((72, 6 * WIDTH), f32),
            shape((4, 72, QKV), bf16),
            shape((72, WIDTH), bf16),
            shape((4, 72, PART), bf16),
            shape((4, 72, WIDTH), bf16),
            shape((16, WIDTH), f32),
        ),
        in_specs=[vmem, vmem, vmem, vmem, vmem, anywhere, anywhere, anywhere, anywhere],
        out_specs=(vmem, vmem, anywhere, anywhere, anywhere, anywhere, anywhere, vmem),
        scratch_shapes=scratch
        + [
            pltpu.SemaphoreType.DMA((ID_COUNT,)),
            pltpu.SemaphoreType.DMA((ID_COUNT,)),
            pltpu.SemaphoreType.DMA((10,)),
        ],
        compiler_params=pltpu.CompilerParams(
            collective_id=0, has_side_effects=True, vmem_limit_bytes=67043328
        ),
        name="whole_block",
    )(tokens[0], out_grad[0], small, ada_weight, adab, wqkv, proj_weight, wfc1, wfc2)
    grad_qkv = (
        oqkv.reshape(4, 72, 3, 4, 72).transpose(1, 2, 3, 0, 4).reshape(72, 3 * WIDTH).astype(f32)
    )
    grad_fc1 = ofc1.reshape(4, 72, 16, 72).transpose(1, 2, 0, 3).reshape(72, HIDDEN).astype(f32)
    grad_fc2 = ofc2.reshape(288, WIDTH).astype(f32)

    def mine(vector, count):
        return lax.dynamic_slice_in_dim(vector, fsdp_at * count, count, 0)

    by_head = osum[12:16, :QKV].reshape(4, 3, 4, 72).transpose(1, 2, 0, 3).reshape(3 * WIDTH)
    return (
        out[None],
        tgrad[None],
        oada,
        mine(osum[:6].reshape(-1), 432),
        grad_qkv,
        mine(jnp.concatenate([by_head[:WIDTH], by_head[2 * WIDTH :]]), 144),
        oproj.astype(f32),
        mine(osum[7], 72),
        grad_fc1,
        mine(osum[8:12].reshape(4, 16, 72).transpose(1, 0, 2).reshape(-1), 288),
        grad_fc2,
        mine(osum[6], 72),
    )


def solution(mesh):
    in_specs = (
        P(("fsdp", "dp"), None, None),
        P(("fsdp", "dp"), None),
        P(("fsdp", "dp"), None),
        P("fsdp", None),
        P("fsdp"),
        P("fsdp", None),
        P("fsdp"),
        P("fsdp", None),
        P("fsdp"),
        P("fsdp", None),
        P("fsdp"),
        P("fsdp", None),
        P("fsdp"),
        P(("fsdp", "dp"), None, None),
    )
    out_specs = (
        P(("fsdp", "dp"), None, None),
        P(("fsdp", "dp"), None, None),
        P("fsdp", None),
        P("fsdp"),
        P("fsdp", None),
        P("fsdp"),
        P("fsdp", None),
        P("fsdp"),
        P("fsdp", None),
        P("fsdp"),
        P("fsdp", None),
        P("fsdp"),
    )
    fits = (mesh.shape["fsdp"], mesh.shape["dp"]) == (16, 2)
    return jax.shard_map(
        one_kernel if fits else general_form, mesh=mesh, in_specs=in_specs, out_specs=out_specs, check_vma=False
    )
```

```python
import functools

import jax
import jax.numpy as jnp
from jax import lax
from jax.experimental import pallas as pl
from jax.experimental.pallas import tpu as pltpu
from jax.sharding import PartitionSpec as P

HEADS = 16
HEAD_DIM = 72


root_half = 0.7978845608028654
norm_eps = 1e-06
masked_score = -1e30


def gelu_tanh(stream):
    return (
        0.5 * stream * (1.0 + jnp.tanh(root_half * (stream + 0.044715 * stream * stream * stream)))
    )


def gelu_slope(stream):
    tanh_inner = jnp.tanh(root_half * (stream + 0.044715 * stream * stream * stream))
    return 0.5 * (1.0 + tanh_inner) + 0.5 * stream * (1.0 - tanh_inner * tanh_inner) * root_half * (
        1.0 + 3.0 * 0.044715 * stream * stream
    )


def normalize(stream):
    centre = jnp.mean(stream, axis=-1, keepdims=True)
    centred = stream - centre
    inv_std = lax.rsqrt(jnp.mean(centred * centred, axis=-1, keepdims=True) + norm_eps)
    return (centred * inv_std, inv_std)


def normalize_back(incoming, normed, inv_std):
    return inv_std * (
        incoming
        - jnp.mean(incoming, axis=-1, keepdims=True)
        - normed * jnp.mean(incoming * normed, axis=-1, keepdims=True)
    )


def head_scores(projected, same_doc, head_index, model_width):
    query_part = lax.dynamic_slice_in_dim(projected, head_index * HEAD_DIM, HEAD_DIM, 1)
    key_part = lax.dynamic_slice_in_dim(projected, model_width + head_index * HEAD_DIM, HEAD_DIM, 1)
    value_part = lax.dynamic_slice_in_dim(
        projected, 2 * model_width + head_index * HEAD_DIM, HEAD_DIM, 1
    )
    raw_scores = jnp.einsum(
        "qd,kd->qk", query_part, key_part, preferred_element_type=jnp.float32
    ) * HEAD_DIM ** (-0.5)
    return (jnp.where(same_doc, raw_scores, masked_score), query_part, key_part, value_part)


def merge_heads(stacked, model_width):
    return jnp.transpose(stacked, (1, 0, 2)).reshape(stacked.shape[1], model_width)


def attend_row(projected, segments_row, model_width):
    same_doc = segments_row[:, None] == segments_row[None, :]

    def one_head(head_index):
        scores, query_part, key_part, value_part = head_scores(
            projected, same_doc, head_index, model_width
        )
        top_score = jnp.max(scores, axis=-1, keepdims=True)
        exp_scores = jnp.exp(scores - top_score)
        denominator = jnp.sum(exp_scores, axis=-1, keepdims=True)
        probabilities = (exp_scores / denominator).astype(jnp.bfloat16)
        mixed_heads = jnp.dot(probabilities, value_part, preferred_element_type=jnp.float32)
        return (mixed_heads, (top_score + jnp.log(denominator))[:, 0])

    mixed_heads, log_total = lax.map(one_head, jnp.arange(HEADS))
    return (merge_heads(mixed_heads, model_width).astype(jnp.bfloat16), log_total)


def attend_back(projected, segments_row, log_total, d_mixed, model_width):
    same_doc = segments_row[:, None] == segments_row[None, :]
    head_scale = HEAD_DIM ** (-0.5)

    def one_head(head_index):
        scores, query_part, key_part, value_part = head_scores(
            projected, same_doc, head_index, model_width
        )
        d_head = lax.dynamic_slice_in_dim(d_mixed, head_index * HEAD_DIM, HEAD_DIM, 1)
        lse_row = lax.dynamic_index_in_dim(log_total, head_index, 0, keepdims=False)
        probabilities = jnp.exp(scores - lse_row[:, None])
        prob_low = probabilities.astype(jnp.bfloat16)
        d_probs = jnp.einsum("qd,kd->qk", d_head, value_part, preferred_element_type=jnp.float32)
        d_value = jnp.einsum("qk,qd->kd", prob_low, d_head, preferred_element_type=jnp.float32)
        d_scores = (
            probabilities * (d_probs - jnp.sum(d_probs * probabilities, axis=-1, keepdims=True))
        ).astype(jnp.bfloat16)
        d_query = (
            jnp.einsum("qk,kd->qd", d_scores, key_part, preferred_element_type=jnp.float32)
            * head_scale
        )
        d_key = (
            jnp.einsum("qk,qd->kd", d_scores, query_part, preferred_element_type=jnp.float32)
            * head_scale
        )
        return (d_query, d_key, d_value)

    d_query, d_key, d_value = lax.map(one_head, jnp.arange(HEADS))
    merged = [
        merge_heads(d_query, model_width),
        merge_heads(d_key, model_width),
        merge_heads(d_value, model_width),
    ]
    return jnp.concatenate(merged, axis=-1).astype(jnp.bfloat16)


def general_form(
    tokens,
    cond,
    segment_ids,
    ada_weight,
    ada_bias,
    qkv_weight,
    qv_bias,
    proj_weight,
    proj_bias,
    fc1_weight,
    fc1_bias,
    fc2_weight,
    fc2_bias,
    out_grad,
):
    row_count, seq_len, model_width = tokens.shape
    ff_width = fc1_weight.shape[1]
    stream = tokens.astype(jnp.float32)
    cond_float = cond.astype(jnp.float32)
    cond_act = (cond_float / (1.0 + jnp.exp(-cond_float))).astype(jnp.bfloat16)
    fsdp_at, dp_at = lax.axis_index("fsdp"), lax.axis_index("dp")
    dp_size = lax.axis_size("dp")
    slice_width, bias_width = ada_weight.shape[0], ada_bias.shape[0]
    act_all = lax.all_gather(cond_act, ("fsdp", "dp"), axis=0, tiled=True)
    act_mine = lax.dynamic_slice_in_dim(act_all, fsdp_at * slice_width, slice_width, 1)
    partial = jnp.dot(act_mine, ada_weight, preferred_element_type=jnp.float32)
    bias_row = lax.dynamic_update_slice_in_dim(
        jnp.zeros((6 * model_width,), jnp.float32),
        ada_bias.astype(jnp.float32),
        fsdp_at * bias_width,
        0,
    )
    partial = (partial + bias_row).reshape(-1, dp_size, row_count, 6 * model_width)
    partial = lax.dynamic_index_in_dim(partial, dp_at, 1, keepdims=False)
    modulation = lax.psum_scatter(
        partial.reshape(-1, 6 * model_width), "fsdp", scatter_dimension=0, tiled=True
    )
    pieces = [
        modulation[:, None, section * model_width : (section + 1) * model_width]
        for section in range(6)
    ]
    shift_one, scale_one, gate_one, shift_two, scale_two, gate_two = pieces
    qkv_full, qv_bias_full, proj_full, proj_bias_full = (
        lax.all_gather(qkv_weight, "fsdp", axis=0, tiled=True),
        lax.all_gather(qv_bias, "fsdp", axis=0, tiled=True),
        lax.all_gather(proj_weight, "fsdp", axis=0, tiled=True),
        lax.all_gather(proj_bias, "fsdp", axis=0, tiled=True),
    )
    normed_one, inv_one = normalize(stream)
    hidden_one = (normed_one * (1.0 + scale_one) + shift_one).astype(jnp.bfloat16)
    qv_float = qv_bias_full.astype(jnp.float32)
    qkv_bias = jnp.concatenate(
        [qv_float[:model_width], jnp.zeros((model_width,), jnp.float32), qv_float[model_width:]]
    )
    projected = (
        jnp.dot(hidden_one, qkv_full, preferred_element_type=jnp.float32) + qkv_bias
    ).astype(jnp.bfloat16)

    def row_forward(row_items):
        return attend_row(row_items[0], row_items[1], model_width)

    mixed_rows, log_total = lax.map(row_forward, (projected, segment_ids))
    branch_one = jnp.dot(
        mixed_rows, proj_full, preferred_element_type=jnp.float32
    ) + proj_bias_full.astype(jnp.float32)
    resid_one = stream + gate_one * branch_one
    fc1_full, fc1_bias_full, fc2_full, fc2_bias_full = (
        lax.all_gather(fc1_weight, "fsdp", axis=0, tiled=True),
        lax.all_gather(fc1_bias, "fsdp", axis=0, tiled=True),
        lax.all_gather(fc2_weight, "fsdp", axis=0, tiled=True),
        lax.all_gather(fc2_bias, "fsdp", axis=0, tiled=True),
    )
    normed_two, inv_two = normalize(resid_one)
    hidden_two = (normed_two * (1.0 + scale_two) + shift_two).astype(jnp.bfloat16)
    pre_act = jnp.dot(
        hidden_two, fc1_full, preferred_element_type=jnp.float32
    ) + fc1_bias_full.astype(jnp.float32)
    active = gelu_tanh(pre_act).astype(jnp.bfloat16)
    branch_two = jnp.dot(
        active, fc2_full, preferred_element_type=jnp.float32
    ) + fc2_bias_full.astype(jnp.float32)
    output = (resid_one + gate_two * branch_two).astype(jnp.bfloat16)
    d_out = out_grad.astype(jnp.float32)
    fc1_back, fc2_back = (
        lax.all_gather(fc1_weight, "fsdp", axis=0, tiled=True),
        lax.all_gather(fc2_weight, "fsdp", axis=0, tiled=True),
    )
    d_gate_two = jnp.sum(d_out * branch_two, axis=1)
    d_branch_two = (d_out * gate_two).astype(jnp.bfloat16)
    fc2_shard = lax.psum_scatter(
        jnp.einsum("rsf,rsd->fd", active, d_branch_two, preferred_element_type=jnp.float32).astype(
            jnp.bfloat16
        ),
        "fsdp",
        scatter_dimension=0,
        tiled=True,
    )
    grad_fc2_bias = jnp.sum(d_branch_two.astype(jnp.float32), axis=(0, 1))
    d_active = jnp.einsum("rsd,fd->rsf", d_branch_two, fc2_back, preferred_element_type=jnp.float32)
    d_pre = (d_active * gelu_slope(pre_act)).astype(jnp.bfloat16)
    grad_fc1_bias = jnp.sum(d_pre.astype(jnp.float32), axis=(0, 1))
    d_hidden_two = jnp.einsum("rsf,ef->rse", d_pre, fc1_back, preferred_element_type=jnp.float32)
    d_scale_two = jnp.sum(d_hidden_two * normed_two, axis=1)
    d_shift_two = jnp.sum(d_hidden_two, axis=1)
    d_resid = d_out + normalize_back(d_hidden_two * (1.0 + scale_two), normed_two, inv_two)
    qkv_back, proj_back = (
        lax.all_gather(qkv_weight, "fsdp", axis=0, tiled=True),
        lax.all_gather(proj_weight, "fsdp", axis=0, tiled=True),
    )
    d_gate_one = jnp.sum(d_resid * branch_one, axis=1)
    d_branch_one = (d_resid * gate_one).astype(jnp.bfloat16)
    grad_proj_bias = jnp.sum(d_branch_one.astype(jnp.float32), axis=(0, 1))
    d_mixed = jnp.einsum(
        "rsd,ed->rse", d_branch_one, proj_back, preferred_element_type=jnp.float32
    ).astype(jnp.bfloat16)

    def row_backward(row_items):
        return attend_back(row_items[0], row_items[1], row_items[2], row_items[3], model_width)

    d_projected = lax.map(row_backward, (projected, segment_ids, log_total, d_mixed))
    d_proj_float = d_projected.astype(jnp.float32)
    grad_qv_bias = jnp.concatenate(
        [
            jnp.sum(d_proj_float[..., :model_width], axis=(0, 1)),
            jnp.sum(d_proj_float[..., 2 * model_width :], axis=(0, 1)),
        ]
    )
    d_hidden_one = jnp.einsum(
        "rsf,ef->rse", d_projected, qkv_back, preferred_element_type=jnp.float32
    )
    d_scale_one = jnp.sum(d_hidden_one * normed_one, axis=1)
    d_shift_one = jnp.sum(d_hidden_one, axis=1)
    tokens_grad = (
        d_resid + normalize_back(d_hidden_one * (1.0 + scale_one), normed_one, inv_one)
    ).astype(jnp.bfloat16)
    d_modulation = jnp.concatenate(
        [d_shift_one, d_scale_one, d_gate_one, d_shift_two, d_scale_two, d_gate_two], axis=-1
    ).astype(jnp.bfloat16)
    d_mod_all = lax.all_gather(d_modulation, ("fsdp", "dp"), axis=0, tiled=True)
    grad_ada = jnp.einsum("rd,re->de", act_mine, d_mod_all, preferred_element_type=jnp.float32)
    grad_ada_bias = jnp.sum(
        lax.dynamic_slice_in_dim(d_mod_all, fsdp_at * bias_width, bias_width, 1).astype(jnp.float32),
        axis=0,
    )

    def owners(term):
        return lax.psum_scatter(
            term.astype(jnp.bfloat16), "fsdp", scatter_dimension=0, tiled=True
        )

    qkv_shard = owners(
        jnp.einsum("rse,rsf->ef", hidden_one, d_projected, preferred_element_type=jnp.float32)
    )
    proj_shard = owners(
        jnp.einsum("rse,rsd->ed", mixed_rows, d_branch_one, preferred_element_type=jnp.float32)
    )
    fc1_shard = owners(
        jnp.einsum("rse,rsf->ef", hidden_two, d_pre, preferred_element_type=jnp.float32)
    )
    bias_shards = (
        None,
        lax.psum_scatter(
            grad_qv_bias.astype(jnp.bfloat16), "fsdp", scatter_dimension=0, tiled=True
        ).astype(jnp.float32),
        lax.psum_scatter(
            grad_proj_bias.astype(jnp.bfloat16), "fsdp", scatter_dimension=0, tiled=True
        ).astype(jnp.float32),
        lax.psum_scatter(
            grad_fc1_bias.astype(jnp.bfloat16), "fsdp", scatter_dimension=0, tiled=True
        ).astype(jnp.float32),
        lax.psum_scatter(
            grad_fc2_bias.astype(jnp.bfloat16), "fsdp", scatter_dimension=0, tiled=True
        ).astype(jnp.float32),
    )
    summed = (
        grad_ada,
        grad_ada_bias,
        lax.psum(qkv_shard.astype(jnp.bfloat16), "dp").astype(jnp.float32),
        lax.psum(bias_shards[1].astype(jnp.bfloat16), "dp").astype(jnp.float32),
        lax.psum(proj_shard.astype(jnp.bfloat16), "dp").astype(jnp.float32),
        lax.psum(bias_shards[2].astype(jnp.bfloat16), "dp").astype(jnp.float32),
        lax.psum(fc1_shard.astype(jnp.bfloat16), "dp").astype(jnp.float32),
        lax.psum(bias_shards[3].astype(jnp.bfloat16), "dp").astype(jnp.float32),
        lax.psum(fc2_shard, "dp").astype(jnp.float32),
        lax.psum(bias_shards[4].astype(jnp.bfloat16), "dp").astype(jnp.float32),
    )
    return (
        output,
        tokens_grad,
        summed[0],
        summed[1],
        summed[2],
        summed[3],
        summed[4],
        summed[5],
        summed[6],
        summed[7],
        summed[8],
        summed[9],
    )


MESH_ID = pl.DeviceIdType.MESH
f32 = jnp.float32
bf16 = jnp.bfloat16

SEQ = 256
WIDTH = 1152
HIDDEN = 4608
PART = 1152
QKV = 864
PAD = 128
LOCAL = 4


def dot_nn(left, right):
    return lax.dot_general(left, right, (((1,), (0,)), ((), ())), preferred_element_type=f32)


def dot_nt(left, right):
    return lax.dot_general(left, right, (((1,), (1,)), ((), ())), preferred_element_type=f32)


def dot_tn(left, right):
    return lax.dot_general(left, right, (((0,), (0,)), ((), ())), preferred_element_type=f32)


def iota(shape, axis):
    return lax.broadcasted_iota(jnp.int32, shape, axis)


def whole_part(value, divisor):
    return jnp.floor((value + 0.5) * (1.0 / divisor))


class Ids:
    def __init__(self):
        self.used = 0

    def take(self, count):
        start = self.used
        self.used += count
        return start


IDS = Ids()
IDS.small_y, IDS.small_z, IDS.small_c = IDS.take(1), IDS.take(6), IDS.take(1)
IDS.small_x, IDS.small_d = IDS.take(1), IDS.take(1)
IDS.mod_c, IDS.mod_y, IDS.mod_z = IDS.take(1), IDS.take(1), IDS.take(3)
IDS.core = [IDS.take(1) for _ in range(3)]
IDS.z = [IDS.take(3) for _ in range(4)]
IDS.y = [IDS.take(4) for _ in range(4)]
IDS.h1, IDS.h2, IDS.d2, IDS.d1 = IDS.take(3), IDS.take(3), IDS.take(3), IDS.take(3)
IDS.r1, IDS.r2, IDS.r3, IDS.r4 = IDS.take(3), IDS.take(3), IDS.take(3), IDS.take(3)
IDS.gy = [IDS.take(4) for _ in range(4)]
IDS.gz = [IDS.take(3) for _ in range(4)]
IDS.gf = [IDS.take(3) for _ in range(4)]
IDS.end_y, IDS.end_z, IDS.end_x, IDS.end_c = IDS.take(1), IDS.take(6), IDS.take(1), IDS.take(1)
ID_COUNT = IDS.used

SCRATCH = (
    ((32, 8, 384), f32),
    ((16, 8, WIDTH), f32),
    ((8, 8, WIDTH), f32),
    ((4, 8, WIDTH), f32),
    ((3, 8, WIDTH), f32),
    ((8, WIDTH), f32),
    ((72, QKV), bf16),
    ((72, PART), bf16),
    ((72, WIDTH), bf16),
    ((72, QKV), bf16),
    ((72, PART), bf16),
    ((72, WIDTH), bf16),
    ((WIDTH, QKV), bf16),
    ((WIDTH, PART), bf16),
    ((PART, WIDTH), bf16),
    ((4, 72, WIDTH), bf16),
    ((288, WIDTH), bf16),
    ((1024, WIDTH), bf16),
    ((1024, WIDTH), bf16),
    ((1024, WIDTH), bf16),
    ((1024, 12 * PAD), bf16),
    ((16, SEQ, SEQ), bf16),
    ((1024, 288), bf16),
    ((1024, PART), bf16),
    ((1024, PART), bf16),
    ((1024, QKV), bf16),
    ((3, SEQ, WIDTH), bf16),
    ((3, SEQ, WIDTH), bf16),
    ((SEQ, WIDTH), bf16),
    ((SEQ, WIDTH), bf16),
    ((SEQ, WIDTH), bf16),
    ((SEQ, WIDTH), f32),
    ((SEQ, WIDTH), f32),
    ((SEQ, WIDTH), f32),
    ((SEQ, WIDTH), f32),
    ((16, WIDTH), f32),
    ((8, WIDTH), f32),
    ((WIDTH, QKV), bf16),
    ((WIDTH, PART), bf16),
    ((PART, WIDTH), bf16),
    ((4, 72, WIDTH), bf16),
    ((4, 144, QKV), bf16),
    ((4, 144, PART), bf16),
    ((4, 144, WIDTH), bf16),
    ((4, 72, WIDTH), bf16),
    ((3, 144, QKV), bf16),
    ((3, 144, PART), bf16),
    ((3, 144, WIDTH), bf16),
    ((3, 72, WIDTH), bf16),
    ((72, QKV), bf16),
    ((72, PART), bf16),
    ((72, WIDTH), bf16),
    ((72, QKV), bf16),
    ((72, PART), bf16),
    ((72, WIDTH), bf16),
    ((4, 72, QKV), bf16),
    ((4, 72, PART), bf16),
    ((4, 72, WIDTH), bf16),
    ((72, WIDTH), bf16),
    ((32, 16, WIDTH), bf16),
)


def block_kernel(
    tok, og, small, ada, adab, wqkv, wproj, wfc1, wfc2, out,
    tgrad, oada, oqkv, oproj, ofc1, ofc2, osum, S, modp, modc,
    mody, modz, mod, own_qkv, own_fc1, own_fc2, xr_qkv, xr_fc1, xr_fc2, G_qkv,
    G_fc1, G_fc2, G_proj, W_proj, H1, H2, D2, qp, P, mixed,
    active, slope, dprj, rrA, rrB, sA, sB, sX, keep, own,
    b1, resid, acc, bias, g_qkv, g_fc1, g_fc2, g_proj, yr_qkv, yr_fc1,
    yr_fc2, yr_proj, zr_qkv, zr_fc1, zr_fc2, zr_proj, fa_qkv, fa_fc1, fa_fc2, fb_qkv,
    fb_fc1, fb_fc2, fr_qkv, fr_fc1, fr_fc2, p_out, E, snd, rcv, loc,
):
    own_w, xr_w, G_w = (own_qkv, own_fc1, own_fc2), (xr_qkv, xr_fc1, xr_fc2), (G_qkv, G_fc1, G_fc2)
    w_in, w_out = (wqkv, wfc1, wfc2), (oqkv, ofc1, ofc2)
    yr_w, zr_w = (yr_qkv, yr_fc1, yr_fc2), (zr_qkv, zr_fc1, zr_fc2)
    fa_w, fb_w, fr_w = (fa_qkv, fa_fc1, fa_fc2), (fb_qkv, fb_fc1, fb_fc2), (fr_qkv, fr_fc1, fr_fc2)
    f = lax.axis_index("fsdp")
    x = lax.axis_index("dp")
    z = lax.div(f, 4)
    y = lax.rem(lax.div(f, 2), 2)
    c = lax.rem(f, 2)
    q = 2 * x + c
    qp_, qx_, qd_ = 2 * x + 1 - c, 2 * (1 - x) + c, 2 * (1 - x) + 1 - c

    def dev(zz, yy, cc, xx):
        return ((zz * 2 + yy) * 2 + cc, xx)

    mate, xnb, diag, ynb = dev(z, y, 1 - c, x), dev(z, y, c, 1 - x), dev(z, y, 1 - c, 1 - x), dev(z, 1 - y, c, x)

    def z_to(k):
        return lax.rem(z + k, 4)

    def z_from(k):
        return lax.rem(z + 4 - k, 4)

    def znb(k):
        return dev(z_to(k), y, c, x)

    def rc(src, dst, ident, to):
        return pltpu.make_async_remote_copy(
            src_ref=src, dst_ref=dst, send_sem=snd.at[ident], recv_sem=rcv.at[ident],
            device_id=to, device_id_type=MESH_ID,
        )

    pending = []

    def send(src, dst, ident, to):
        rc(src, dst, ident, to).start()
        pending.append((src, ident, to))

    def got(dst, ident):
        rc(dst, dst, ident, mate).wait_recv()

    def sent(src, ident):
        rc(src, src, ident, mate).wait_send()

    def settle(first):
        keep_on = []
        for item in pending:
            if item[1] in first:
                sent(item[0], item[1])
            else:
                keep_on.append(item)
        pending[:] = keep_on

    barrier = pltpu.get_barrier_semaphore()
    neighbours = [mate, xnb, diag, ynb, znb(1), znb(2), znb(3)]
    for to in neighbours:
        pl.semaphore_signal(barrier, inc=1, device_id=to, device_id_type=MESH_ID)
    pl.semaphore_wait(barrier, len(neighbours))


    def slot_of(cc, xx, yy, zz):
        return ((cc * 2 + xx) * 2 + yy) * 4 + zz

    my_slot = slot_of(c, x, y, z)
    send(small, S.at[my_slot], IDS.small_y, ynb)
    kinds = (0, 1, 2)
    for kind in kinds:
        send(w_in[kind].at[qp_], xr_w[kind], IDS.core[kind], mate)
    own_copies = []
    for at, kind in enumerate(kinds):
        own_copies.append(pltpu.make_async_copy(w_in[kind].at[q], own_w[kind], loc.at[at]))
        own_copies[-1].start()
    S[my_slot] = small[...]
    acc[...] = jnp.zeros((16, WIDTH), f32)
    in_column = y == x
    proj_copy = pltpu.make_async_copy(wproj, G_proj.at[z], loc.at[3])

    def chip_rows(zz, yy):
        return pl.ds(pl.multiple_of((2 * zz + yy) * 144, 16), 144)

    def own_part(kind):
        return G_w[kind].at[chip_rows(z, y), :]

    def assemble(kind):
        own_copies[kind].wait()
        got(xr_w[kind], IDS.core[kind])
        mine = own_w[kind][...].astype(f32)
        other = xr_w[kind][...].astype(f32)
        low = jnp.where(c == 0, mine, other)
        high = jnp.where(c == 0, other, mine)
        G_w[kind][chip_rows(z, y), :] = jnp.concatenate([low, high], axis=0).astype(bf16)

    def own_y(kind):
        send(own_part(kind), own_part(kind), IDS.y[kind], ynb)

    def own_z(kind, steps):
        for k in steps:
            send(own_part(kind), own_part(kind), IDS.z[kind] + k - 1, znb(k))

    STEPS = (1, 3, 2)

    def forward(kind, k):
        part = G_w[kind].at[chip_rows(z_from(k), y), :]
        got(part, IDS.z[kind] + k - 1)
        send(part, part, IDS.y[kind] + k, ynb)

    def arrived(kind):
        other = 1 - y
        got(G_w[kind].at[chip_rows(z, other), :], IDS.y[kind])
        for k in STEPS:
            got(G_w[kind].at[chip_rows(z_from(k), other), :], IDS.y[kind] + k)

    def proj_z():
        @pl.when(in_column)
        def _():
            proj_copy.start()
            for k in STEPS:
                rc(wproj, G_proj.at[z], IDS.z[3] + k - 1, znb(k)).start()

    def proj_y():
        @pl.when(in_column)
        def _():
            rc(wproj, G_proj.at[z], IDS.y[3], ynb).start()

    def proj_forward(k):
        @pl.when(in_column)
        def _():
            part = G_proj.at[z_from(k)]
            got(part, IDS.z[3] + k - 1)
            rc(part, part, IDS.y[3] + k, ynb).start()

    def proj_arrived():
        @pl.when(in_column)
        def _():
            proj_copy.wait()
            for k in (1, 2, 3):
                sent(wproj, IDS.z[3] + k - 1)
            sent(wproj, IDS.y[3])
            for k in STEPS:
                sent(G_proj.at[z_from(k)], IDS.y[3] + k)

        @pl.when(jnp.logical_not(in_column))
        def _():
            got(G_proj.at[z], IDS.y[3])
            for k in STEPS:
                got(G_proj.at[z_from(k)], IDS.y[3] + k)

        W_proj[...] = jnp.concatenate(
            [G_proj[head].astype(f32) for head in range(LOCAL)], axis=0
        ).astype(bf16)

    got(S.at[slot_of(c, x, 1 - y, z)], IDS.small_y)
    for k in (2, 1, 3):
        for yy in range(2):
            part = S.at[slot_of(c, x, yy, z)]
            send(part, part, IDS.small_z + 2 * (k - 1) + yy, znb(k))
    assemble(0)
    own_y(0)
    own_z(0, (1,))
    for k in (1, 2, 3):
        for yy in range(2):
            got(S.at[slot_of(c, x, yy, z_from(k))], IDS.small_z + 2 * (k - 1) + yy)
    eight = lambda cc, xx: S.at[pl.ds((cc * 2 + xx) * 8, 8)]
    send(eight(c, x), eight(c, x), IDS.small_c, mate)
    send(eight(c, x), eight(c, x), IDS.small_x, xnb)
    assemble(1)

    def pick_columns(rows):
        total = None
        for piece in range(3):
            kk = iota((384, PAD), 0) + piece * 384
            jj = iota((384, PAD), 1)
            chosen = ((kk == 72 * f + jj) & (jj < 72)).astype(f32).astype(bf16)
            term = dot_nn(rows(piece), chosen)
            total = term if total is None else total + term
        return total.astype(bf16)

    got(eight(1 - c, x), IDS.small_c)
    act = pick_columns(
        lambda piece: jnp.concatenate(
            [S[pl.ds((cc * 2 + x) * 8, 8), piece, :] for cc in range(2)], axis=0
        ).astype(bf16)
    )[:, :72]
    for section in range(6):
        modp[:, section, :] = dot_nn(
            act, ada[:, section * WIDTH : (section + 1) * WIDTH]
        ) + adab[section : section + 1, :]
    for section in (6, 7):
        modp[:, section, :] = jnp.zeros((16, WIDTH), f32)
    theirs, ours = modp.at[pl.ds((1 - c) * 8, 8)], modp.at[pl.ds(c * 8, 8)]
    send(theirs, modc, IDS.mod_c, mate)
    assemble(2)
    got(modc, IDS.mod_c)
    for at in range(8):
        ours[at] += modc[at]
    send(modp.at[pl.ds(c * 8 + (1 - y) * 4, 4)], mody, IDS.mod_y, ynb)
    forward(0, 1)
    got(mody, IDS.mod_y)
    base = c * 8 + y * 4
    for at in range(4):
        modp[base + at] += mody[at]
    for k in (2, 1, 3):
        send(modp.at[base + z_to(k)], modz.at[k - 1], IDS.mod_z + k - 1, znb(k))
    own_z(0, (3, 2))
    proj_z()
    own_z(1, STEPS)
    own_z(2, STEPS)
    got(eight(c, 1 - x), IDS.small_x)
    send(eight(c, 1 - x), eight(c, 1 - x), IDS.small_d, mate)

    def place(row, width, lane_of, owner_of):
        kk = iota((384, width), 1).astype(f32)
        jj = iota((384, width), 0).astype(f32)
        chosen = (jj == lane_of(kk)).astype(f32).astype(bf16)
        spread = dot_nn(row.astype(bf16), chosen)
        at = iota((16, width), 0)
        slot_f = ((lax.rem(at, 4) * 2 + lax.rem(lax.div(at, 4), 2)) * 2 + lax.div(at, 8)).astype(f32)
        mine = slot_f == owner_of(iota((16, width), 1).astype(f32))
        return jnp.sum(jnp.where(mine, spread, 0.0), axis=0, keepdims=True)

    def plane(piece):
        return jnp.concatenate([S[pl.ds((cc * 2 + x) * 8, 8), piece, :] for cc in range(2)], axis=0)

    def mod72(kk):
        return kk - 72.0 * whole_part(kk, 72)

    by72 = lambda kk: whole_part(kk, 72)
    qf, xf, cf = q.astype(f32), x.astype(f32), c.astype(f32)
    row3, row4 = plane(3), plane(4)
    bias[0:1, :] = place(row3, WIDTH, lambda kk: 144.0 + mod72(kk), by72)
    bias[1:2, :] = place(row3, WIDTH, lambda kk: 216.0 + mod72(kk), by72)
    bias[2:3, :] = place(row4, WIDTH, lambda kk: 72.0 * qf + mod72(kk), by72)

    def qkv_owner(kk):
        third = whole_part(kk, 288)
        head = whole_part(kk - 288.0 * third, 72)
        owner = 2.0 * head + xf + 4.0 * third
        return jnp.where((third == 1.0) | (third > 2.5), -1.0, owner)

    bias[3:4, :] = place(row3, WIDTH, lambda kk: 72.0 * cf + mod72(kk), qkv_owner)

    for k in (1, 2, 3):
        got(modz.at[k - 1], IDS.mod_z + k - 1)
    mod[...] = modp[base + z] + modz[0] + modz[1] + modz[2]

    def row_of(section):
        return mod[section : section + 1, :]

    def slot_rows(slot):
        return pl.ds(pl.multiple_of(slot * SEQ, SEQ), SEQ)

    TILE = 64

    def tiles(body):
        def step(at, carry):
            body(pl.multiple_of(at * TILE, TILE))
            return carry

        lax.fori_loop(0, SEQ // TILE, step, 0)


    def norm_one(at):
        normed, _ = normalize(tok[pl.ds(at, TILE), :].astype(f32))
        H1[pl.ds(pl.multiple_of(q * SEQ + at, TILE), TILE), :] = (
            normed * (1.0 + row_of(1)) + row_of(0)
        ).astype(bf16)

    tiles(norm_one)

    def spread_start(buf, ident):
        part = buf.at[slot_rows(q), :]
        send(part, part, ident, mate)
        send(part, part, ident + 1, xnb)

    def spread_mid(buf, ident):
        part = buf.at[slot_rows(qx_), :]
        got(part, ident + 1)
        send(part, part, ident + 2, mate)

    def spread_mate(buf, ident):
        got(buf.at[slot_rows(qp_), :], ident)

    def spread_end(buf, ident):
        got(buf.at[slot_rows(qd_), :], ident + 2)

    spread_start(H1, IDS.h1)

    def add_row(at, value):
        acc[at : at + 1, :] += jnp.sum(value, axis=0, keepdims=True)

    def out_gate(at):
        low = (og[pl.ds(at, TILE), :].astype(f32) * row_of(5)).astype(bf16)
        D2[pl.ds(pl.multiple_of(q * SEQ + at, TILE), TILE), :] = low
        add_row(6, low.astype(f32))

    tiles(out_gate)
    spread_start(D2, IDS.d2)
    spread_mate(H1, IDS.h1)
    forward(0, 3)
    forward(0, 2)
    proj_y()
    own_y(1)
    spread_mid(H1, IDS.h1)
    arrived(0)


    def project(slot):
        rows = slot_rows(slot)
        value = (dot_nn(H1[rows, :], G_qkv[...]) + bias[3:4, :QKV]).astype(bf16)
        blank = jnp.zeros((SEQ, PAD - HEAD_DIM), bf16)
        for at in range(12):
            qp[rows, at * PAD : (at + 1) * PAD] = jnp.concatenate(
                [value[:, at * HEAD_DIM : (at + 1) * HEAD_DIM], blank], axis=1
            )

    def attend(slot):
        rows = slot_rows(slot)
        where_seg = slot_of(lax.rem(slot, 2), lax.div(slot, 2), y, z)
        seg = S[where_seg, 5:6, :SEQ]
        seg_column = jnp.transpose(jnp.broadcast_to(seg, (8, SEQ)))[:, :1]
        same = seg_column == seg
        pieces = []
        for head in range(LOCAL):
            query = qp[rows, head * PAD : (head + 1) * PAD]
            key = qp[rows, (LOCAL + head) * PAD : (LOCAL + head + 1) * PAD]
            value = qp[rows, (2 * LOCAL + head) * PAD : (2 * LOCAL + head + 1) * PAD]
            scores = jnp.where(same, dot_nt(query, key) * HEAD_DIM ** (-0.5), masked_score)
            exp_scores = jnp.exp(scores - jnp.max(scores, axis=1, keepdims=True))
            probs = (exp_scores / jnp.sum(exp_scores, axis=1, keepdims=True)).astype(bf16)
            P[slot * LOCAL + head] = probs
            pieces.append(dot_nn(probs, value).astype(bf16)[:, :HEAD_DIM])
        mixed[rows, :] = jnp.concatenate(pieces, axis=1)

    def pair(body, group):
        def step(at, carry):
            body(2 * group + lax.rem(c + at, 2))
            return carry

        lax.fori_loop(0, 2, step, 0)

    got(eight(1 - c, 1 - x), IDS.small_d)
    pair(project, x)
    pair(attend, x)
    proj_forward(1)
    spread_end(H1, IDS.h1)
    pair(project, 1 - x)
    proj_forward(3)
    pair(attend, 1 - x)
    proj_forward(2)
    forward(1, 1)
    spread_mate(D2, IDS.d2)
    spread_mid(D2, IDS.d2)


    def reduce_first(partial, rr, ident):
        sA[...] = partial(qd_).astype(bf16)
        send(sA, rr.at[0], ident, mate)
        keep[...] = partial(qx_)
        sB[...] = partial(qp_).astype(bf16)

    def reduce_next(partial, rr, ident):
        got(rr.at[0], ident)
        sX[...] = (keep[...] + rr[0].astype(f32)).astype(bf16)
        send(sX, rr.at[2], ident + 2, xnb)
        send(sB, rr.at[1], ident + 1, mate)
        own[...] = partial(q)

    def reduce_last(rr, ident):
        got(rr.at[1], ident + 1)
        got(rr.at[2], ident + 2)
        settle((ident, ident + 1, ident + 2))

    def total_rows(rr, at):
        rows = pl.ds(at, TILE)
        return own[rows, :] + rr[1, rows, :].astype(f32) + rr[2, rows, :].astype(f32)

    proj_arrived()

    def part_one(slot):
        return dot_nn(mixed[slot_rows(slot), :], W_proj[...])

    reduce_first(part_one, rrA, IDS.r1)
    reduce_next(part_one, rrA, IDS.r1)
    forward(1, 3)
    own_y(2)
    reduce_last(rrA, IDS.r1)


    def norm_two(at):
        rows = pl.ds(at, TILE)
        branch = total_rows(rrA, at) + bias[0:1, :]
        b1[rows, :] = branch
        stream = tok[rows, :].astype(f32) + row_of(2) * branch
        resid[rows, :] = stream
        normed, _ = normalize(stream)
        H2[pl.ds(pl.multiple_of(q * SEQ + at, TILE), TILE), :] = (
            normed * (1.0 + row_of(4)) + row_of(3)
        ).astype(bf16)

    tiles(norm_two)
    spread_start(H2, IDS.h2)
    forward(1, 2)
    spread_end(D2, IDS.d2)
    spread_mate(H2, IDS.h2)
    spread_mid(H2, IDS.h2)
    arrived(1)

    CHUNK = 384

    def first_layer(slot):
        rows = slot_rows(slot)
        for at in range(0, PART, CHUNK):
            pre = dot_nn(H2[rows, :], G_fc1[:, at : at + CHUNK]) + bias[2:3, at : at + CHUNK]
            square = pre * pre
            bend = jnp.tanh(root_half * (pre + 0.044715 * square * pre))
            active[rows, at : at + CHUNK] = (0.5 * pre * (1.0 + bend)).astype(bf16)
            slope[rows, at : at + CHUNK] = (
                0.5 * (1.0 + bend)
                + 0.5 * pre * (1.0 - bend * bend) * root_half * (1.0 + 3.0 * 0.044715 * square)
            ).astype(bf16)

    pair(first_layer, x)
    forward(2, 1)
    spread_end(H2, IDS.h2)
    pair(first_layer, 1 - x)
    forward(2, 3)

    def cross(left, right, dest, width):
        for at in range(0, width, CHUNK):
            dest[at : at + CHUNK, :] = dot_tn(left[:, at : at + CHUNK], right[...]).astype(bf16)

    cross(active, D2, g_fc2, PART)

    def grad_start(kind, grads, steps):
        for k in steps:
            send(
                grads.at[chip_rows(z_to(k), 1 - y), :], yr_w[kind].at[k], IDS.gy[kind] + k, ynb
            )

    def add_block(grads, rows_at, extra):
        def step(at, carry):
            rows = pl.ds(pl.multiple_of(rows_at + at * 48, 16), 48)
            grads[rows, :] = (
                grads[rows, :].astype(f32) + extra[pl.ds(pl.multiple_of(at * 48, 16), 48), :].astype(f32)
            ).astype(bf16)
            return carry

        lax.fori_loop(0, 3, step, 0)

    def grad_mid(kind, grads, k):
        zz = z_to(k)
        got(yr_w[kind].at[k], IDS.gy[kind] + k)
        add_block(grads, (2 * zz + y) * 144, yr_w[kind].at[k])
        send(
            grads.at[chip_rows(zz, y), :], zr_w[kind].at[k - 1], IDS.gz[kind] + k - 1, znb(k)
        )

    def grad_end(kind, grads):
        got(yr_w[kind].at[0], IDS.gy[kind])
        for k in (1, 2, 3):
            got(zr_w[kind].at[k - 1], IDS.gz[kind] + k - 1)
        width = grads.shape[1]
        A, B, fr = fa_w[kind], fb_w[kind], fr_w[kind]
        for at in range(0, width, CHUNK):
            cols = slice(at, min(at + CHUNK, width))
            total = grads[chip_rows(z, y), cols].astype(f32) + yr_w[kind][0, :, cols].astype(f32)
            for k in range(3):
                total = total + zr_w[kind][k, :, cols].astype(f32)
            low, high = total[:72], total[72:]
            mine = jnp.where(c == 0, low, high).astype(bf16)
            A[:, cols] = mine
            B[:, cols] = jnp.where(c == 0, high, low).astype(bf16)
            fr[q, :, cols] = mine
        send(B, fr.at[q], IDS.gf[kind], mate)
        send(A, fr.at[q], IDS.gf[kind] + 1, xnb)
        send(B, fr.at[q], IDS.gf[kind] + 2, diag)

    out_copies = []

    def grad_out(kind, at):
        fr = fr_w[kind]
        for step, source in enumerate((qp_, qx_, qd_)):
            got(fr.at[source], IDS.gf[kind] + step)
        copy = pltpu.make_async_copy(fr, w_out[kind], loc.at[at])
        copy.start()
        out_copies.append(copy)

    grad_start(2, g_fc2, (1,))
    forward(2, 2)
    grad_start(2, g_fc2, (3, 2, 0))
    arrived(2)

    def back_hidden(slot):
        rows = slot_rows(slot)
        for at in range(0, PART, CHUNK):
            low = (
                dot_nt(D2[rows, :], G_fc2[at : at + CHUNK, :])
                * slope[rows, at : at + CHUNK].astype(f32)
            ).astype(bf16)
            slope[rows, at : at + CHUNK] = low
            acc[8:9, at : at + CHUNK] += jnp.sum(low.astype(f32), axis=0, keepdims=True)

    pair(back_hidden, x)
    pair(back_hidden, 1 - x)
    d_pre = slope
    settle(tuple(IDS.d2 + step for step in range(3)))
    D1 = D2
    def part_three(slot):
        return dot_nt(d_pre[slot_rows(slot), :], G_fc1[...])

    reduce_first(part_three, rrA, IDS.r3)
    reduce_next(part_three, rrA, IDS.r3)
    cross(H2, d_pre, g_fc1, WIDTH)
    grad_start(1, g_fc1, (1, 3, 2, 0))
    grad_mid(2, g_fc2, 1)
    reduce_last(rrA, IDS.r3)

    def back_two(at):
        rows = pl.ds(at, TILE)
        d_hidden = total_rows(rrA, at)
        normed, inv = normalize(resid[rows, :])
        add_row(3, d_hidden)
        add_row(4, d_hidden * normed)
        d_resid = og[rows, :].astype(f32) + normalize_back(d_hidden * (1.0 + row_of(4)), normed, inv)
        add_row(2, d_resid * b1[rows, :])
        low = (d_resid * row_of(2)).astype(bf16)
        add_row(7, low.astype(f32))
        D1[pl.ds(pl.multiple_of(q * SEQ + at, TILE), TILE), :] = low
        b1[rows, :] = d_resid

    tiles(back_two)
    spread_start(D1, IDS.d1)

    def part_two(slot):
        return dot_nn(active[slot_rows(slot), :], G_fc2[...])

    reduce_first(part_two, rrB, IDS.r2)
    reduce_next(part_two, rrB, IDS.r2)

    def finish_forward(at):
        rows = pl.ds(at, TILE)
        branch = total_rows(rrB, at) + bias[1:2, :]
        out[rows, :] = (resid[rows, :] + row_of(5) * branch).astype(bf16)
        add_row(5, og[rows, :].astype(f32) * branch)

    grad_mid(2, g_fc2, 3)
    spread_mate(D1, IDS.d1)


    def attend_backward(slot):
        rows = slot_rows(slot)
        d_mix = dot_nt(D1[rows, :], W_proj[...]).astype(bf16)
        blank = jnp.zeros((SEQ, PAD - HEAD_DIM), bf16)
        scale = HEAD_DIM ** (-0.5)
        d_query, d_key, d_value = [], [], []
        for head in range(LOCAL):
            query = qp[rows, head * PAD : (head + 1) * PAD]
            key = qp[rows, (LOCAL + head) * PAD : (LOCAL + head + 1) * PAD]
            value = qp[rows, (2 * LOCAL + head) * PAD : (2 * LOCAL + head + 1) * PAD]
            d_head = jnp.concatenate([d_mix[:, head * HEAD_DIM : (head + 1) * HEAD_DIM], blank], axis=1)
            probs = P[slot * LOCAL + head]
            d_probs = dot_nt(d_head, value)
            d_value.append(dot_tn(probs, d_head).astype(bf16)[:, :HEAD_DIM])
            wide = probs.astype(f32)
            d_scores = (wide * (d_probs - jnp.sum(d_probs * wide, axis=1, keepdims=True))).astype(bf16)
            d_query.append((dot_nn(d_scores, key) * scale).astype(bf16)[:, :HEAD_DIM])
            d_key.append((dot_tn(d_scores, query) * scale).astype(bf16)[:, :HEAD_DIM])
        value = jnp.concatenate(d_query + d_key + d_value, axis=1)
        dprj[rows, :] = value
        acc[9:10, :QKV] += jnp.sum(value.astype(f32), axis=0, keepdims=True)

    pair(attend_backward, x)
    spread_mid(D1, IDS.d1)
    grad_mid(2, g_fc2, 2)
    spread_end(D1, IDS.d1)
    pair(attend_backward, 1 - x)
    cross(H1, dprj, g_qkv, WIDTH)
    grad_start(0, g_qkv, (1, 3, 2, 0))
    grad_mid(1, g_fc1, 1)
    proj_grads = dot_tn(mixed[...], D1[...])
    for head in range(LOCAL):
        g_proj[head] = proj_grads[head * 72 : (head + 1) * 72].astype(bf16)

    @pl.when(jnp.logical_not(in_column))
    def _():
        for k in range(4):
            rc(g_proj.at[z_to(k)], yr_proj.at[k], IDS.gy[3] + k, ynb).start()

    def part_four(slot):
        return dot_nt(dprj[slot_rows(slot), :], G_qkv[...])

    settle((IDS.r2, IDS.r2 + 1))
    reduce_first(part_four, rrA, IDS.r4)
    reduce_last(rrB, IDS.r2)
    tiles(finish_forward)
    reduce_next(part_four, rrA, IDS.r4)
    grad_mid(1, g_fc1, 3)
    grad_mid(1, g_fc1, 2)
    grad_end(2, g_fc2)
    reduce_last(rrA, IDS.r4)

    def back_one(at):
        rows = pl.ds(at, TILE)
        d_hidden = total_rows(rrA, at)
        normed, inv = normalize(tok[rows, :].astype(f32))
        add_row(0, d_hidden)
        add_row(1, d_hidden * normed)
        tgrad[rows, :] = (
            b1[rows, :] + normalize_back(d_hidden * (1.0 + row_of(1)), normed, inv)
        ).astype(bf16)

    tiles(back_one)

    E[my_slot] = acc[...].astype(bf16)
    send(E.at[my_slot], E.at[my_slot], IDS.end_y, ynb)

    @pl.when(in_column)
    def _():
        for k in STEPS:
            zz = z_to(k)
            got(yr_proj.at[k], IDS.gy[3] + k)
            g_proj[zz] = (g_proj[zz].astype(f32) + yr_proj[k].astype(f32)).astype(bf16)
            rc(g_proj.at[zz], zr_proj.at[k - 1], IDS.gz[3] + k - 1, znb(k)).start()

    got(E.at[slot_of(c, x, 1 - y, z)], IDS.end_y)
    for k in (2, 1, 3):
        for yy in range(2):
            part = E.at[slot_of(c, x, yy, z)]
            send(part, part, IDS.end_z + 2 * (k - 1) + yy, znb(k))
    for k in STEPS:
        grad_mid(0, g_qkv, k)
    for k in (1, 2, 3):
        for yy in range(2):
            got(E.at[slot_of(c, x, yy, z_from(k))], IDS.end_z + 2 * (k - 1) + yy)
    group = lambda cc, xx: E.at[pl.ds((cc * 2 + xx) * 8, 8)]
    send(group(c, x), group(c, x), IDS.end_x, xnb)
    grad_end(1, g_fc1)

    @pl.when(in_column)
    def _():
        got(yr_proj.at[0], IDS.gy[3])
        total = g_proj[z].astype(f32) + yr_proj[0].astype(f32)
        for k in (1, 2, 3):
            got(zr_proj.at[k - 1], IDS.gz[3] + k - 1)
            total = total + zr_proj[k - 1].astype(f32)
        p_out[...] = total.astype(bf16)
        rc(p_out, p_out, IDS.gf[3], xnb).start()

    got(group(c, 1 - x), IDS.end_x)
    send(E.at[pl.ds(c * 16, 16)], E.at[pl.ds(c * 16, 16)], IDS.end_c, mate)
    grad_out(2, 0)

    @pl.when(jnp.logical_not(in_column))
    def _():
        got(p_out, IDS.gf[3])

    copy = pltpu.make_async_copy(p_out, oproj, loc.at[3])
    copy.start()
    out_copies.append(copy)
    got(E.at[pl.ds((1 - c) * 16, 16)], IDS.end_c)

    act_all = pick_columns(lambda piece: S[:, piece, :].astype(bf16))[:, :72]
    for section in range(6):
        rows = E[:, section, :]
        stage = (keep, own)[section // 3].at[(section % 3) * 72 : (section % 3 + 1) * 72, :]
        stage[...] = dot_tn(act_all, rows)
        copy = pltpu.make_async_copy(
            stage, oada.at[:, section * WIDTH : (section + 1) * WIDTH], loc.at[4 + section]
        )
        copy.start()
        out_copies.append(copy)
        osum[section : section + 1, :] = jnp.sum(rows.astype(f32), axis=0, keepdims=True)
    for section in (6, 7):
        osum[section : section + 1, :] = jnp.sum(E[:, section, :].astype(f32), axis=0, keepdims=True)
    for section in (8, 9):
        for quarter in range(4):
            start = ((quarter % 2) * 2 + quarter // 2) * 8
            at = 8 + 4 * (section - 8) + quarter
            osum[at : at + 1, :] = jnp.sum(
                E[start : start + 8, section, :].astype(f32), axis=0, keepdims=True
            )
    grad_out(1, 1)
    grad_end(0, g_qkv)
    grad_out(0, 2)
    for copy in out_copies:
        copy.wait()
    for src, ident, _ in pending:
        sent(src, ident)

    @pl.when(in_column)
    def _():
        for k in (1, 2, 3):
            sent(p_out, IDS.gz[3] + k - 1)
        sent(p_out, IDS.gf[3])

    @pl.when(jnp.logical_not(in_column))
    def _():
        for k in range(4):
            sent(p_out, IDS.gy[3] + k)


def one_kernel(
    tokens,
    cond,
    segment_ids,
    ada_weight,
    ada_bias,
    qkv_weight,
    qv_bias,
    proj_weight,
    proj_bias,
    fc1_weight,
    fc1_bias,
    fc2_weight,
    fc2_bias,
    out_grad,
):
    fsdp_at = lax.axis_index("fsdp")
    cond_float = cond[0].astype(f32)
    cond_act = (cond_float / (1.0 + jnp.exp(-cond_float))).astype(bf16).astype(f32)
    blank = lambda count: jnp.zeros((count,), f32)
    small = jnp.concatenate(
        [
            cond_act,
            qv_bias.astype(f32),
            proj_bias.astype(f32),
            fc2_bias.astype(f32),
            blank(96),
            fc1_bias.astype(f32),
            blank(96),
            segment_ids[0].astype(f32),
            blank(128 + 768),
        ]
    ).reshape(8, 384)
    adab = lax.dynamic_update_slice_in_dim(
        blank(8 * WIDTH), ada_bias.astype(f32), fsdp_at * 432, 0
    ).reshape(8, WIDTH)
    wqkv = qkv_weight.reshape(72, 3, 4, 4, 72).transpose(3, 0, 1, 2, 4).reshape(4, 72, QKV)
    wfc1 = fc1_weight.reshape(72, 16, 4, 72).transpose(2, 0, 1, 3).reshape(4, 72, PART)
    wfc2 = fc2_weight.reshape(4, 72, WIDTH)
    vmem = pl.BlockSpec(memory_space=pltpu.VMEM)
    anywhere = pl.BlockSpec(memory_space=pl.ANY)
    shape = jax.ShapeDtypeStruct
    scratch = [pltpu.VMEM(dims, kind) for dims, kind in SCRATCH]
    out, tgrad, oada, oqkv, oproj, ofc1, ofc2, osum = pl.pallas_call(
        block_kernel,
        out_shape=(
            shape((SEQ, WIDTH), bf16),
            shape((SEQ, WIDTH), bf16),
            shape((72, 6 * WIDTH), f32),
            shape((4, 72, QKV), bf16),
            shape((72, WIDTH), bf16),
            shape((4, 72, PART), bf16),
            shape((4, 72, WIDTH), bf16),
            shape((16, WIDTH), f32),
        ),
        in_specs=[vmem, vmem, vmem, vmem, vmem, anywhere, anywhere, anywhere, anywhere],
        out_specs=(vmem, vmem, anywhere, anywhere, anywhere, anywhere, anywhere, vmem),
        scratch_shapes=scratch
        + [
            pltpu.SemaphoreType.DMA((ID_COUNT,)),
            pltpu.SemaphoreType.DMA((ID_COUNT,)),
            pltpu.SemaphoreType.DMA((10,)),
        ],
        compiler_params=pltpu.CompilerParams(
            collective_id=0, has_side_effects=True, vmem_limit_bytes=67043328
        ),
        name="whole_block",
    )(tokens[0], out_grad[0], small, ada_weight, adab, wqkv, proj_weight, wfc1, wfc2)
    grad_qkv = (
        oqkv.reshape(4, 72, 3, 4, 72).transpose(1, 2, 3, 0, 4).reshape(72, 3 * WIDTH).astype(f32)
    )
    grad_fc1 = ofc1.reshape(4, 72, 16, 72).transpose(1, 2, 0, 3).reshape(72, HIDDEN).astype(f32)
    grad_fc2 = ofc2.reshape(288, WIDTH).astype(f32)

    def mine(vector, count):
        return lax.dynamic_slice_in_dim(vector, fsdp_at * count, count, 0)

    by_head = osum[12:16, :QKV].reshape(4, 3, 4, 72).transpose(1, 2, 0, 3).reshape(3 * WIDTH)
    return (
        out[None],
        tgrad[None],
        oada,
        mine(osum[:6].reshape(-1), 432),
        grad_qkv,
        mine(jnp.concatenate([by_head[:WIDTH], by_head[2 * WIDTH :]]), 144),
        oproj.astype(f32),
        mine(osum[7], 72),
        grad_fc1,
        mine(osum[8:12].reshape(4, 16, 72).transpose(1, 0, 2).reshape(-1), 288),
        grad_fc2,
        mine(osum[6], 72),
    )


def solution(mesh):
    in_specs = (
        P(("fsdp", "dp"), None, None),
        P(("fsdp", "dp"), None),
        P(("fsdp", "dp"), None),
        P("fsdp", None),
        P("fsdp"),
        P("fsdp", None),
        P("fsdp"),
        P("fsdp", None),
        P("fsdp"),
        P("fsdp", None),
        P("fsdp"),
        P("fsdp", None),
        P("fsdp"),
        P(("fsdp", "dp"), None, None),
    )
    out_specs = (
        P(("fsdp", "dp"), None, None),
        P(("fsdp", "dp"), None, None),
        P("fsdp", None),
        P("fsdp"),
        P("fsdp", None),
        P("fsdp"),
        P("fsdp", None),
        P("fsdp"),
        P("fsdp", None),
        P("fsdp"),
        P("fsdp", None),
        P("fsdp"),
    )
    fits = (mesh.shape["fsdp"], mesh.shape["dp"]) == (16, 2)
    return jax.shard_map(
        one_kernel if fits else general_form, mesh=mesh, in_specs=in_specs, out_specs=out_specs, check_vma=False
    )
```

```python
import functools

import jax
import jax.numpy as jnp
from jax import lax
from jax.experimental import pallas as pl
from jax.experimental.pallas import tpu as pltpu
from jax.sharding import PartitionSpec as P

HEADS = 16
HEAD_DIM = 72


root_half = 0.7978845608028654
norm_eps = 1e-06
masked_score = -1e30


def gelu_tanh(stream):
    return (
        0.5 * stream * (1.0 + jnp.tanh(root_half * (stream + 0.044715 * stream * stream * stream)))
    )


def gelu_slope(stream):
    tanh_inner = jnp.tanh(root_half * (stream + 0.044715 * stream * stream * stream))
    return 0.5 * (1.0 + tanh_inner) + 0.5 * stream * (1.0 - tanh_inner * tanh_inner) * root_half * (
        1.0 + 3.0 * 0.044715 * stream * stream
    )


def normalize(stream):
    centre = jnp.mean(stream, axis=-1, keepdims=True)
    centred = stream - centre
    inv_std = lax.rsqrt(jnp.mean(centred * centred, axis=-1, keepdims=True) + norm_eps)
    return (centred * inv_std, inv_std)


def normalize_back(incoming, normed, inv_std):
    return inv_std * (
        incoming
        - jnp.mean(incoming, axis=-1, keepdims=True)
        - normed * jnp.mean(incoming * normed, axis=-1, keepdims=True)
    )


def head_scores(projected, same_doc, head_index, model_width):
    query_part = lax.dynamic_slice_in_dim(projected, head_index * HEAD_DIM, HEAD_DIM, 1)
    key_part = lax.dynamic_slice_in_dim(projected, model_width + head_index * HEAD_DIM, HEAD_DIM, 1)
    value_part = lax.dynamic_slice_in_dim(
        projected, 2 * model_width + head_index * HEAD_DIM, HEAD_DIM, 1
    )
    raw_scores = jnp.einsum(
        "qd,kd->qk", query_part, key_part, preferred_element_type=jnp.float32
    ) * HEAD_DIM ** (-0.5)
    return (jnp.where(same_doc, raw_scores, masked_score), query_part, key_part, value_part)


def merge_heads(stacked, model_width):
    return jnp.transpose(stacked, (1, 0, 2)).reshape(stacked.shape[1], model_width)


def attend_row(projected, segments_row, model_width):
    same_doc = segments_row[:, None] == segments_row[None, :]

    def one_head(head_index):
        scores, query_part, key_part, value_part = head_scores(
            projected, same_doc, head_index, model_width
        )
        top_score = jnp.max(scores, axis=-1, keepdims=True)
        exp_scores = jnp.exp(scores - top_score)
        denominator = jnp.sum(exp_scores, axis=-1, keepdims=True)
        probabilities = (exp_scores / denominator).astype(jnp.bfloat16)
        mixed_heads = jnp.dot(probabilities, value_part, preferred_element_type=jnp.float32)
        return (mixed_heads, (top_score + jnp.log(denominator))[:, 0])

    mixed_heads, log_total = lax.map(one_head, jnp.arange(HEADS))
    return (merge_heads(mixed_heads, model_width).astype(jnp.bfloat16), log_total)


def attend_back(projected, segments_row, log_total, d_mixed, model_width):
    same_doc = segments_row[:, None] == segments_row[None, :]
    head_scale = HEAD_DIM ** (-0.5)

    def one_head(head_index):
        scores, query_part, key_part, value_part = head_scores(
            projected, same_doc, head_index, model_width
        )
        d_head = lax.dynamic_slice_in_dim(d_mixed, head_index * HEAD_DIM, HEAD_DIM, 1)
        lse_row = lax.dynamic_index_in_dim(log_total, head_index, 0, keepdims=False)
        probabilities = jnp.exp(scores - lse_row[:, None])
        prob_low = probabilities.astype(jnp.bfloat16)
        d_probs = jnp.einsum("qd,kd->qk", d_head, value_part, preferred_element_type=jnp.float32)
        d_value = jnp.einsum("qk,qd->kd", prob_low, d_head, preferred_element_type=jnp.float32)
        d_scores = (
            probabilities * (d_probs - jnp.sum(d_probs * probabilities, axis=-1, keepdims=True))
        ).astype(jnp.bfloat16)
        d_query = (
            jnp.einsum("qk,kd->qd", d_scores, key_part, preferred_element_type=jnp.float32)
            * head_scale
        )
        d_key = (
            jnp.einsum("qk,qd->kd", d_scores, query_part, preferred_element_type=jnp.float32)
            * head_scale
        )
        return (d_query, d_key, d_value)

    d_query, d_key, d_value = lax.map(one_head, jnp.arange(HEADS))
    merged = [
        merge_heads(d_query, model_width),
        merge_heads(d_key, model_width),
        merge_heads(d_value, model_width),
    ]
    return jnp.concatenate(merged, axis=-1).astype(jnp.bfloat16)


def general_form(
    tokens,
    cond,
    segment_ids,
    ada_weight,
    ada_bias,
    qkv_weight,
    qv_bias,
    proj_weight,
    proj_bias,
    fc1_weight,
    fc1_bias,
    fc2_weight,
    fc2_bias,
    out_grad,
):
    row_count, seq_len, model_width = tokens.shape
    ff_width = fc1_weight.shape[1]
    stream = tokens.astype(jnp.float32)
    cond_float = cond.astype(jnp.float32)
    cond_act = (cond_float / (1.0 + jnp.exp(-cond_float))).astype(jnp.bfloat16)
    fsdp_at, dp_at = lax.axis_index("fsdp"), lax.axis_index("dp")
    dp_size = lax.axis_size("dp")
    slice_width, bias_width = ada_weight.shape[0], ada_bias.shape[0]
    act_all = lax.all_gather(cond_act, ("fsdp", "dp"), axis=0, tiled=True)
    act_mine = lax.dynamic_slice_in_dim(act_all, fsdp_at * slice_width, slice_width, 1)
    partial = jnp.dot(act_mine, ada_weight, preferred_element_type=jnp.float32)
    bias_row = lax.dynamic_update_slice_in_dim(
        jnp.zeros((6 * model_width,), jnp.float32),
        ada_bias.astype(jnp.float32),
        fsdp_at * bias_width,
        0,
    )
    partial = (partial + bias_row).reshape(-1, dp_size, row_count, 6 * model_width)
    partial = lax.dynamic_index_in_dim(partial, dp_at, 1, keepdims=False)
    modulation = lax.psum_scatter(
        partial.reshape(-1, 6 * model_width), "fsdp", scatter_dimension=0, tiled=True
    )
    pieces = [
        modulation[:, None, section * model_width : (section + 1) * model_width]
        for section in range(6)
    ]
    shift_one, scale_one, gate_one, shift_two, scale_two, gate_two = pieces
    qkv_full, qv_bias_full, proj_full, proj_bias_full = (
        lax.all_gather(qkv_weight, "fsdp", axis=0, tiled=True),
        lax.all_gather(qv_bias, "fsdp", axis=0, tiled=True),
        lax.all_gather(proj_weight, "fsdp", axis=0, tiled=True),
        lax.all_gather(proj_bias, "fsdp", axis=0, tiled=True),
    )
    normed_one, inv_one = normalize(stream)
    hidden_one = (normed_one * (1.0 + scale_one) + shift_one).astype(jnp.bfloat16)
    qv_float = qv_bias_full.astype(jnp.float32)
    qkv_bias = jnp.concatenate(
        [qv_float[:model_width], jnp.zeros((model_width,), jnp.float32), qv_float[model_width:]]
    )
    projected = (
        jnp.dot(hidden_one, qkv_full, preferred_element_type=jnp.float32) + qkv_bias
    ).astype(jnp.bfloat16)

    def row_forward(row_items):
        return attend_row(row_items[0], row_items[1], model_width)

    mixed_rows, log_total = lax.map(row_forward, (projected, segment_ids))
    branch_one = jnp.dot(
        mixed_rows, proj_full, preferred_element_type=jnp.float32
    ) + proj_bias_full.astype(jnp.float32)
    resid_one = stream + gate_one * branch_one
    fc1_full, fc1_bias_full, fc2_full, fc2_bias_full = (
        lax.all_gather(fc1_weight, "fsdp", axis=0, tiled=True),
        lax.all_gather(fc1_bias, "fsdp", axis=0, tiled=True),
        lax.all_gather(fc2_weight, "fsdp", axis=0, tiled=True),
        lax.all_gather(fc2_bias, "fsdp", axis=0, tiled=True),
    )
    normed_two, inv_two = normalize(resid_one)
    hidden_two = (normed_two * (1.0 + scale_two) + shift_two).astype(jnp.bfloat16)
    pre_act = jnp.dot(
        hidden_two, fc1_full, preferred_element_type=jnp.float32
    ) + fc1_bias_full.astype(jnp.float32)
    active = gelu_tanh(pre_act).astype(jnp.bfloat16)
    branch_two = jnp.dot(
        active, fc2_full, preferred_element_type=jnp.float32
    ) + fc2_bias_full.astype(jnp.float32)
    output = (resid_one + gate_two * branch_two).astype(jnp.bfloat16)
    d_out = out_grad.astype(jnp.float32)
    fc1_back, fc2_back = (
        lax.all_gather(fc1_weight, "fsdp", axis=0, tiled=True),
        lax.all_gather(fc2_weight, "fsdp", axis=0, tiled=True),
    )
    d_gate_two = jnp.sum(d_out * branch_two, axis=1)
    d_branch_two = (d_out * gate_two).astype(jnp.bfloat16)
    fc2_shard = lax.psum_scatter(
        jnp.einsum("rsf,rsd->fd", active, d_branch_two, preferred_element_type=jnp.float32).astype(
            jnp.bfloat16
        ),
        "fsdp",
        scatter_dimension=0,
        tiled=True,
    )
    grad_fc2_bias = jnp.sum(d_branch_two.astype(jnp.float32), axis=(0, 1))
    d_active = jnp.einsum("rsd,fd->rsf", d_branch_two, fc2_back, preferred_element_type=jnp.float32)
    d_pre = (d_active * gelu_slope(pre_act)).astype(jnp.bfloat16)
    grad_fc1_bias = jnp.sum(d_pre.astype(jnp.float32), axis=(0, 1))
    d_hidden_two = jnp.einsum("rsf,ef->rse", d_pre, fc1_back, preferred_element_type=jnp.float32)
    d_scale_two = jnp.sum(d_hidden_two * normed_two, axis=1)
    d_shift_two = jnp.sum(d_hidden_two, axis=1)
    d_resid = d_out + normalize_back(d_hidden_two * (1.0 + scale_two), normed_two, inv_two)
    qkv_back, proj_back = (
        lax.all_gather(qkv_weight, "fsdp", axis=0, tiled=True),
        lax.all_gather(proj_weight, "fsdp", axis=0, tiled=True),
    )
    d_gate_one = jnp.sum(d_resid * branch_one, axis=1)
    d_branch_one = (d_resid * gate_one).astype(jnp.bfloat16)
    grad_proj_bias = jnp.sum(d_branch_one.astype(jnp.float32), axis=(0, 1))
    d_mixed = jnp.einsum(
        "rsd,ed->rse", d_branch_one, proj_back, preferred_element_type=jnp.float32
    ).astype(jnp.bfloat16)

    def row_backward(row_items):
        return attend_back(row_items[0], row_items[1], row_items[2], row_items[3], model_width)

    d_projected = lax.map(row_backward, (projected, segment_ids, log_total, d_mixed))
    d_proj_float = d_projected.astype(jnp.float32)
    grad_qv_bias = jnp.concatenate(
        [
            jnp.sum(d_proj_float[..., :model_width], axis=(0, 1)),
            jnp.sum(d_proj_float[..., 2 * model_width :], axis=(0, 1)),
        ]
    )
    d_hidden_one = jnp.einsum(
        "rsf,ef->rse", d_projected, qkv_back, preferred_element_type=jnp.float32
    )
    d_scale_one = jnp.sum(d_hidden_one * normed_one, axis=1)
    d_shift_one = jnp.sum(d_hidden_one, axis=1)
    tokens_grad = (
        d_resid + normalize_back(d_hidden_one * (1.0 + scale_one), normed_one, inv_one)
    ).astype(jnp.bfloat16)
    d_modulation = jnp.concatenate(
        [d_shift_one, d_scale_one, d_gate_one, d_shift_two, d_scale_two, d_gate_two], axis=-1
    ).astype(jnp.bfloat16)
    d_mod_all = lax.all_gather(d_modulation, ("fsdp", "dp"), axis=0, tiled=True)
    grad_ada = jnp.einsum("rd,re->de", act_mine, d_mod_all, preferred_element_type=jnp.float32)
    grad_ada_bias = jnp.sum(
        lax.dynamic_slice_in_dim(d_mod_all, fsdp_at * bias_width, bias_width, 1).astype(jnp.float32),
        axis=0,
    )

    def owners(term):
        return lax.psum_scatter(
            term.astype(jnp.bfloat16), "fsdp", scatter_dimension=0, tiled=True
        )

    qkv_shard = owners(
        jnp.einsum("rse,rsf->ef", hidden_one, d_projected, preferred_element_type=jnp.float32)
    )
    proj_shard = owners(
        jnp.einsum("rse,rsd->ed", mixed_rows, d_branch_one, preferred_element_type=jnp.float32)
    )
    fc1_shard = owners(
        jnp.einsum("rse,rsf->ef", hidden_two, d_pre, preferred_element_type=jnp.float32)
    )
    bias_shards = (
        None,
        lax.psum_scatter(
            grad_qv_bias.astype(jnp.bfloat16), "fsdp", scatter_dimension=0, tiled=True
        ).astype(jnp.float32),
        lax.psum_scatter(
            grad_proj_bias.astype(jnp.bfloat16), "fsdp", scatter_dimension=0, tiled=True
        ).astype(jnp.float32),
        lax.psum_scatter(
            grad_fc1_bias.astype(jnp.bfloat16), "fsdp", scatter_dimension=0, tiled=True
        ).astype(jnp.float32),
        lax.psum_scatter(
            grad_fc2_bias.astype(jnp.bfloat16), "fsdp", scatter_dimension=0, tiled=True
        ).astype(jnp.float32),
    )
    summed = (
        grad_ada,
        grad_ada_bias,
        lax.psum(qkv_shard.astype(jnp.bfloat16), "dp").astype(jnp.float32),
        lax.psum(bias_shards[1].astype(jnp.bfloat16), "dp").astype(jnp.float32),
        lax.psum(proj_shard.astype(jnp.bfloat16), "dp").astype(jnp.float32),
        lax.psum(bias_shards[2].astype(jnp.bfloat16), "dp").astype(jnp.float32),
        lax.psum(fc1_shard.astype(jnp.bfloat16), "dp").astype(jnp.float32),
        lax.psum(bias_shards[3].astype(jnp.bfloat16), "dp").astype(jnp.float32),
        lax.psum(fc2_shard, "dp").astype(jnp.float32),
        lax.psum(bias_shards[4].astype(jnp.bfloat16), "dp").astype(jnp.float32),
    )
    return (
        output,
        tokens_grad,
        summed[0],
        summed[1],
        summed[2],
        summed[3],
        summed[4],
        summed[5],
        summed[6],
        summed[7],
        summed[8],
        summed[9],
    )


MESH_ID = pl.DeviceIdType.MESH
f32 = jnp.float32
bf16 = jnp.bfloat16

SEQ = 256
WIDTH = 1152
HIDDEN = 4608
PART = 1152
QKV = 864
PAD = 128
LOCAL = 4


def dot_nn(left, right):
    return lax.dot_general(left, right, (((1,), (0,)), ((), ())), preferred_element_type=f32)


def dot_nt(left, right):
    return lax.dot_general(left, right, (((1,), (1,)), ((), ())), preferred_element_type=f32)


def dot_tn(left, right):
    return lax.dot_general(left, right, (((0,), (0,)), ((), ())), preferred_element_type=f32)


def iota(shape, axis):
    return lax.broadcasted_iota(jnp.int32, shape, axis)


def whole_part(value, divisor):
    return jnp.floor((value + 0.5) * (1.0 / divisor))


class Ids:
    def __init__(self):
        self.used = 0

    def take(self, count):
        start = self.used
        self.used += count
        return start


IDS = Ids()
IDS.small_y, IDS.small_z, IDS.small_c = IDS.take(1), IDS.take(6), IDS.take(1)
IDS.small_x, IDS.small_d = IDS.take(1), IDS.take(1)
IDS.mod_c, IDS.mod_y, IDS.mod_z = IDS.take(1), IDS.take(1), IDS.take(3)
IDS.core = [IDS.take(1) for _ in range(3)]
IDS.z = [IDS.take(3) for _ in range(4)]
IDS.y = [IDS.take(4) for _ in range(4)]
IDS.h1, IDS.h2, IDS.d2, IDS.d1 = IDS.take(3), IDS.take(3), IDS.take(3), IDS.take(3)
IDS.r1, IDS.r2, IDS.r3, IDS.r4 = IDS.take(3), IDS.take(3), IDS.take(3), IDS.take(3)
IDS.gy = [IDS.take(4) for _ in range(4)]
IDS.gz = [IDS.take(3) for _ in range(4)]
IDS.gf = [IDS.take(3) for _ in range(4)]
IDS.end_y, IDS.end_z, IDS.end_x, IDS.end_c = IDS.take(1), IDS.take(6), IDS.take(1), IDS.take(1)
ID_COUNT = IDS.used

SCRATCH = (
    ((32, 8, 384), f32),
    ((16, 8, WIDTH), f32),
    ((8, 8, WIDTH), f32),
    ((4, 8, WIDTH), f32),
    ((3, 8, WIDTH), f32),
    ((8, WIDTH), f32),
    ((72, WIDTH), bf16),
    ((72, QKV), bf16),
    ((72, PART), bf16),
    ((72, WIDTH), bf16),
    ((WIDTH, QKV), bf16),
    ((WIDTH, PART), bf16),
    ((PART, WIDTH), bf16),
    ((4, 72, WIDTH), bf16),
    ((288, WIDTH), bf16),
    ((1024, WIDTH), bf16),
    ((1024, WIDTH), bf16),
    ((1024, WIDTH), bf16),
    ((1024, 12 * PAD), bf16),
    ((16, SEQ, SEQ), bf16),
    ((1024, 288), bf16),
    ((1024, PART), bf16),
    ((1024, PART), bf16),
    ((1024, QKV), bf16),
    ((3, SEQ, WIDTH), bf16),
    ((3, SEQ, WIDTH), bf16),
    ((SEQ, WIDTH), bf16),
    ((SEQ, WIDTH), bf16),
    ((SEQ, WIDTH), bf16),
    ((SEQ, WIDTH), f32),
    ((SEQ, WIDTH), f32),
    ((SEQ, WIDTH), f32),
    ((SEQ, WIDTH), f32),
    ((16, WIDTH), f32),
    ((8, WIDTH), f32),
    ((WIDTH, QKV), bf16),
    ((WIDTH, PART), bf16),
    ((PART, WIDTH), bf16),
    ((4, 72, WIDTH), bf16),
    ((4, 144, QKV), bf16),
    ((4, 144, PART), bf16),
    ((4, 144, WIDTH), bf16),
    ((4, 72, WIDTH), bf16),
    ((3, 144, QKV), bf16),
    ((3, 144, PART), bf16),
    ((3, 144, WIDTH), bf16),
    ((3, 72, WIDTH), bf16),
    ((72, QKV), bf16),
    ((72, PART), bf16),
    ((72, WIDTH), bf16),
    ((72, QKV), bf16),
    ((72, PART), bf16),
    ((72, WIDTH), bf16),
    ((4, 72, QKV), bf16),
    ((4, 72, PART), bf16),
    ((4, 72, WIDTH), bf16),
    ((72, WIDTH), bf16),
    ((32, 16, WIDTH), bf16),
)


def block_kernel(
    tok, og, small, ada, adab, wqkv, wproj, wfc1, wfc2, out,
    tgrad, oada, oqkv, oproj, ofc1, ofc2, osum, S, modp, modc,
    mody, modz, mod, own_fc2, xr_qkv, xr_fc1, xr_fc2, G_qkv,
    G_fc1, G_fc2, G_proj, W_proj, H1, H2, D2, qp, P, mixed,
    active, slope, dprj, rrA, rrB, sA, sB, sX, keep, own,
    b1, resid, acc, bias, g_qkv, g_fc1, g_fc2, g_proj, yr_qkv, yr_fc1,
    yr_fc2, yr_proj, zr_qkv, zr_fc1, zr_fc2, zr_proj, fa_qkv, fa_fc1, fa_fc2, fb_qkv,
    fb_fc1, fb_fc2, fr_qkv, fr_fc1, fr_fc2, p_out, E, snd, rcv, loc,
):
    xr_w, G_w = (xr_qkv, xr_fc1, xr_fc2), (G_qkv, G_fc1, G_fc2)
    yr_w, zr_w = (yr_qkv, yr_fc1, yr_fc2), (zr_qkv, zr_fc1, zr_fc2)
    fa_w, fb_w, fr_w = (fa_qkv, fa_fc1, fa_fc2), (fb_qkv, fb_fc1, fb_fc2), (fr_qkv, fr_fc1, fr_fc2)
    f = lax.axis_index("fsdp")
    x = lax.axis_index("dp")
    z = lax.div(f, 4)
    y = lax.rem(lax.div(f, 2), 2)
    c = lax.rem(f, 2)
    q = 2 * x + c
    qp_, qx_, qd_ = 2 * x + 1 - c, 2 * (1 - x) + c, 2 * (1 - x) + 1 - c

    def dev(zz, yy, cc, xx):
        return ((zz * 2 + yy) * 2 + cc, xx)

    mate, xnb, diag, ynb = dev(z, y, 1 - c, x), dev(z, y, c, 1 - x), dev(z, y, 1 - c, 1 - x), dev(z, 1 - y, c, x)

    def z_to(k):
        return lax.rem(z + k, 4)

    def z_from(k):
        return lax.rem(z + 4 - k, 4)

    def znb(k):
        return dev(z_to(k), y, c, x)

    def rc(src, dst, ident, to):
        return pltpu.make_async_remote_copy(
            src_ref=src, dst_ref=dst, send_sem=snd.at[ident], recv_sem=rcv.at[ident],
            device_id=to, device_id_type=MESH_ID,
        )

    pending = []

    def send(src, dst, ident, to):
        rc(src, dst, ident, to).start()
        pending.append((src, ident, to))

    def got(dst, ident):
        rc(dst, dst, ident, mate).wait_recv()

    def sent(src, ident):
        rc(src, src, ident, mate).wait_send()

    def settle(first):
        keep_on = []
        for item in pending:
            if item[1] in first:
                sent(item[0], item[1])
            else:
                keep_on.append(item)
        pending[:] = keep_on

    barrier = pltpu.get_barrier_semaphore()
    neighbours = [mate, xnb, diag, ynb, znb(1), znb(2), znb(3)]
    for to in neighbours:
        pl.semaphore_signal(barrier, inc=1, device_id=to, device_id_type=MESH_ID)
    pl.semaphore_wait(barrier, len(neighbours))


    def slot_of(cc, xx, yy, zz):
        return ((cc * 2 + xx) * 2 + yy) * 4 + zz

    my_slot = slot_of(c, x, y, z)
    send(small, S.at[my_slot], IDS.small_y, ynb)
    own_copy = pltpu.make_async_copy(wfc2.at[q], own_fc2, loc.at[0])
    own_copy.start()
    send(wfc2.at[qp_], xr_fc2, IDS.core[2], mate)

    def split_qkv():
        for at in range(4):
            fr_qkv[at] = jnp.concatenate(
                [wqkv[:, (4 * step + at) * 72 : (4 * step + at + 1) * 72] for step in range(12)], axis=1
            )
        send(fr_qkv.at[qp_], xr_qkv, IDS.core[0], mate)

    def split_fc1():
        for at in range(4):
            fr_fc1[at] = jnp.concatenate(
                [wfc1[:, (4 * step + at) * 72 : (4 * step + at + 1) * 72] for step in range(16)], axis=1
            )
        send(fr_fc1.at[qp_], xr_fc1, IDS.core[1], mate)

    split_qkv()
    S[my_slot] = small[...]
    acc[...] = jnp.zeros((16, WIDTH), f32)
    in_column = y == x
    proj_copy = pltpu.make_async_copy(wproj, G_proj.at[z], loc.at[1])

    def chip_rows(zz, yy):
        return pl.ds(pl.multiple_of((2 * zz + yy) * 144, 16), 144)

    def own_part(kind):
        return G_w[kind].at[chip_rows(z, y), :]

    def assemble(kind):
        got(xr_w[kind], IDS.core[kind])
        mine = (own_fc2[...] if kind == 2 else fr_w[kind][q]).astype(f32)
        other = xr_w[kind][...].astype(f32)
        low = jnp.where(c == 0, mine, other)
        high = jnp.where(c == 0, other, mine)
        G_w[kind][chip_rows(z, y), :] = jnp.concatenate([low, high], axis=0).astype(bf16)

    def own_y(kind):
        send(own_part(kind), own_part(kind), IDS.y[kind], ynb)

    def own_z(kind, steps):
        for k in steps:
            send(own_part(kind), own_part(kind), IDS.z[kind] + k - 1, znb(k))

    STEPS = (1, 3, 2)

    def forward(kind, k):
        part = G_w[kind].at[chip_rows(z_from(k), y), :]
        got(part, IDS.z[kind] + k - 1)
        send(part, part, IDS.y[kind] + k, ynb)

    def arrived(kind):
        other = 1 - y
        got(G_w[kind].at[chip_rows(z, other), :], IDS.y[kind])
        for k in STEPS:
            got(G_w[kind].at[chip_rows(z_from(k), other), :], IDS.y[kind] + k)

    def proj_z():
        @pl.when(in_column)
        def _():
            proj_copy.start()
            for k in STEPS:
                rc(wproj, G_proj.at[z], IDS.z[3] + k - 1, znb(k)).start()

    def proj_y():
        @pl.when(in_column)
        def _():
            rc(wproj, G_proj.at[z], IDS.y[3], ynb).start()

    def proj_forward(k):
        @pl.when(in_column)
        def _():
            part = G_proj.at[z_from(k)]
            got(part, IDS.z[3] + k - 1)
            rc(part, part, IDS.y[3] + k, ynb).start()

    def proj_arrived():
        @pl.when(in_column)
        def _():
            proj_copy.wait()
            for k in (1, 2, 3):
                sent(wproj, IDS.z[3] + k - 1)
            sent(wproj, IDS.y[3])
            for k in STEPS:
                sent(G_proj.at[z_from(k)], IDS.y[3] + k)

        @pl.when(jnp.logical_not(in_column))
        def _():
            got(G_proj.at[z], IDS.y[3])
            for k in STEPS:
                got(G_proj.at[z_from(k)], IDS.y[3] + k)

        W_proj[...] = jnp.concatenate(
            [G_proj[head].astype(f32) for head in range(LOCAL)], axis=0
        ).astype(bf16)

    got(S.at[slot_of(c, x, 1 - y, z)], IDS.small_y)
    for k in (2, 1, 3):
        for yy in range(2):
            part = S.at[slot_of(c, x, yy, z)]
            send(part, part, IDS.small_z + 2 * (k - 1) + yy, znb(k))
    assemble(0)
    own_y(0)
    own_z(0, (1, 3))
    for k in (1, 2, 3):
        for yy in range(2):
            got(S.at[slot_of(c, x, yy, z_from(k))], IDS.small_z + 2 * (k - 1) + yy)
    eight = lambda cc, xx: S.at[pl.ds((cc * 2 + xx) * 8, 8)]
    send(eight(c, x), eight(c, x), IDS.small_c, mate)
    send(eight(c, x), eight(c, x), IDS.small_x, xnb)
    split_fc1()

    def pick_columns(rows):
        total = None
        for piece in range(3):
            kk = iota((384, PAD), 0) + piece * 384
            jj = iota((384, PAD), 1)
            chosen = ((kk == 72 * f + jj) & (jj < 72)).astype(f32).astype(bf16)
            term = dot_nn(rows(piece), chosen)
            total = term if total is None else total + term
        return total.astype(bf16)

    got(eight(1 - c, x), IDS.small_c)
    act = pick_columns(
        lambda piece: jnp.concatenate(
            [S[pl.ds((cc * 2 + x) * 8, 8), piece, :] for cc in range(2)], axis=0
        ).astype(bf16)
    )[:, :72]
    for section in range(6):
        modp[:, section, :] = dot_nn(
            act, ada[:, section * WIDTH : (section + 1) * WIDTH]
        ) + adab[section : section + 1, :]
    for section in (6, 7):
        modp[:, section, :] = jnp.zeros((16, WIDTH), f32)
    theirs, ours = modp.at[pl.ds((1 - c) * 8, 8)], modp.at[pl.ds(c * 8, 8)]
    send(theirs, modc, IDS.mod_c, mate)
    own_copy.wait()
    assemble(1)
    assemble(2)
    got(modc, IDS.mod_c)
    for at in range(8):
        ours[at] += modc[at]
    send(modp.at[pl.ds(c * 8 + (1 - y) * 4, 4)], mody, IDS.mod_y, ynb)
    forward(0, 1)
    got(mody, IDS.mod_y)
    base = c * 8 + y * 4
    for at in range(4):
        modp[base + at] += mody[at]
    for k in (2, 1, 3):
        send(modp.at[base + z_to(k)], modz.at[k - 1], IDS.mod_z + k - 1, znb(k))
    own_z(0, (2,))
    proj_z()
    own_z(1, STEPS)
    own_z(2, STEPS)
    proj_y()
    own_y(1)
    got(eight(c, 1 - x), IDS.small_x)
    send(eight(c, 1 - x), eight(c, 1 - x), IDS.small_d, mate)

    def place(row, width, lane_of, owner_of):
        kk = iota((384, width), 1).astype(f32)
        jj = iota((384, width), 0).astype(f32)
        chosen = (jj == lane_of(kk)).astype(f32).astype(bf16)
        spread = dot_nn(row.astype(bf16), chosen)
        at = iota((16, width), 0)
        slot_f = ((lax.rem(at, 4) * 2 + lax.rem(lax.div(at, 4), 2)) * 2 + lax.div(at, 8)).astype(f32)
        mine = slot_f == owner_of(iota((16, width), 1).astype(f32))
        return jnp.sum(jnp.where(mine, spread, 0.0), axis=0, keepdims=True)

    def plane(piece):
        return jnp.concatenate([S[pl.ds((cc * 2 + x) * 8, 8), piece, :] for cc in range(2)], axis=0)

    def mod72(kk):
        return kk - 72.0 * whole_part(kk, 72)

    by72 = lambda kk: whole_part(kk, 72)
    qf, xf, cf = q.astype(f32), x.astype(f32), c.astype(f32)
    row3, row4 = plane(3), plane(4)
    bias[0:1, :] = place(row3, WIDTH, lambda kk: 144.0 + mod72(kk), by72)
    bias[1:2, :] = place(row3, WIDTH, lambda kk: 216.0 + mod72(kk), by72)
    bias[2:3, :] = place(row4, WIDTH, lambda kk: 72.0 * qf + mod72(kk), by72)

    def qkv_owner(kk):
        third = whole_part(kk, 288)
        head = whole_part(kk - 288.0 * third, 72)
        owner = 2.0 * head + xf + 4.0 * third
        return jnp.where((third == 1.0) | (third > 2.5), -1.0, owner)

    bias[3:4, :] = place(row3, WIDTH, lambda kk: 72.0 * cf + mod72(kk), qkv_owner)

    for k in (1, 2, 3):
        got(modz.at[k - 1], IDS.mod_z + k - 1)
    mod[...] = modp[base + z] + modz[0] + modz[1] + modz[2]

    def row_of(section):
        return mod[section : section + 1, :]

    def slot_rows(slot):
        return pl.ds(pl.multiple_of(slot * SEQ, SEQ), SEQ)

    TILE = 64

    def tiles(body):
        def step(at, carry):
            body(pl.multiple_of(at * TILE, TILE))
            return carry

        lax.fori_loop(0, SEQ // TILE, step, 0)


    def norm_one(at):
        normed, _ = normalize(tok[pl.ds(at, TILE), :].astype(f32))
        H1[pl.ds(pl.multiple_of(q * SEQ + at, TILE), TILE), :] = (
            normed * (1.0 + row_of(1)) + row_of(0)
        ).astype(bf16)

    tiles(norm_one)

    def spread_start(buf, ident):
        part = buf.at[slot_rows(q), :]
        send(part, part, ident, mate)
        send(part, part, ident + 1, xnb)

    def spread_mid(buf, ident):
        part = buf.at[slot_rows(qx_), :]
        got(part, ident + 1)
        send(part, part, ident + 2, mate)

    def spread_mate(buf, ident):
        got(buf.at[slot_rows(qp_), :], ident)

    def spread_end(buf, ident):
        got(buf.at[slot_rows(qd_), :], ident + 2)

    spread_start(H1, IDS.h1)
    settle(tuple(IDS.core))

    def add_row(at, value):
        acc[at : at + 1, :] += jnp.sum(value, axis=0, keepdims=True)

    def out_gate(at):
        low = (og[pl.ds(at, TILE), :].astype(f32) * row_of(5)).astype(bf16)
        D2[pl.ds(pl.multiple_of(q * SEQ + at, TILE), TILE), :] = low
        add_row(6, low.astype(f32))

    tiles(out_gate)
    spread_start(D2, IDS.d2)
    spread_mate(H1, IDS.h1)
    forward(0, 3)
    forward(0, 2)
    spread_mid(H1, IDS.h1)
    arrived(0)


    def project(slot):
        rows = slot_rows(slot)
        value = (dot_nn(H1[rows, :], G_qkv[...]) + bias[3:4, :QKV]).astype(bf16)
        blank = jnp.zeros((SEQ, PAD - HEAD_DIM), bf16)
        for at in range(12):
            qp[rows, at * PAD : (at + 1) * PAD] = jnp.concatenate(
                [value[:, at * HEAD_DIM : (at + 1) * HEAD_DIM], blank], axis=1
            )

    def attend(slot):
        rows = slot_rows(slot)
        where_seg = slot_of(lax.rem(slot, 2), lax.div(slot, 2), y, z)
        seg = S[where_seg, 5:6, :SEQ]
        seg_column = jnp.transpose(jnp.broadcast_to(seg, (8, SEQ)))[:, :1]
        same = seg_column == seg
        pieces = []
        for head in range(LOCAL):
            query = qp[rows, head * PAD : (head + 1) * PAD]
            key = qp[rows, (LOCAL + head) * PAD : (LOCAL + head + 1) * PAD]
            value = qp[rows, (2 * LOCAL + head) * PAD : (2 * LOCAL + head + 1) * PAD]
            scores = jnp.where(same, dot_nt(query, key) * HEAD_DIM ** (-0.5), masked_score)
            exp_scores = jnp.exp(scores - jnp.max(scores, axis=1, keepdims=True))
            probs = (exp_scores / jnp.sum(exp_scores, axis=1, keepdims=True)).astype(bf16)
            P[slot * LOCAL + head] = probs
            pieces.append(dot_nn(probs, value).astype(bf16)[:, :HEAD_DIM])
        mixed[rows, :] = jnp.concatenate(pieces, axis=1)

    def pair(body, group):
        def step(at, carry):
            body(2 * group + lax.rem(c + at, 2))
            return carry

        lax.fori_loop(0, 2, step, 0)

    got(eight(1 - c, 1 - x), IDS.small_d)
    pair(project, x)
    pair(attend, x)
    proj_forward(1)
    spread_end(H1, IDS.h1)
    pair(project, 1 - x)
    proj_forward(3)
    pair(attend, 1 - x)
    proj_forward(2)
    forward(1, 1)
    spread_mate(D2, IDS.d2)
    spread_mid(D2, IDS.d2)


    def reduce_first(partial, rr, ident):
        sA[...] = partial(qd_).astype(bf16)
        send(sA, rr.at[0], ident, mate)
        keep[...] = partial(qx_)
        sB[...] = partial(qp_).astype(bf16)

    def reduce_next(partial, rr, ident):
        got(rr.at[0], ident)
        sX[...] = (keep[...] + rr[0].astype(f32)).astype(bf16)
        send(sX, rr.at[2], ident + 2, xnb)
        send(sB, rr.at[1], ident + 1, mate)
        own[...] = partial(q)

    def reduce_last(rr, ident):
        got(rr.at[1], ident + 1)
        got(rr.at[2], ident + 2)
        settle((ident, ident + 1, ident + 2))

    def total_rows(rr, at):
        rows = pl.ds(at, TILE)
        return own[rows, :] + rr[1, rows, :].astype(f32) + rr[2, rows, :].astype(f32)

    proj_arrived()

    def part_one(slot):
        return dot_nn(mixed[slot_rows(slot), :], W_proj[...])

    reduce_first(part_one, rrA, IDS.r1)
    reduce_next(part_one, rrA, IDS.r1)
    forward(1, 3)
    own_y(2)
    reduce_last(rrA, IDS.r1)


    def norm_two(at):
        rows = pl.ds(at, TILE)
        branch = total_rows(rrA, at) + bias[0:1, :]
        b1[rows, :] = branch
        stream = tok[rows, :].astype(f32) + row_of(2) * branch
        resid[rows, :] = stream
        normed, _ = normalize(stream)
        H2[pl.ds(pl.multiple_of(q * SEQ + at, TILE), TILE), :] = (
            normed * (1.0 + row_of(4)) + row_of(3)
        ).astype(bf16)

    tiles(norm_two)
    spread_start(H2, IDS.h2)
    forward(1, 2)
    spread_end(D2, IDS.d2)
    spread_mate(H2, IDS.h2)
    spread_mid(H2, IDS.h2)
    arrived(1)

    CHUNK = 384

    def first_layer(slot):
        rows = slot_rows(slot)
        for at in range(0, PART, CHUNK):
            pre = dot_nn(H2[rows, :], G_fc1[:, at : at + CHUNK]) + bias[2:3, at : at + CHUNK]
            square = pre * pre
            bend = jnp.tanh(root_half * (pre + 0.044715 * square * pre))
            active[rows, at : at + CHUNK] = (0.5 * pre * (1.0 + bend)).astype(bf16)
            slope[rows, at : at + CHUNK] = (
                0.5 * (1.0 + bend)
                + 0.5 * pre * (1.0 - bend * bend) * root_half * (1.0 + 3.0 * 0.044715 * square)
            ).astype(bf16)

    pair(first_layer, x)
    forward(2, 1)
    spread_end(H2, IDS.h2)
    pair(first_layer, 1 - x)
    forward(2, 3)

    def cross(left, right, dest, width):
        def step(at, carry):
            part = pl.ds(pl.multiple_of(at * CHUNK, CHUNK), CHUNK)
            dest[part, :] = dot_tn(left[:, part], right[...]).astype(bf16)
            return carry

        lax.fori_loop(0, width // CHUNK, step, 0)

    cross(active, D2, g_fc2, PART)

    def grad_start(kind, grads, steps):
        for k in steps:
            send(
                grads.at[chip_rows(z_to(k), 1 - y), :], yr_w[kind].at[k], IDS.gy[kind] + k, ynb
            )

    def add_block(grads, rows_at, extra):
        def step(at, carry):
            rows = pl.ds(pl.multiple_of(rows_at + at * 48, 16), 48)
            grads[rows, :] = (
                grads[rows, :].astype(f32) + extra[pl.ds(pl.multiple_of(at * 48, 16), 48), :].astype(f32)
            ).astype(bf16)
            return carry

        lax.fori_loop(0, 3, step, 0)

    def grad_mid(kind, grads, k):
        zz = z_to(k)
        got(yr_w[kind].at[k], IDS.gy[kind] + k)
        add_block(grads, (2 * zz + y) * 144, yr_w[kind].at[k])
        send(
            grads.at[chip_rows(zz, y), :], zr_w[kind].at[k - 1], IDS.gz[kind] + k - 1, znb(k)
        )

    def grad_end(kind, grads):
        got(yr_w[kind].at[0], IDS.gy[kind])
        for k in (1, 2, 3):
            got(zr_w[kind].at[k - 1], IDS.gz[kind] + k - 1)
        width = grads.shape[1]
        A, B, fr = fa_w[kind], fb_w[kind], fr_w[kind]
        for at in range(0, width, CHUNK):
            cols = slice(at, min(at + CHUNK, width))
            total = grads[chip_rows(z, y), cols].astype(f32) + yr_w[kind][0, :, cols].astype(f32)
            for k in range(3):
                total = total + zr_w[kind][k, :, cols].astype(f32)
            low, high = total[:72], total[72:]
            mine = jnp.where(c == 0, low, high).astype(bf16)
            A[:, cols] = mine
            B[:, cols] = jnp.where(c == 0, high, low).astype(bf16)
            fr[q, :, cols] = mine
        send(B, fr.at[q], IDS.gf[kind], mate)
        send(A, fr.at[q], IDS.gf[kind] + 1, xnb)
        send(B, fr.at[q], IDS.gf[kind] + 2, diag)

    slots = [area.at[72 * at : 72 * (at + 1), :] for area in (resid, b1, keep, own) for at in range(3)]
    out_copies = []

    def leave(value, target):
        at = len(out_copies)
        if at >= len(slots):
            out_copies[at - len(slots)].wait()
        slots[at % len(slots)][...] = value
        copy = pltpu.make_async_copy(slots[at % len(slots)], target, loc.at[2 + at])
        copy.start()
        out_copies.append(copy)

    def columns_of(ref, piece):
        return ref.at[:, piece * WIDTH : (piece + 1) * WIDTH]

    def grad_out(kind):
        fr = fr_w[kind]
        for step, source in enumerate((qp_, qx_, qd_)):
            got(fr.at[source], IDS.gf[kind] + step)
        if kind == 2:
            for at in range(4):
                leave(fr[at].astype(f32), ofc2.at[at])
            return
        for piece in range(3 if kind == 0 else 4):
            leave(
                jnp.concatenate(
                    [
                        fr[at, :, (4 * piece + step) * 72 : (4 * piece + step + 1) * 72]
                        for step in range(4)
                        for at in range(4)
                    ],
                    axis=1,
                ).astype(f32),
                columns_of(oqkv if kind == 0 else ofc1, piece),
            )

    grad_start(2, g_fc2, (1,))
    forward(2, 2)
    grad_start(2, g_fc2, (3, 2, 0))
    arrived(2)

    def back_hidden(slot):
        rows = slot_rows(slot)
        for at in range(0, PART, CHUNK):
            low = (
                dot_nt(D2[rows, :], G_fc2[at : at + CHUNK, :])
                * slope[rows, at : at + CHUNK].astype(f32)
            ).astype(bf16)
            slope[rows, at : at + CHUNK] = low
            acc[8:9, at : at + CHUNK] += jnp.sum(low.astype(f32), axis=0, keepdims=True)

    pair(back_hidden, x)
    pair(back_hidden, 1 - x)
    d_pre = slope
    settle(tuple(IDS.d2 + step for step in range(3)))
    D1 = D2
    def part_three(slot):
        return dot_nt(d_pre[slot_rows(slot), :], G_fc1[...])

    reduce_first(part_three, rrA, IDS.r3)
    reduce_next(part_three, rrA, IDS.r3)
    cross(H2, d_pre, g_fc1, WIDTH)
    grad_start(1, g_fc1, (1, 3, 2, 0))
    grad_mid(2, g_fc2, 1)
    reduce_last(rrA, IDS.r3)

    def back_two(at):
        rows = pl.ds(at, TILE)
        d_hidden = total_rows(rrA, at)
        normed, inv = normalize(resid[rows, :])
        add_row(3, d_hidden)
        add_row(4, d_hidden * normed)
        d_resid = og[rows, :].astype(f32) + normalize_back(d_hidden * (1.0 + row_of(4)), normed, inv)
        add_row(2, d_resid * b1[rows, :])
        low = (d_resid * row_of(2)).astype(bf16)
        add_row(7, low.astype(f32))
        D1[pl.ds(pl.multiple_of(q * SEQ + at, TILE), TILE), :] = low
        b1[rows, :] = d_resid

    tiles(back_two)
    spread_start(D1, IDS.d1)

    def part_two(slot):
        return dot_nn(active[slot_rows(slot), :], G_fc2[...])

    reduce_first(part_two, rrB, IDS.r2)
    reduce_next(part_two, rrB, IDS.r2)

    def finish_forward(at):
        rows = pl.ds(at, TILE)
        branch = total_rows(rrB, at) + bias[1:2, :]
        rrB[0, rows, :] = (resid[rows, :] + row_of(5) * branch).astype(bf16)
        add_row(5, og[rows, :].astype(f32) * branch)

    grad_mid(2, g_fc2, 3)
    spread_mate(D1, IDS.d1)


    def attend_backward(slot):
        rows = slot_rows(slot)
        d_mix = dot_nt(D1[rows, :], W_proj[...]).astype(bf16)
        blank = jnp.zeros((SEQ, PAD - HEAD_DIM), bf16)
        scale = HEAD_DIM ** (-0.5)
        d_query, d_key, d_value = [], [], []
        for head in range(LOCAL):
            query = qp[rows, head * PAD : (head + 1) * PAD]
            key = qp[rows, (LOCAL + head) * PAD : (LOCAL + head + 1) * PAD]
            value = qp[rows, (2 * LOCAL + head) * PAD : (2 * LOCAL + head + 1) * PAD]
            d_head = jnp.concatenate([d_mix[:, head * HEAD_DIM : (head + 1) * HEAD_DIM], blank], axis=1)
            probs = P[slot * LOCAL + head]
            d_probs = dot_nt(d_head, value)
            d_value.append(dot_tn(probs, d_head).astype(bf16)[:, :HEAD_DIM])
            wide = probs.astype(f32)
            d_scores = (wide * (d_probs - jnp.sum(d_probs * wide, axis=1, keepdims=True))).astype(bf16)
            d_query.append((dot_nn(d_scores, key) * scale).astype(bf16)[:, :HEAD_DIM])
            d_key.append((dot_tn(d_scores, query) * scale).astype(bf16)[:, :HEAD_DIM])
        value = jnp.concatenate(d_query + d_key + d_value, axis=1)
        dprj[rows, :] = value
        acc[9:10, :QKV] += jnp.sum(value.astype(f32), axis=0, keepdims=True)

    pair(attend_backward, x)
    spread_mid(D1, IDS.d1)
    grad_mid(2, g_fc2, 2)
    spread_end(D1, IDS.d1)
    pair(attend_backward, 1 - x)
    cross(H1, dprj, g_qkv, WIDTH)
    grad_start(0, g_qkv, (1, 3, 2, 0))
    grad_mid(1, g_fc1, 1)
    proj_grads = dot_tn(mixed[...], D1[...])
    for head in range(LOCAL):
        g_proj[head] = proj_grads[head * 72 : (head + 1) * 72].astype(bf16)

    @pl.when(jnp.logical_not(in_column))
    def _():
        for k in range(4):
            rc(g_proj.at[z_to(k)], yr_proj.at[k], IDS.gy[3] + k, ynb).start()

    def part_four(slot):
        return dot_nt(dprj[slot_rows(slot), :], G_qkv[...])

    settle((IDS.r2, IDS.r2 + 1))
    reduce_first(part_four, rrA, IDS.r4)
    reduce_last(rrB, IDS.r2)
    tiles(finish_forward)
    row_copies = [pltpu.make_async_copy(rrB.at[0], out, loc.at[20])]
    row_copies[0].start()
    reduce_next(part_four, rrA, IDS.r4)
    grad_mid(1, g_fc1, 3)
    grad_mid(1, g_fc1, 2)
    grad_end(2, g_fc2)
    reduce_last(rrA, IDS.r4)

    def back_one(at):
        rows = pl.ds(at, TILE)
        d_hidden = total_rows(rrA, at)
        normed, inv = normalize(tok[rows, :].astype(f32))
        add_row(0, d_hidden)
        add_row(1, d_hidden * normed)
        sA[rows, :] = (
            b1[rows, :] + normalize_back(d_hidden * (1.0 + row_of(1)), normed, inv)
        ).astype(bf16)

    tiles(back_one)
    row_copies.append(pltpu.make_async_copy(sA, tgrad, loc.at[21]))
    row_copies[1].start()

    E[my_slot] = acc[...].astype(bf16)
    send(E.at[my_slot], E.at[my_slot], IDS.end_y, ynb)

    @pl.when(in_column)
    def _():
        for k in STEPS:
            zz = z_to(k)
            got(yr_proj.at[k], IDS.gy[3] + k)
            g_proj[zz] = (g_proj[zz].astype(f32) + yr_proj[k].astype(f32)).astype(bf16)
            rc(g_proj.at[zz], zr_proj.at[k - 1], IDS.gz[3] + k - 1, znb(k)).start()

    got(E.at[slot_of(c, x, 1 - y, z)], IDS.end_y)
    for k in (2, 1, 3):
        for yy in range(2):
            part = E.at[slot_of(c, x, yy, z)]
            send(part, part, IDS.end_z + 2 * (k - 1) + yy, znb(k))
    for k in STEPS:
        grad_mid(0, g_qkv, k)
    for k in (1, 2, 3):
        for yy in range(2):
            got(E.at[slot_of(c, x, yy, z_from(k))], IDS.end_z + 2 * (k - 1) + yy)
    group = lambda cc, xx: E.at[pl.ds((cc * 2 + xx) * 8, 8)]
    send(group(c, x), group(c, x), IDS.end_x, xnb)
    grad_end(1, g_fc1)

    @pl.when(in_column)
    def _():
        got(yr_proj.at[0], IDS.gy[3])
        total = g_proj[z].astype(f32) + yr_proj[0].astype(f32)
        for k in (1, 2, 3):
            got(zr_proj.at[k - 1], IDS.gz[3] + k - 1)
            total = total + zr_proj[k - 1].astype(f32)
        p_out[...] = total.astype(bf16)
        rc(p_out, p_out, IDS.gf[3], xnb).start()

    got(group(c, 1 - x), IDS.end_x)
    send(E.at[pl.ds(c * 16, 16)], E.at[pl.ds(c * 16, 16)], IDS.end_c, mate)
    grad_out(2)

    @pl.when(jnp.logical_not(in_column))
    def _():
        got(p_out, IDS.gf[3])

    leave(p_out[...].astype(f32), oproj)
    got(E.at[pl.ds((1 - c) * 16, 16)], IDS.end_c)

    act_all = pick_columns(lambda piece: S[:, piece, :].astype(bf16))[:, :72]
    for section in range(6):
        rows = E[:, section, :]
        leave(dot_tn(act_all, rows), columns_of(oada, section))
        osum[section : section + 1, :] = jnp.sum(rows.astype(f32), axis=0, keepdims=True)
    for section in (6, 7):
        osum[section : section + 1, :] = jnp.sum(E[:, section, :].astype(f32), axis=0, keepdims=True)
    for section in (8, 9):
        for quarter in range(4):
            start = ((quarter % 2) * 2 + quarter // 2) * 8
            at = 8 + 4 * (section - 8) + quarter
            osum[at : at + 1, :] = jnp.sum(
                E[start : start + 8, section, :].astype(f32), axis=0, keepdims=True
            )
    grad_out(1)
    grad_end(0, g_qkv)
    grad_out(0)
    for copy in out_copies[-len(slots) :]:
        copy.wait()
    for copy in row_copies:
        copy.wait()
    for src, ident, _ in pending:
        sent(src, ident)

    @pl.when(in_column)
    def _():
        for k in (1, 2, 3):
            sent(p_out, IDS.gz[3] + k - 1)
        sent(p_out, IDS.gf[3])

    @pl.when(jnp.logical_not(in_column))
    def _():
        for k in range(4):
            sent(p_out, IDS.gy[3] + k)


def one_kernel(
    tokens,
    cond,
    segment_ids,
    ada_weight,
    ada_bias,
    qkv_weight,
    qv_bias,
    proj_weight,
    proj_bias,
    fc1_weight,
    fc1_bias,
    fc2_weight,
    fc2_bias,
    out_grad,
):
    fsdp_at = lax.axis_index("fsdp")
    cond_float = cond[0].astype(f32)
    cond_act = (cond_float / (1.0 + jnp.exp(-cond_float))).astype(bf16).astype(f32)
    blank = lambda count: jnp.zeros((count,), f32)
    small = jnp.concatenate(
        [
            cond_act,
            qv_bias.astype(f32),
            proj_bias.astype(f32),
            fc2_bias.astype(f32),
            blank(96),
            fc1_bias.astype(f32),
            blank(96),
            segment_ids[0].astype(f32),
            blank(128 + 768),
        ]
    ).reshape(8, 384)
    adab = lax.dynamic_update_slice_in_dim(
        blank(8 * WIDTH), ada_bias.astype(f32), fsdp_at * 432, 0
    ).reshape(8, WIDTH)
    wfc2 = fc2_weight.reshape(4, 72, WIDTH)
    vmem = pl.BlockSpec(memory_space=pltpu.VMEM)
    anywhere = pl.BlockSpec(memory_space=pl.ANY)
    outside = pl.BlockSpec(memory_space=pltpu.HBM)
    shape = jax.ShapeDtypeStruct
    scratch = [pltpu.VMEM(dims, kind) for dims, kind in SCRATCH]
    out, tgrad, oada, oqkv, oproj, ofc1, ofc2, osum = pl.pallas_call(
        block_kernel,
        out_shape=(
            shape((SEQ, WIDTH), bf16),
            shape((SEQ, WIDTH), bf16),
            shape((72, 6 * WIDTH), f32),
            shape((72, 3 * WIDTH), f32),
            shape((72, WIDTH), f32),
            shape((72, HIDDEN), f32),
            shape((4, 72, WIDTH), f32),
            shape((16, WIDTH), f32),
        ),
        in_specs=[vmem, vmem, vmem, vmem, vmem, vmem, anywhere, vmem, anywhere],
        out_specs=(outside,) * 7 + (vmem,),
        scratch_shapes=scratch
        + [
            pltpu.SemaphoreType.DMA((ID_COUNT,)),
            pltpu.SemaphoreType.DMA((ID_COUNT,)),
            pltpu.SemaphoreType.DMA((22,)),
        ],
        compiler_params=pltpu.CompilerParams(
            collective_id=0, has_side_effects=True, vmem_limit_bytes=67043328
        ),
        name="whole_block",
    )(tokens[0], out_grad[0], small, ada_weight, adab, qkv_weight, proj_weight, fc1_weight, wfc2)
    def mine(vector, count):
        return lax.dynamic_slice_in_dim(vector, fsdp_at * count, count, 0)

    by_head = osum[12:16, :QKV].reshape(4, 3, 4, 72).transpose(1, 2, 0, 3).reshape(3 * WIDTH)
    return (
        out[None],
        tgrad[None],
        oada,
        mine(osum[:6].reshape(-1), 432),
        oqkv,
        mine(jnp.concatenate([by_head[:WIDTH], by_head[2 * WIDTH :]]), 144),
        oproj,
        mine(osum[7], 72),
        ofc1,
        mine(osum[8:12].reshape(4, 16, 72).transpose(1, 0, 2).reshape(-1), 288),
        ofc2.reshape(288, WIDTH),
        mine(osum[6], 72),
    )


def solution(mesh):
    in_specs = (
        P(("fsdp", "dp"), None, None),
        P(("fsdp", "dp"), None),
        P(("fsdp", "dp"), None),
        P("fsdp", None),
        P("fsdp"),
        P("fsdp", None),
        P("fsdp"),
        P("fsdp", None),
        P("fsdp"),
        P("fsdp", None),
        P("fsdp"),
        P("fsdp", None),
        P("fsdp"),
        P(("fsdp", "dp"), None, None),
    )
    out_specs = (
        P(("fsdp", "dp"), None, None),
        P(("fsdp", "dp"), None, None),
        P("fsdp", None),
        P("fsdp"),
        P("fsdp", None),
        P("fsdp"),
        P("fsdp", None),
        P("fsdp"),
        P("fsdp", None),
        P("fsdp"),
        P("fsdp", None),
        P("fsdp"),
    )
    fits = (mesh.shape["fsdp"], mesh.shape["dp"]) == (16, 2)
    return jax.shard_map(
        one_kernel if fits else general_form, mesh=mesh, in_specs=in_specs, out_specs=out_specs, check_vma=False
    )
```

```python
import functools

import jax
import jax.numpy as jnp
from jax import lax
from jax.experimental import pallas as pl
from jax.experimental.pallas import tpu as pltpu
from jax.sharding import PartitionSpec as P

HEADS = 16
HEAD_DIM = 72


root_half = 0.7978845608028654
norm_eps = 1e-06
masked_score = -1e30


def gelu_tanh(stream):
    return (
        0.5 * stream * (1.0 + jnp.tanh(root_half * (stream + 0.044715 * stream * stream * stream)))
    )


def gelu_slope(stream):
    tanh_inner = jnp.tanh(root_half * (stream + 0.044715 * stream * stream * stream))
    return 0.5 * (1.0 + tanh_inner) + 0.5 * stream * (1.0 - tanh_inner * tanh_inner) * root_half * (
        1.0 + 3.0 * 0.044715 * stream * stream
    )


def normalize(stream):
    centre = jnp.mean(stream, axis=-1, keepdims=True)
    centred = stream - centre
    inv_std = lax.rsqrt(jnp.mean(centred * centred, axis=-1, keepdims=True) + norm_eps)
    return (centred * inv_std, inv_std)


def normalize_back(incoming, normed, inv_std):
    return inv_std * (
        incoming
        - jnp.mean(incoming, axis=-1, keepdims=True)
        - normed * jnp.mean(incoming * normed, axis=-1, keepdims=True)
    )


def head_scores(projected, same_doc, head_index, model_width):
    query_part = lax.dynamic_slice_in_dim(projected, head_index * HEAD_DIM, HEAD_DIM, 1)
    key_part = lax.dynamic_slice_in_dim(projected, model_width + head_index * HEAD_DIM, HEAD_DIM, 1)
    value_part = lax.dynamic_slice_in_dim(
        projected, 2 * model_width + head_index * HEAD_DIM, HEAD_DIM, 1
    )
    raw_scores = jnp.einsum(
        "qd,kd->qk", query_part, key_part, preferred_element_type=jnp.float32
    ) * HEAD_DIM ** (-0.5)
    return (jnp.where(same_doc, raw_scores, masked_score), query_part, key_part, value_part)


def merge_heads(stacked, model_width):
    return jnp.transpose(stacked, (1, 0, 2)).reshape(stacked.shape[1], model_width)


def attend_row(projected, segments_row, model_width):
    same_doc = segments_row[:, None] == segments_row[None, :]

    def one_head(head_index):
        scores, query_part, key_part, value_part = head_scores(
            projected, same_doc, head_index, model_width
        )
        top_score = jnp.max(scores, axis=-1, keepdims=True)
        exp_scores = jnp.exp(scores - top_score)
        denominator = jnp.sum(exp_scores, axis=-1, keepdims=True)
        probabilities = (exp_scores / denominator).astype(jnp.bfloat16)
        mixed_heads = jnp.dot(probabilities, value_part, preferred_element_type=jnp.float32)
        return (mixed_heads, (top_score + jnp.log(denominator))[:, 0])

    mixed_heads, log_total = lax.map(one_head, jnp.arange(HEADS))
    return (merge_heads(mixed_heads, model_width).astype(jnp.bfloat16), log_total)


def attend_back(projected, segments_row, log_total, d_mixed, model_width):
    same_doc = segments_row[:, None] == segments_row[None, :]
    head_scale = HEAD_DIM ** (-0.5)

    def one_head(head_index):
        scores, query_part, key_part, value_part = head_scores(
            projected, same_doc, head_index, model_width
        )
        d_head = lax.dynamic_slice_in_dim(d_mixed, head_index * HEAD_DIM, HEAD_DIM, 1)
        lse_row = lax.dynamic_index_in_dim(log_total, head_index, 0, keepdims=False)
        probabilities = jnp.exp(scores - lse_row[:, None])
        prob_low = probabilities.astype(jnp.bfloat16)
        d_probs = jnp.einsum("qd,kd->qk", d_head, value_part, preferred_element_type=jnp.float32)
        d_value = jnp.einsum("qk,qd->kd", prob_low, d_head, preferred_element_type=jnp.float32)
        d_scores = (
            probabilities * (d_probs - jnp.sum(d_probs * probabilities, axis=-1, keepdims=True))
        ).astype(jnp.bfloat16)
        d_query = (
            jnp.einsum("qk,kd->qd", d_scores, key_part, preferred_element_type=jnp.float32)
            * head_scale
        )
        d_key = (
            jnp.einsum("qk,qd->kd", d_scores, query_part, preferred_element_type=jnp.float32)
            * head_scale
        )
        return (d_query, d_key, d_value)

    d_query, d_key, d_value = lax.map(one_head, jnp.arange(HEADS))
    merged = [
        merge_heads(d_query, model_width),
        merge_heads(d_key, model_width),
        merge_heads(d_value, model_width),
    ]
    return jnp.concatenate(merged, axis=-1).astype(jnp.bfloat16)


def general_form(
    tokens,
    cond,
    segment_ids,
    ada_weight,
    ada_bias,
    qkv_weight,
    qv_bias,
    proj_weight,
    proj_bias,
    fc1_weight,
    fc1_bias,
    fc2_weight,
    fc2_bias,
    out_grad,
):
    row_count, seq_len, model_width = tokens.shape
    ff_width = fc1_weight.shape[1]
    stream = tokens.astype(jnp.float32)
    cond_float = cond.astype(jnp.float32)
    cond_act = (cond_float / (1.0 + jnp.exp(-cond_float))).astype(jnp.bfloat16)
    fsdp_at, dp_at = lax.axis_index("fsdp"), lax.axis_index("dp")
    dp_size = lax.axis_size("dp")
    slice_width, bias_width = ada_weight.shape[0], ada_bias.shape[0]
    act_all = lax.all_gather(cond_act, ("fsdp", "dp"), axis=0, tiled=True)
    act_mine = lax.dynamic_slice_in_dim(act_all, fsdp_at * slice_width, slice_width, 1)
    partial = jnp.dot(act_mine, ada_weight, preferred_element_type=jnp.float32)
    bias_row = lax.dynamic_update_slice_in_dim(
        jnp.zeros((6 * model_width,), jnp.float32),
        ada_bias.astype(jnp.float32),
        fsdp_at * bias_width,
        0,
    )
    partial = (partial + bias_row).reshape(-1, dp_size, row_count, 6 * model_width)
    partial = lax.dynamic_index_in_dim(partial, dp_at, 1, keepdims=False)
    modulation = lax.psum_scatter(
        partial.reshape(-1, 6 * model_width), "fsdp", scatter_dimension=0, tiled=True
    )
    pieces = [
        modulation[:, None, section * model_width : (section + 1) * model_width]
        for section in range(6)
    ]
    shift_one, scale_one, gate_one, shift_two, scale_two, gate_two = pieces
    qkv_full, qv_bias_full, proj_full, proj_bias_full = (
        lax.all_gather(qkv_weight, "fsdp", axis=0, tiled=True),
        lax.all_gather(qv_bias, "fsdp", axis=0, tiled=True),
        lax.all_gather(proj_weight, "fsdp", axis=0, tiled=True),
        lax.all_gather(proj_bias, "fsdp", axis=0, tiled=True),
    )
    normed_one, inv_one = normalize(stream)
    hidden_one = (normed_one * (1.0 + scale_one) + shift_one).astype(jnp.bfloat16)
    qv_float = qv_bias_full.astype(jnp.float32)
    qkv_bias = jnp.concatenate(
        [qv_float[:model_width], jnp.zeros((model_width,), jnp.float32), qv_float[model_width:]]
    )
    projected = (
        jnp.dot(hidden_one, qkv_full, preferred_element_type=jnp.float32) + qkv_bias
    ).astype(jnp.bfloat16)

    def row_forward(row_items):
        return attend_row(row_items[0], row_items[1], model_width)

    mixed_rows, log_total = lax.map(row_forward, (projected, segment_ids))
    branch_one = jnp.dot(
        mixed_rows, proj_full, preferred_element_type=jnp.float32
    ) + proj_bias_full.astype(jnp.float32)
    resid_one = stream + gate_one * branch_one
    fc1_full, fc1_bias_full, fc2_full, fc2_bias_full = (
        lax.all_gather(fc1_weight, "fsdp", axis=0, tiled=True),
        lax.all_gather(fc1_bias, "fsdp", axis=0, tiled=True),
        lax.all_gather(fc2_weight, "fsdp", axis=0, tiled=True),
        lax.all_gather(fc2_bias, "fsdp", axis=0, tiled=True),
    )
    normed_two, inv_two = normalize(resid_one)
    hidden_two = (normed_two * (1.0 + scale_two) + shift_two).astype(jnp.bfloat16)
    pre_act = jnp.dot(
        hidden_two, fc1_full, preferred_element_type=jnp.float32
    ) + fc1_bias_full.astype(jnp.float32)
    active = gelu_tanh(pre_act).astype(jnp.bfloat16)
    branch_two = jnp.dot(
        active, fc2_full, preferred_element_type=jnp.float32
    ) + fc2_bias_full.astype(jnp.float32)
    output = (resid_one + gate_two * branch_two).astype(jnp.bfloat16)
    d_out = out_grad.astype(jnp.float32)
    fc1_back, fc2_back = (
        lax.all_gather(fc1_weight, "fsdp", axis=0, tiled=True),
        lax.all_gather(fc2_weight, "fsdp", axis=0, tiled=True),
    )
    d_gate_two = jnp.sum(d_out * branch_two, axis=1)
    d_branch_two = (d_out * gate_two).astype(jnp.bfloat16)
    fc2_shard = lax.psum_scatter(
        jnp.einsum("rsf,rsd->fd", active, d_branch_two, preferred_element_type=jnp.float32).astype(
            jnp.bfloat16
        ),
        "fsdp",
        scatter_dimension=0,
        tiled=True,
    )
    grad_fc2_bias = jnp.sum(d_branch_two.astype(jnp.float32), axis=(0, 1))
    d_active = jnp.einsum("rsd,fd->rsf", d_branch_two, fc2_back, preferred_element_type=jnp.float32)
    d_pre = (d_active * gelu_slope(pre_act)).astype(jnp.bfloat16)
    grad_fc1_bias = jnp.sum(d_pre.astype(jnp.float32), axis=(0, 1))
    d_hidden_two = jnp.einsum("rsf,ef->rse", d_pre, fc1_back, preferred_element_type=jnp.float32)
    d_scale_two = jnp.sum(d_hidden_two * normed_two, axis=1)
    d_shift_two = jnp.sum(d_hidden_two, axis=1)
    d_resid = d_out + normalize_back(d_hidden_two * (1.0 + scale_two), normed_two, inv_two)
    qkv_back, proj_back = (
        lax.all_gather(qkv_weight, "fsdp", axis=0, tiled=True),
        lax.all_gather(proj_weight, "fsdp", axis=0, tiled=True),
    )
    d_gate_one = jnp.sum(d_resid * branch_one, axis=1)
    d_branch_one = (d_resid * gate_one).astype(jnp.bfloat16)
    grad_proj_bias = jnp.sum(d_branch_one.astype(jnp.float32), axis=(0, 1))
    d_mixed = jnp.einsum(
        "rsd,ed->rse", d_branch_one, proj_back, preferred_element_type=jnp.float32
    ).astype(jnp.bfloat16)

    def row_backward(row_items):
        return attend_back(row_items[0], row_items[1], row_items[2], row_items[3], model_width)

    d_projected = lax.map(row_backward, (projected, segment_ids, log_total, d_mixed))
    d_proj_float = d_projected.astype(jnp.float32)
    grad_qv_bias = jnp.concatenate(
        [
            jnp.sum(d_proj_float[..., :model_width], axis=(0, 1)),
            jnp.sum(d_proj_float[..., 2 * model_width :], axis=(0, 1)),
        ]
    )
    d_hidden_one = jnp.einsum(
        "rsf,ef->rse", d_projected, qkv_back, preferred_element_type=jnp.float32
    )
    d_scale_one = jnp.sum(d_hidden_one * normed_one, axis=1)
    d_shift_one = jnp.sum(d_hidden_one, axis=1)
    tokens_grad = (
        d_resid + normalize_back(d_hidden_one * (1.0 + scale_one), normed_one, inv_one)
    ).astype(jnp.bfloat16)
    d_modulation = jnp.concatenate(
        [d_shift_one, d_scale_one, d_gate_one, d_shift_two, d_scale_two, d_gate_two], axis=-1
    ).astype(jnp.bfloat16)
    d_mod_all = lax.all_gather(d_modulation, ("fsdp", "dp"), axis=0, tiled=True)
    grad_ada = jnp.einsum("rd,re->de", act_mine, d_mod_all, preferred_element_type=jnp.float32)
    grad_ada_bias = jnp.sum(
        lax.dynamic_slice_in_dim(d_mod_all, fsdp_at * bias_width, bias_width, 1).astype(jnp.float32),
        axis=0,
    )

    def owners(term):
        return lax.psum_scatter(
            term.astype(jnp.bfloat16), "fsdp", scatter_dimension=0, tiled=True
        )

    qkv_shard = owners(
        jnp.einsum("rse,rsf->ef", hidden_one, d_projected, preferred_element_type=jnp.float32)
    )
    proj_shard = owners(
        jnp.einsum("rse,rsd->ed", mixed_rows, d_branch_one, preferred_element_type=jnp.float32)
    )
    fc1_shard = owners(
        jnp.einsum("rse,rsf->ef", hidden_two, d_pre, preferred_element_type=jnp.float32)
    )
    bias_shards = (
        None,
        lax.psum_scatter(
            grad_qv_bias.astype(jnp.bfloat16), "fsdp", scatter_dimension=0, tiled=True
        ).astype(jnp.float32),
        lax.psum_scatter(
            grad_proj_bias.astype(jnp.bfloat16), "fsdp", scatter_dimension=0, tiled=True
        ).astype(jnp.float32),
        lax.psum_scatter(
            grad_fc1_bias.astype(jnp.bfloat16), "fsdp", scatter_dimension=0, tiled=True
        ).astype(jnp.float32),
        lax.psum_scatter(
            grad_fc2_bias.astype(jnp.bfloat16), "fsdp", scatter_dimension=0, tiled=True
        ).astype(jnp.float32),
    )
    summed = (
        grad_ada,
        grad_ada_bias,
        lax.psum(qkv_shard.astype(jnp.bfloat16), "dp").astype(jnp.float32),
        lax.psum(bias_shards[1].astype(jnp.bfloat16), "dp").astype(jnp.float32),
        lax.psum(proj_shard.astype(jnp.bfloat16), "dp").astype(jnp.float32),
        lax.psum(bias_shards[2].astype(jnp.bfloat16), "dp").astype(jnp.float32),
        lax.psum(fc1_shard.astype(jnp.bfloat16), "dp").astype(jnp.float32),
        lax.psum(bias_shards[3].astype(jnp.bfloat16), "dp").astype(jnp.float32),
        lax.psum(fc2_shard, "dp").astype(jnp.float32),
        lax.psum(bias_shards[4].astype(jnp.bfloat16), "dp").astype(jnp.float32),
    )
    return (
        output,
        tokens_grad,
        summed[0],
        summed[1],
        summed[2],
        summed[3],
        summed[4],
        summed[5],
        summed[6],
        summed[7],
        summed[8],
        summed[9],
    )


MESH_ID = pl.DeviceIdType.MESH
f32 = jnp.float32
bf16 = jnp.bfloat16

SEQ = 256
WIDTH = 1152
HIDDEN = 4608
PART = 1152
QKV = 864
PAD = 128
LOCAL = 4


def dot_nn(left, right):
    return lax.dot_general(left, right, (((1,), (0,)), ((), ())), preferred_element_type=f32)


def dot_nt(left, right):
    return lax.dot_general(left, right, (((1,), (1,)), ((), ())), preferred_element_type=f32)


def dot_tn(left, right):
    return lax.dot_general(left, right, (((0,), (0,)), ((), ())), preferred_element_type=f32)


def iota(shape, axis):
    return lax.broadcasted_iota(jnp.int32, shape, axis)


def whole_part(value, divisor):
    return jnp.floor((value + 0.5) * (1.0 / divisor))


class Ids:
    def __init__(self):
        self.used = 0

    def take(self, count):
        start = self.used
        self.used += count
        return start


IDS = Ids()
IDS.small_y, IDS.small_z, IDS.small_c = IDS.take(1), IDS.take(6), IDS.take(1)
IDS.small_x, IDS.small_d = IDS.take(1), IDS.take(1)
IDS.mod_c, IDS.mod_y, IDS.mod_z = IDS.take(1), IDS.take(1), IDS.take(3)
IDS.core = [IDS.take(1) for _ in range(3)]
IDS.z = [IDS.take(3) for _ in range(4)]
IDS.y = [IDS.take(4) for _ in range(4)]
IDS.h1, IDS.h2, IDS.d2, IDS.d1 = IDS.take(3), IDS.take(3), IDS.take(3), IDS.take(3)
IDS.r1, IDS.r2, IDS.r3, IDS.r4 = IDS.take(3), IDS.take(3), IDS.take(3), IDS.take(3)
IDS.gy = [IDS.take(4) for _ in range(4)]
IDS.gz = [IDS.take(3) for _ in range(4)]
IDS.gf = [IDS.take(3) for _ in range(4)]
IDS.end_y, IDS.end_z, IDS.end_x, IDS.end_c = IDS.take(1), IDS.take(6), IDS.take(1), IDS.take(1)
ID_COUNT = IDS.used

SCRATCH = (
    ((32, 8, 384), f32),
    ((16, 8, WIDTH), f32),
    ((8, 8, WIDTH), f32),
    ((4, 8, WIDTH), f32),
    ((3, 8, WIDTH), f32),
    ((8, WIDTH), f32),
    ((72, WIDTH), bf16),
    ((72, QKV), bf16),
    ((72, PART), bf16),
    ((72, WIDTH), bf16),
    ((WIDTH, QKV), bf16),
    ((WIDTH, PART), bf16),
    ((PART, WIDTH), bf16),
    ((4, 72, WIDTH), bf16),
    ((288, WIDTH), bf16),
    ((1024, WIDTH), bf16),
    ((1024, WIDTH), bf16),
    ((1024, WIDTH), bf16),
    ((1024, 12 * PAD), bf16),
    ((16, SEQ, SEQ), bf16),
    ((1024, 288), bf16),
    ((1024, PART), bf16),
    ((1024, PART), bf16),
    ((1024, QKV), bf16),
    ((3, SEQ, WIDTH), bf16),
    ((3, SEQ, WIDTH), bf16),
    ((SEQ, WIDTH), bf16),
    ((SEQ, WIDTH), bf16),
    ((SEQ, WIDTH), bf16),
    ((SEQ, WIDTH), f32),
    ((SEQ, WIDTH), f32),
    ((SEQ, WIDTH), f32),
    ((SEQ, WIDTH), f32),
    ((16, WIDTH), f32),
    ((8, WIDTH), f32),
    ((WIDTH, QKV), bf16),
    ((WIDTH, PART), bf16),
    ((PART, WIDTH), bf16),
    ((4, 72, WIDTH), bf16),
    ((4, 144, QKV), bf16),
    ((4, 144, PART), bf16),
    ((4, 144, WIDTH), bf16),
    ((4, 72, WIDTH), bf16),
    ((3, 144, QKV), bf16),
    ((3, 144, PART), bf16),
    ((3, 144, WIDTH), bf16),
    ((3, 72, WIDTH), bf16),
    ((72, QKV), bf16),
    ((72, PART), bf16),
    ((72, WIDTH), bf16),
    ((72, QKV), bf16),
    ((72, PART), bf16),
    ((72, WIDTH), bf16),
    ((4, 72, QKV), bf16),
    ((4, 72, PART), bf16),
    ((4, 72, WIDTH), bf16),
    ((72, WIDTH), bf16),
    ((32, 16, WIDTH), bf16),
)


def block_kernel(
    tok, og, small, ada, adab, wqkv, wproj, wfc1, wfc2, out,
    tgrad, oada, oqkv, oproj, ofc1, ofc2, osum, S, modp, modc,
    mody, modz, mod, own_fc2, xr_qkv, xr_fc1, xr_fc2, G_qkv,
    G_fc1, G_fc2, G_proj, W_proj, H1, H2, D2, qp, P, mixed,
    active, slope, dprj, rrA, rrB, sA, sB, sX, keep, own,
    b1, resid, acc, bias, g_qkv, g_fc1, g_fc2, g_proj, yr_qkv, yr_fc1,
    yr_fc2, yr_proj, zr_qkv, zr_fc1, zr_fc2, zr_proj, fa_qkv, fa_fc1, fa_fc2, fb_qkv,
    fb_fc1, fb_fc2, fr_qkv, fr_fc1, fr_fc2, p_out, E, snd, rcv, loc,
):
    xr_w, G_w = (xr_qkv, xr_fc1, xr_fc2), (G_qkv, G_fc1, G_fc2)
    yr_w, zr_w = (yr_qkv, yr_fc1, yr_fc2), (zr_qkv, zr_fc1, zr_fc2)
    fa_w, fb_w, fr_w = (fa_qkv, fa_fc1, fa_fc2), (fb_qkv, fb_fc1, fb_fc2), (fr_qkv, fr_fc1, fr_fc2)
    f = lax.axis_index("fsdp")
    x = lax.axis_index("dp")
    z = lax.div(f, 4)
    y = lax.rem(lax.div(f, 2), 2)
    c = lax.rem(f, 2)
    q = 2 * x + c
    qp_, qx_, qd_ = 2 * x + 1 - c, 2 * (1 - x) + c, 2 * (1 - x) + 1 - c

    def dev(zz, yy, cc, xx):
        return ((zz * 2 + yy) * 2 + cc, xx)

    mate, xnb, diag, ynb = dev(z, y, 1 - c, x), dev(z, y, c, 1 - x), dev(z, y, 1 - c, 1 - x), dev(z, 1 - y, c, x)

    def z_to(k):
        return lax.rem(z + k, 4)

    def z_from(k):
        return lax.rem(z + 4 - k, 4)

    def znb(k):
        return dev(z_to(k), y, c, x)

    def rc(src, dst, ident, to):
        return pltpu.make_async_remote_copy(
            src_ref=src, dst_ref=dst, send_sem=snd.at[ident], recv_sem=rcv.at[ident],
            device_id=to, device_id_type=MESH_ID,
        )

    pending = []

    def send(src, dst, ident, to):
        rc(src, dst, ident, to).start()
        pending.append((src, ident, to))

    def got(dst, ident):
        rc(dst, dst, ident, mate).wait_recv()

    def sent(src, ident):
        rc(src, src, ident, mate).wait_send()

    def settle(first):
        keep_on = []
        for item in pending:
            if item[1] in first:
                sent(item[0], item[1])
            else:
                keep_on.append(item)
        pending[:] = keep_on

    barrier = pltpu.get_barrier_semaphore()
    neighbours = [mate, xnb, diag, ynb, znb(1), znb(2), znb(3)]
    for to in neighbours:
        pl.semaphore_signal(barrier, inc=1, device_id=to, device_id_type=MESH_ID)
    pl.semaphore_wait(barrier, len(neighbours))


    def slot_of(cc, xx, yy, zz):
        return ((cc * 2 + xx) * 2 + yy) * 4 + zz

    my_slot = slot_of(c, x, y, z)
    send(small, S.at[my_slot], IDS.small_y, ynb)
    own_copy = pltpu.make_async_copy(wfc2.at[q], own_fc2, loc.at[0])
    own_copy.start()
    send(wfc2.at[qp_], xr_fc2, IDS.core[2], mate)

    def split_qkv():
        for at in range(4):
            fr_qkv[at] = jnp.concatenate(
                [wqkv[:, (4 * step + at) * 72 : (4 * step + at + 1) * 72] for step in range(12)], axis=1
            )
        send(fr_qkv.at[qp_], xr_qkv, IDS.core[0], mate)

    def split_fc1():
        for at in range(4):
            fr_fc1[at] = jnp.concatenate(
                [wfc1[:, (4 * step + at) * 72 : (4 * step + at + 1) * 72] for step in range(16)], axis=1
            )
        send(fr_fc1.at[qp_], xr_fc1, IDS.core[1], mate)

    split_qkv()
    S[my_slot] = small[...]
    acc[...] = jnp.zeros((16, WIDTH), f32)
    in_column = y == x
    proj_copy = pltpu.make_async_copy(wproj, G_proj.at[z], loc.at[1])

    def chip_rows(zz, yy):
        return pl.ds(pl.multiple_of((2 * zz + yy) * 144, 16), 144)

    def own_part(kind):
        return G_w[kind].at[chip_rows(z, y), :]

    def assemble(kind):
        got(xr_w[kind], IDS.core[kind])
        mine = (own_fc2[...] if kind == 2 else fr_w[kind][q]).astype(f32)
        other = xr_w[kind][...].astype(f32)
        low = jnp.where(c == 0, mine, other)
        high = jnp.where(c == 0, other, mine)
        G_w[kind][chip_rows(z, y), :] = jnp.concatenate([low, high], axis=0).astype(bf16)

    def own_y(kind):
        send(own_part(kind), own_part(kind), IDS.y[kind], ynb)

    def own_z(kind, steps):
        for k in steps:
            send(own_part(kind), own_part(kind), IDS.z[kind] + k - 1, znb(k))

    STEPS = (1, 3, 2)

    def forward(kind, k):
        part = G_w[kind].at[chip_rows(z_from(k), y), :]
        got(part, IDS.z[kind] + k - 1)
        send(part, part, IDS.y[kind] + k, ynb)

    def arrived(kind):
        other = 1 - y
        got(G_w[kind].at[chip_rows(z, other), :], IDS.y[kind])
        for k in STEPS:
            got(G_w[kind].at[chip_rows(z_from(k), other), :], IDS.y[kind] + k)

    def proj_z():
        @pl.when(in_column)
        def _():
            proj_copy.start()
            for k in STEPS:
                rc(wproj, G_proj.at[z], IDS.z[3] + k - 1, znb(k)).start()

    def proj_y():
        @pl.when(in_column)
        def _():
            rc(wproj, G_proj.at[z], IDS.y[3], ynb).start()

    def proj_forward(k):
        @pl.when(in_column)
        def _():
            part = G_proj.at[z_from(k)]
            got(part, IDS.z[3] + k - 1)
            rc(part, part, IDS.y[3] + k, ynb).start()

    def proj_arrived():
        @pl.when(in_column)
        def _():
            proj_copy.wait()
            for k in (1, 2, 3):
                sent(wproj, IDS.z[3] + k - 1)
            sent(wproj, IDS.y[3])
            for k in STEPS:
                sent(G_proj.at[z_from(k)], IDS.y[3] + k)

        @pl.when(jnp.logical_not(in_column))
        def _():
            got(G_proj.at[z], IDS.y[3])
            for k in STEPS:
                got(G_proj.at[z_from(k)], IDS.y[3] + k)

        W_proj[...] = jnp.concatenate(
            [G_proj[head].astype(f32) for head in range(LOCAL)], axis=0
        ).astype(bf16)

    got(S.at[slot_of(c, x, 1 - y, z)], IDS.small_y)
    for k in (2, 1, 3):
        for yy in range(2):
            part = S.at[slot_of(c, x, yy, z)]
            send(part, part, IDS.small_z + 2 * (k - 1) + yy, znb(k))
    assemble(0)
    own_y(0)
    own_z(0, (1, 3))
    for k in (1, 2, 3):
        for yy in range(2):
            got(S.at[slot_of(c, x, yy, z_from(k))], IDS.small_z + 2 * (k - 1) + yy)
    eight = lambda cc, xx: S.at[pl.ds((cc * 2 + xx) * 8, 8)]
    send(eight(c, x), eight(c, x), IDS.small_c, mate)
    send(eight(c, x), eight(c, x), IDS.small_x, xnb)

    def pick_columns(rows):
        total = None
        for piece in range(3):
            kk = iota((384, PAD), 0) + piece * 384
            jj = iota((384, PAD), 1)
            chosen = ((kk == 72 * f + jj) & (jj < 72)).astype(f32).astype(bf16)
            term = dot_nn(rows(piece), chosen)
            total = term if total is None else total + term
        return total.astype(bf16)

    got(eight(1 - c, x), IDS.small_c)
    own_z(0, (2,))
    act = pick_columns(
        lambda piece: jnp.concatenate(
            [S[pl.ds((cc * 2 + x) * 8, 8), piece, :] for cc in range(2)], axis=0
        ).astype(bf16)
    )[:, :72]
    for section in range(6):
        modp[:, section, :] = dot_nn(
            act, ada[:, section * WIDTH : (section + 1) * WIDTH]
        ) + adab[section : section + 1, :]
    for section in (6, 7):
        modp[:, section, :] = jnp.zeros((16, WIDTH), f32)
    theirs, ours = modp.at[pl.ds((1 - c) * 8, 8)], modp.at[pl.ds(c * 8, 8)]
    send(theirs, modc, IDS.mod_c, mate)
    split_fc1()
    got(modc, IDS.mod_c)
    for at in range(8):
        ours[at] += modc[at]
    send(modp.at[pl.ds(c * 8 + (1 - y) * 4, 4)], mody, IDS.mod_y, ynb)
    forward(0, 1)
    own_copy.wait()
    assemble(1)
    got(mody, IDS.mod_y)
    base = c * 8 + y * 4
    for at in range(4):
        modp[base + at] += mody[at]
    for k in (2, 1, 3):
        send(modp.at[base + z_to(k)], modz.at[k - 1], IDS.mod_z + k - 1, znb(k))
    proj_z()
    own_z(1, STEPS)
    assemble(2)
    own_z(2, STEPS)
    proj_y()
    own_y(1)
    got(eight(c, 1 - x), IDS.small_x)
    send(eight(c, 1 - x), eight(c, 1 - x), IDS.small_d, mate)

    def place(row, width, lane_of, owner_of):
        kk = iota((384, width), 1).astype(f32)
        jj = iota((384, width), 0).astype(f32)
        chosen = (jj == lane_of(kk)).astype(f32).astype(bf16)
        spread = dot_nn(row.astype(bf16), chosen)
        at = iota((16, width), 0)
        slot_f = ((lax.rem(at, 4) * 2 + lax.rem(lax.div(at, 4), 2)) * 2 + lax.div(at, 8)).astype(f32)
        mine = slot_f == owner_of(iota((16, width), 1).astype(f32))
        return jnp.sum(jnp.where(mine, spread, 0.0), axis=0, keepdims=True)

    def plane(piece):
        return jnp.concatenate([S[pl.ds((cc * 2 + x) * 8, 8), piece, :] for cc in range(2)], axis=0)

    def mod72(kk):
        return kk - 72.0 * whole_part(kk, 72)

    by72 = lambda kk: whole_part(kk, 72)
    qf, xf, cf = q.astype(f32), x.astype(f32), c.astype(f32)
    row3, row4 = plane(3), plane(4)
    bias[0:1, :] = place(row3, WIDTH, lambda kk: 144.0 + mod72(kk), by72)
    bias[1:2, :] = place(row3, WIDTH, lambda kk: 216.0 + mod72(kk), by72)
    bias[2:3, :] = place(row4, WIDTH, lambda kk: 72.0 * qf + mod72(kk), by72)

    def qkv_owner(kk):
        third = whole_part(kk, 288)
        head = whole_part(kk - 288.0 * third, 72)
        owner = 2.0 * head + xf + 4.0 * third
        return jnp.where((third == 1.0) | (third > 2.5), -1.0, owner)

    bias[3:4, :] = place(row3, WIDTH, lambda kk: 72.0 * cf + mod72(kk), qkv_owner)

    for k in (1, 2, 3):
        got(modz.at[k - 1], IDS.mod_z + k - 1)
    mod[...] = modp[base + z] + modz[0] + modz[1] + modz[2]

    def row_of(section):
        return mod[section : section + 1, :]

    def slot_rows(slot):
        return pl.ds(pl.multiple_of(slot * SEQ, SEQ), SEQ)

    TILE = 64

    def tiles(body):
        def step(at, carry):
            body(pl.multiple_of(at * TILE, TILE))
            return carry

        lax.fori_loop(0, SEQ // TILE, step, 0)


    def norm_one(at):
        normed, _ = normalize(tok[pl.ds(at, TILE), :].astype(f32))
        H1[pl.ds(pl.multiple_of(q * SEQ + at, TILE), TILE), :] = (
            normed * (1.0 + row_of(1)) + row_of(0)
        ).astype(bf16)

    tiles(norm_one)

    def spread_start(buf, ident):
        part = buf.at[slot_rows(q), :]
        send(part, part, ident, mate)
        send(part, part, ident + 1, xnb)

    def spread_mid(buf, ident):
        part = buf.at[slot_rows(qx_), :]
        got(part, ident + 1)
        send(part, part, ident + 2, mate)

    def spread_mate(buf, ident):
        got(buf.at[slot_rows(qp_), :], ident)

    def spread_end(buf, ident):
        got(buf.at[slot_rows(qd_), :], ident + 2)

    spread_start(H1, IDS.h1)
    settle(tuple(IDS.core))

    def add_row(at, value):
        acc[at : at + 1, :] += jnp.sum(value, axis=0, keepdims=True)

    def out_gate(at):
        low = (og[pl.ds(at, TILE), :].astype(f32) * row_of(5)).astype(bf16)
        D2[pl.ds(pl.multiple_of(q * SEQ + at, TILE), TILE), :] = low
        add_row(6, low.astype(f32))

    tiles(out_gate)
    spread_start(D2, IDS.d2)
    spread_mate(H1, IDS.h1)
    forward(0, 3)
    forward(0, 2)
    spread_mid(H1, IDS.h1)
    arrived(0)


    def project(slot):
        rows = slot_rows(slot)
        value = (dot_nn(H1[rows, :], G_qkv[...]) + bias[3:4, :QKV]).astype(bf16)
        blank = jnp.zeros((SEQ, PAD - HEAD_DIM), bf16)
        for at in range(12):
            qp[rows, at * PAD : (at + 1) * PAD] = jnp.concatenate(
                [value[:, at * HEAD_DIM : (at + 1) * HEAD_DIM], blank], axis=1
            )

    def attend(slot):
        rows = slot_rows(slot)
        where_seg = slot_of(lax.rem(slot, 2), lax.div(slot, 2), y, z)
        seg = S[where_seg, 5:6, :SEQ]
        seg_column = jnp.transpose(jnp.broadcast_to(seg, (8, SEQ)))[:, :1]
        same = seg_column == seg
        pieces = []
        for head in range(LOCAL):
            query = qp[rows, head * PAD : (head + 1) * PAD]
            key = qp[rows, (LOCAL + head) * PAD : (LOCAL + head + 1) * PAD]
            value = qp[rows, (2 * LOCAL + head) * PAD : (2 * LOCAL + head + 1) * PAD]
            scores = jnp.where(same, dot_nt(query, key) * HEAD_DIM ** (-0.5), masked_score)
            exp_scores = jnp.exp(scores - jnp.max(scores, axis=1, keepdims=True))
            probs = (exp_scores / jnp.sum(exp_scores, axis=1, keepdims=True)).astype(bf16)
            P[slot * LOCAL + head] = probs
            pieces.append(dot_nn(probs, value).astype(bf16)[:, :HEAD_DIM])
        mixed[rows, :] = jnp.concatenate(pieces, axis=1)

    def pair(body, group):
        def step(at, carry):
            body(2 * group + lax.rem(c + at, 2))
            return carry

        lax.fori_loop(0, 2, step, 0)

    got(eight(1 - c, 1 - x), IDS.small_d)
    pair(project, x)
    pair(attend, x)
    proj_forward(1)
    spread_end(H1, IDS.h1)
    pair(project, 1 - x)
    proj_forward(3)
    pair(attend, 1 - x)
    proj_forward(2)
    forward(1, 1)
    spread_mate(D2, IDS.d2)
    spread_mid(D2, IDS.d2)


    def reduce_first(partial, rr, ident):
        sA[...] = partial(qd_).astype(bf16)
        send(sA, rr.at[0], ident, mate)
        keep[...] = partial(qx_)
        sB[...] = partial(qp_).astype(bf16)

    def reduce_next(partial, rr, ident):
        got(rr.at[0], ident)
        sX[...] = (keep[...] + rr[0].astype(f32)).astype(bf16)
        send(sX, rr.at[2], ident + 2, xnb)
        send(sB, rr.at[1], ident + 1, mate)
        own[...] = partial(q)

    def reduce_last(rr, ident):
        got(rr.at[1], ident + 1)
        got(rr.at[2], ident + 2)
        settle((ident, ident + 1, ident + 2))

    def total_rows(rr, at):
        rows = pl.ds(at, TILE)
        return own[rows, :] + rr[1, rows, :].astype(f32) + rr[2, rows, :].astype(f32)

    proj_arrived()

    def part_one(slot):
        return dot_nn(mixed[slot_rows(slot), :], W_proj[...])

    reduce_first(part_one, rrA, IDS.r1)
    reduce_next(part_one, rrA, IDS.r1)
    forward(1, 3)
    own_y(2)
    reduce_last(rrA, IDS.r1)


    def norm_two(at):
        rows = pl.ds(at, TILE)
        branch = total_rows(rrA, at) + bias[0:1, :]
        b1[rows, :] = branch
        stream = tok[rows, :].astype(f32) + row_of(2) * branch
        resid[rows, :] = stream
        normed, _ = normalize(stream)
        H2[pl.ds(pl.multiple_of(q * SEQ + at, TILE), TILE), :] = (
            normed * (1.0 + row_of(4)) + row_of(3)
        ).astype(bf16)

    tiles(norm_two)
    spread_start(H2, IDS.h2)
    forward(1, 2)
    spread_end(D2, IDS.d2)
    spread_mate(H2, IDS.h2)
    spread_mid(H2, IDS.h2)
    arrived(1)

    CHUNK = 384

    def first_layer(slot):
        rows = slot_rows(slot)
        for at in range(0, PART, CHUNK):
            pre = dot_nn(H2[rows, :], G_fc1[:, at : at + CHUNK]) + bias[2:3, at : at + CHUNK]
            square = pre * pre
            bend = jnp.tanh(root_half * (pre + 0.044715 * square * pre))
            active[rows, at : at + CHUNK] = (0.5 * pre * (1.0 + bend)).astype(bf16)
            slope[rows, at : at + CHUNK] = (
                0.5 * (1.0 + bend)
                + 0.5 * pre * (1.0 - bend * bend) * root_half * (1.0 + 3.0 * 0.044715 * square)
            ).astype(bf16)

    pair(first_layer, x)
    forward(2, 1)
    spread_end(H2, IDS.h2)
    pair(first_layer, 1 - x)
    forward(2, 3)

    def cross(left, right, dest, width):
        def step(at, carry):
            part = pl.ds(pl.multiple_of(at * CHUNK, CHUNK), CHUNK)
            dest[part, :] = dot_tn(left[:, part], right[...]).astype(bf16)
            return carry

        lax.fori_loop(0, width // CHUNK, step, 0)

    cross(active, D2, g_fc2, PART)

    def grad_start(kind, grads, steps):
        for k in steps:
            send(
                grads.at[chip_rows(z_to(k), 1 - y), :], yr_w[kind].at[k], IDS.gy[kind] + k, ynb
            )

    def add_block(grads, rows_at, extra):
        def step(at, carry):
            rows = pl.ds(pl.multiple_of(rows_at + at * 48, 16), 48)
            grads[rows, :] = (
                grads[rows, :].astype(f32) + extra[pl.ds(pl.multiple_of(at * 48, 16), 48), :].astype(f32)
            ).astype(bf16)
            return carry

        lax.fori_loop(0, 3, step, 0)

    def grad_mid(kind, grads, k):
        zz = z_to(k)
        got(yr_w[kind].at[k], IDS.gy[kind] + k)
        add_block(grads, (2 * zz + y) * 144, yr_w[kind].at[k])
        send(
            grads.at[chip_rows(zz, y), :], zr_w[kind].at[k - 1], IDS.gz[kind] + k - 1, znb(k)
        )

    def grad_end(kind, grads):
        got(yr_w[kind].at[0], IDS.gy[kind])
        for k in (1, 2, 3):
            got(zr_w[kind].at[k - 1], IDS.gz[kind] + k - 1)
        width = grads.shape[1]
        A, B, fr = fa_w[kind], fb_w[kind], fr_w[kind]
        for at in range(0, width, CHUNK):
            cols = slice(at, min(at + CHUNK, width))
            total = grads[chip_rows(z, y), cols].astype(f32) + yr_w[kind][0, :, cols].astype(f32)
            for k in range(3):
                total = total + zr_w[kind][k, :, cols].astype(f32)
            low, high = total[:72], total[72:]
            mine = jnp.where(c == 0, low, high).astype(bf16)
            A[:, cols] = mine
            B[:, cols] = jnp.where(c == 0, high, low).astype(bf16)
            fr[q, :, cols] = mine
        send(B, fr.at[q], IDS.gf[kind], mate)
        send(A, fr.at[q], IDS.gf[kind] + 1, xnb)
        send(B, fr.at[q], IDS.gf[kind] + 2, diag)

    slots = [area.at[72 * at : 72 * (at + 1), :] for area in (resid, b1, keep, own) for at in range(3)]
    out_copies = []

    def leave(value, target):
        at = len(out_copies)
        if at >= len(slots):
            out_copies[at - len(slots)].wait()
        slots[at % len(slots)][...] = value
        copy = pltpu.make_async_copy(slots[at % len(slots)], target, loc.at[2 + at])
        copy.start()
        out_copies.append(copy)

    def columns_of(ref, piece):
        return ref.at[:, piece * WIDTH : (piece + 1) * WIDTH]

    def grad_out(kind):
        fr = fr_w[kind]
        for step, source in enumerate((qp_, qx_, qd_)):
            got(fr.at[source], IDS.gf[kind] + step)
        if kind == 2:
            for at in range(4):
                leave(fr[at].astype(f32), ofc2.at[at])
            return
        for piece in range(3 if kind == 0 else 4):
            leave(
                jnp.concatenate(
                    [
                        fr[at, :, (4 * piece + step) * 72 : (4 * piece + step + 1) * 72]
                        for step in range(4)
                        for at in range(4)
                    ],
                    axis=1,
                ).astype(f32),
                columns_of(oqkv if kind == 0 else ofc1, piece),
            )

    grad_start(2, g_fc2, (1,))
    forward(2, 2)
    grad_start(2, g_fc2, (3, 2, 0))
    arrived(2)

    def back_hidden(slot):
        rows = slot_rows(slot)
        for at in range(0, PART, CHUNK):
            low = (
                dot_nt(D2[rows, :], G_fc2[at : at + CHUNK, :])
                * slope[rows, at : at + CHUNK].astype(f32)
            ).astype(bf16)
            slope[rows, at : at + CHUNK] = low
            acc[8:9, at : at + CHUNK] += jnp.sum(low.astype(f32), axis=0, keepdims=True)

    pair(back_hidden, x)
    pair(back_hidden, 1 - x)
    d_pre = slope
    settle(tuple(IDS.d2 + step for step in range(3)))
    D1 = D2
    def part_three(slot):
        return dot_nt(d_pre[slot_rows(slot), :], G_fc1[...])

    reduce_first(part_three, rrA, IDS.r3)
    reduce_next(part_three, rrA, IDS.r3)
    cross(H2, d_pre, g_fc1, WIDTH)
    grad_start(1, g_fc1, (1, 3, 2, 0))
    grad_mid(2, g_fc2, 1)
    reduce_last(rrA, IDS.r3)

    def back_two(at):
        rows = pl.ds(at, TILE)
        d_hidden = total_rows(rrA, at)
        normed, inv = normalize(resid[rows, :])
        add_row(3, d_hidden)
        add_row(4, d_hidden * normed)
        d_resid = og[rows, :].astype(f32) + normalize_back(d_hidden * (1.0 + row_of(4)), normed, inv)
        add_row(2, d_resid * b1[rows, :])
        low = (d_resid * row_of(2)).astype(bf16)
        add_row(7, low.astype(f32))
        D1[pl.ds(pl.multiple_of(q * SEQ + at, TILE), TILE), :] = low
        b1[rows, :] = d_resid

    tiles(back_two)
    spread_start(D1, IDS.d1)

    def part_two(slot):
        return dot_nn(active[slot_rows(slot), :], G_fc2[...])

    reduce_first(part_two, rrB, IDS.r2)
    reduce_next(part_two, rrB, IDS.r2)

    def finish_forward(at):
        rows = pl.ds(at, TILE)
        branch = total_rows(rrB, at) + bias[1:2, :]
        rrB[0, rows, :] = (resid[rows, :] + row_of(5) * branch).astype(bf16)
        add_row(5, og[rows, :].astype(f32) * branch)

    grad_mid(2, g_fc2, 3)
    spread_mate(D1, IDS.d1)


    def attend_backward(slot):
        rows = slot_rows(slot)
        d_mix = dot_nt(D1[rows, :], W_proj[...]).astype(bf16)
        blank = jnp.zeros((SEQ, PAD - HEAD_DIM), bf16)
        scale = HEAD_DIM ** (-0.5)
        d_query, d_key, d_value = [], [], []
        for head in range(LOCAL):
            query = qp[rows, head * PAD : (head + 1) * PAD]
            key = qp[rows, (LOCAL + head) * PAD : (LOCAL + head + 1) * PAD]
            value = qp[rows, (2 * LOCAL + head) * PAD : (2 * LOCAL + head + 1) * PAD]
            d_head = jnp.concatenate([d_mix[:, head * HEAD_DIM : (head + 1) * HEAD_DIM], blank], axis=1)
            probs = P[slot * LOCAL + head]
            d_probs = dot_nt(d_head, value)
            d_value.append(dot_tn(probs, d_head).astype(bf16)[:, :HEAD_DIM])
            wide = probs.astype(f32)
            d_scores = (wide * (d_probs - jnp.sum(d_probs * wide, axis=1, keepdims=True))).astype(bf16)
            d_query.append((dot_nn(d_scores, key) * scale).astype(bf16)[:, :HEAD_DIM])
            d_key.append((dot_tn(d_scores, query) * scale).astype(bf16)[:, :HEAD_DIM])
        value = jnp.concatenate(d_query + d_key + d_value, axis=1)
        dprj[rows, :] = value
        acc[9:10, :QKV] += jnp.sum(value.astype(f32), axis=0, keepdims=True)

    pair(attend_backward, x)
    spread_mid(D1, IDS.d1)
    grad_mid(2, g_fc2, 2)
    grad_mid(1, g_fc1, 1)
    spread_end(D1, IDS.d1)
    pair(attend_backward, 1 - x)
    grad_mid(1, g_fc1, 3)
    cross(H1, dprj, g_qkv, WIDTH)
    grad_start(0, g_qkv, (1, 3, 2, 0))

    def part_four(slot):
        return dot_nt(dprj[slot_rows(slot), :], G_qkv[...])

    settle((IDS.r2, IDS.r2 + 1))
    reduce_first(part_four, rrA, IDS.r4)
    grad_mid(1, g_fc1, 2)
    reduce_last(rrB, IDS.r2)
    tiles(finish_forward)
    row_copies = [pltpu.make_async_copy(rrB.at[0], out, loc.at[20])]
    row_copies[0].start()
    reduce_next(part_four, rrA, IDS.r4)
    proj_grads = dot_tn(mixed[...], D1[...])
    for head in range(LOCAL):
        g_proj[head] = proj_grads[head * 72 : (head + 1) * 72].astype(bf16)
    grad_mid(0, g_qkv, 1)
    grad_end(2, g_fc2)
    grad_mid(0, g_qkv, 3)
    reduce_last(rrA, IDS.r4)

    def back_one(at):
        rows = pl.ds(at, TILE)
        d_hidden = total_rows(rrA, at)
        normed, inv = normalize(tok[rows, :].astype(f32))
        add_row(0, d_hidden)
        add_row(1, d_hidden * normed)
        sA[rows, :] = (
            b1[rows, :] + normalize_back(d_hidden * (1.0 + row_of(1)), normed, inv)
        ).astype(bf16)

    tiles(back_one)
    row_copies.append(pltpu.make_async_copy(sA, tgrad, loc.at[21]))
    row_copies[1].start()

    E[my_slot] = acc[...].astype(bf16)
    send(E.at[my_slot], E.at[my_slot], IDS.end_y, ynb)

    @pl.when(jnp.logical_not(in_column))
    def _():
        for k in range(4):
            rc(g_proj.at[z_to(k)], yr_proj.at[k], IDS.gy[3] + k, ynb).start()

    grad_mid(0, g_qkv, 2)
    grad_end(1, g_fc1)
    got(E.at[slot_of(c, x, 1 - y, z)], IDS.end_y)
    for k in (2, 1, 3):
        for yy in range(2):
            part = E.at[slot_of(c, x, yy, z)]
            send(part, part, IDS.end_z + 2 * (k - 1) + yy, znb(k))

    @pl.when(in_column)
    def _():
        for k in STEPS:
            zz = z_to(k)
            got(yr_proj.at[k], IDS.gy[3] + k)
            g_proj[zz] = (g_proj[zz].astype(f32) + yr_proj[k].astype(f32)).astype(bf16)
            rc(g_proj.at[zz], zr_proj.at[k - 1], IDS.gz[3] + k - 1, znb(k)).start()

    grad_out(2)
    for k in (1, 2, 3):
        for yy in range(2):
            got(E.at[slot_of(c, x, yy, z_from(k))], IDS.end_z + 2 * (k - 1) + yy)
    group = lambda cc, xx: E.at[pl.ds((cc * 2 + xx) * 8, 8)]
    send(group(c, x), group(c, x), IDS.end_x, xnb)
    grad_end(0, g_qkv)

    @pl.when(in_column)
    def _():
        got(yr_proj.at[0], IDS.gy[3])
        total = g_proj[z].astype(f32) + yr_proj[0].astype(f32)
        for k in (1, 2, 3):
            got(zr_proj.at[k - 1], IDS.gz[3] + k - 1)
            total = total + zr_proj[k - 1].astype(f32)
        p_out[...] = total.astype(bf16)
        rc(p_out, p_out, IDS.gf[3], xnb).start()

    grad_out(1)
    got(group(c, 1 - x), IDS.end_x)
    send(E.at[pl.ds(c * 16, 16)], E.at[pl.ds(c * 16, 16)], IDS.end_c, mate)

    @pl.when(jnp.logical_not(in_column))
    def _():
        got(p_out, IDS.gf[3])

    leave(p_out[...].astype(f32), oproj)
    got(E.at[pl.ds((1 - c) * 16, 16)], IDS.end_c)

    act_all = pick_columns(lambda piece: S[:, piece, :].astype(bf16))[:, :72]
    for section in range(6):
        rows = E[:, section, :]
        leave(dot_tn(act_all, rows), columns_of(oada, section))
        osum[section : section + 1, :] = jnp.sum(rows.astype(f32), axis=0, keepdims=True)
    for section in (6, 7):
        osum[section : section + 1, :] = jnp.sum(E[:, section, :].astype(f32), axis=0, keepdims=True)
    for section in (8, 9):
        for quarter in range(4):
            start = ((quarter % 2) * 2 + quarter // 2) * 8
            at = 8 + 4 * (section - 8) + quarter
            osum[at : at + 1, :] = jnp.sum(
                E[start : start + 8, section, :].astype(f32), axis=0, keepdims=True
            )
    grad_out(0)
    for copy in out_copies[-len(slots) :]:
        copy.wait()
    for copy in row_copies:
        copy.wait()
    for src, ident, _ in pending:
        sent(src, ident)

    @pl.when(in_column)
    def _():
        for k in (1, 2, 3):
            sent(p_out, IDS.gz[3] + k - 1)
        sent(p_out, IDS.gf[3])

    @pl.when(jnp.logical_not(in_column))
    def _():
        for k in range(4):
            sent(p_out, IDS.gy[3] + k)


def one_kernel(
    tokens,
    cond,
    segment_ids,
    ada_weight,
    ada_bias,
    qkv_weight,
    qv_bias,
    proj_weight,
    proj_bias,
    fc1_weight,
    fc1_bias,
    fc2_weight,
    fc2_bias,
    out_grad,
):
    fsdp_at = lax.axis_index("fsdp")
    cond_float = cond[0].astype(f32)
    cond_act = (cond_float / (1.0 + jnp.exp(-cond_float))).astype(bf16).astype(f32)
    blank = lambda count: jnp.zeros((count,), f32)
    small = jnp.concatenate(
        [
            cond_act,
            qv_bias.astype(f32),
            proj_bias.astype(f32),
            fc2_bias.astype(f32),
            blank(96),
            fc1_bias.astype(f32),
            blank(96),
            segment_ids[0].astype(f32),
            blank(128 + 768),
        ]
    ).reshape(8, 384)
    adab = lax.dynamic_update_slice_in_dim(
        blank(8 * WIDTH), ada_bias.astype(f32), fsdp_at * 432, 0
    ).reshape(8, WIDTH)
    wfc2 = fc2_weight.reshape(4, 72, WIDTH)
    vmem = pl.BlockSpec(memory_space=pltpu.VMEM)
    anywhere = pl.BlockSpec(memory_space=pl.ANY)
    outside = pl.BlockSpec(memory_space=pltpu.HBM)
    shape = jax.ShapeDtypeStruct
    scratch = [pltpu.VMEM(dims, kind) for dims, kind in SCRATCH]
    out, tgrad, oada, oqkv, oproj, ofc1, ofc2, osum = pl.pallas_call(
        block_kernel,
        out_shape=(
            shape((SEQ, WIDTH), bf16),
            shape((SEQ, WIDTH), bf16),
            shape((72, 6 * WIDTH), f32),
            shape((72, 3 * WIDTH), f32),
            shape((72, WIDTH), f32),
            shape((72, HIDDEN), f32),
            shape((4, 72, WIDTH), f32),
            shape((16, WIDTH), f32),
        ),
        in_specs=[vmem, vmem, vmem, vmem, vmem, vmem, anywhere, vmem, anywhere],
        out_specs=(outside,) * 7 + (vmem,),
        scratch_shapes=scratch
        + [
            pltpu.SemaphoreType.DMA((ID_COUNT,)),
            pltpu.SemaphoreType.DMA((ID_COUNT,)),
            pltpu.SemaphoreType.DMA((22,)),
        ],
        compiler_params=pltpu.CompilerParams(
            collective_id=0, has_side_effects=True, vmem_limit_bytes=67043328
        ),
        name="whole_block",
    )(tokens[0], out_grad[0], small, ada_weight, adab, qkv_weight, proj_weight, fc1_weight, wfc2)
    def mine(vector, count):
        return lax.dynamic_slice_in_dim(vector, fsdp_at * count, count, 0)

    by_head = osum[12:16, :QKV].reshape(4, 3, 4, 72).transpose(1, 2, 0, 3).reshape(3 * WIDTH)
    return (
        out[None],
        tgrad[None],
        oada,
        mine(osum[:6].reshape(-1), 432),
        oqkv,
        mine(jnp.concatenate([by_head[:WIDTH], by_head[2 * WIDTH :]]), 144),
        oproj,
        mine(osum[7], 72),
        ofc1,
        mine(osum[8:12].reshape(4, 16, 72).transpose(1, 0, 2).reshape(-1), 288),
        ofc2.reshape(288, WIDTH),
        mine(osum[6], 72),
    )


def solution(mesh):
    in_specs = (
        P(("fsdp", "dp"), None, None),
        P(("fsdp", "dp"), None),
        P(("fsdp", "dp"), None),
        P("fsdp", None),
        P("fsdp"),
        P("fsdp", None),
        P("fsdp"),
        P("fsdp", None),
        P("fsdp"),
        P("fsdp", None),
        P("fsdp"),
        P("fsdp", None),
        P("fsdp"),
        P(("fsdp", "dp"), None, None),
    )
    out_specs = (
        P(("fsdp", "dp"), None, None),
        P(("fsdp", "dp"), None, None),
        P("fsdp", None),
        P("fsdp"),
        P("fsdp", None),
        P("fsdp"),
        P("fsdp", None),
        P("fsdp"),
        P("fsdp", None),
        P("fsdp"),
        P("fsdp", None),
        P("fsdp"),
    )
    fits = (mesh.shape["fsdp"], mesh.shape["dp"]) == (16, 2)
    return jax.shard_map(
        one_kernel if fits else general_form, mesh=mesh, in_specs=in_specs, out_specs=out_specs, check_vma=False
    )
```

```python
import functools

import jax
import jax.numpy as jnp
from jax import lax
from jax.experimental import pallas as pl
from jax.experimental.pallas import tpu as pltpu
from jax.sharding import PartitionSpec as P

HEADS = 16
HEAD_DIM = 72


root_half = 0.7978845608028654
norm_eps = 1e-06
masked_score = -1e30


def gelu_tanh(stream):
    return (
        0.5 * stream * (1.0 + jnp.tanh(root_half * (stream + 0.044715 * stream * stream * stream)))
    )


def gelu_slope(stream):
    tanh_inner = jnp.tanh(root_half * (stream + 0.044715 * stream * stream * stream))
    return 0.5 * (1.0 + tanh_inner) + 0.5 * stream * (1.0 - tanh_inner * tanh_inner) * root_half * (
        1.0 + 3.0 * 0.044715 * stream * stream
    )


def normalize(stream):
    centre = jnp.mean(stream, axis=-1, keepdims=True)
    centred = stream - centre
    inv_std = lax.rsqrt(jnp.mean(centred * centred, axis=-1, keepdims=True) + norm_eps)
    return (centred * inv_std, inv_std)


def normalize_back(incoming, normed, inv_std):
    return inv_std * (
        incoming
        - jnp.mean(incoming, axis=-1, keepdims=True)
        - normed * jnp.mean(incoming * normed, axis=-1, keepdims=True)
    )


def head_scores(projected, same_doc, head_index, model_width):
    query_part = lax.dynamic_slice_in_dim(projected, head_index * HEAD_DIM, HEAD_DIM, 1)
    key_part = lax.dynamic_slice_in_dim(projected, model_width + head_index * HEAD_DIM, HEAD_DIM, 1)
    value_part = lax.dynamic_slice_in_dim(
        projected, 2 * model_width + head_index * HEAD_DIM, HEAD_DIM, 1
    )
    raw_scores = jnp.einsum(
        "qd,kd->qk", query_part, key_part, preferred_element_type=jnp.float32
    ) * HEAD_DIM ** (-0.5)
    return (jnp.where(same_doc, raw_scores, masked_score), query_part, key_part, value_part)


def merge_heads(stacked, model_width):
    return jnp.transpose(stacked, (1, 0, 2)).reshape(stacked.shape[1], model_width)


def attend_row(projected, segments_row, model_width):
    same_doc = segments_row[:, None] == segments_row[None, :]

    def one_head(head_index):
        scores, query_part, key_part, value_part = head_scores(
            projected, same_doc, head_index, model_width
        )
        top_score = jnp.max(scores, axis=-1, keepdims=True)
        exp_scores = jnp.exp(scores - top_score)
        denominator = jnp.sum(exp_scores, axis=-1, keepdims=True)
        probabilities = (exp_scores / denominator).astype(jnp.bfloat16)
        mixed_heads = jnp.dot(probabilities, value_part, preferred_element_type=jnp.float32)
        return (mixed_heads, (top_score + jnp.log(denominator))[:, 0])

    mixed_heads, log_total = lax.map(one_head, jnp.arange(HEADS))
    return (merge_heads(mixed_heads, model_width).astype(jnp.bfloat16), log_total)


def attend_back(projected, segments_row, log_total, d_mixed, model_width):
    same_doc = segments_row[:, None] == segments_row[None, :]
    head_scale = HEAD_DIM ** (-0.5)

    def one_head(head_index):
        scores, query_part, key_part, value_part = head_scores(
            projected, same_doc, head_index, model_width
        )
        d_head = lax.dynamic_slice_in_dim(d_mixed, head_index * HEAD_DIM, HEAD_DIM, 1)
        lse_row = lax.dynamic_index_in_dim(log_total, head_index, 0, keepdims=False)
        probabilities = jnp.exp(scores - lse_row[:, None])
        prob_low = probabilities.astype(jnp.bfloat16)
        d_probs = jnp.einsum("qd,kd->qk", d_head, value_part, preferred_element_type=jnp.float32)
        d_value = jnp.einsum("qk,qd->kd", prob_low, d_head, preferred_element_type=jnp.float32)
        d_scores = (
            probabilities * (d_probs - jnp.sum(d_probs * probabilities, axis=-1, keepdims=True))
        ).astype(jnp.bfloat16)
        d_query = (
            jnp.einsum("qk,kd->qd", d_scores, key_part, preferred_element_type=jnp.float32)
            * head_scale
        )
        d_key = (
            jnp.einsum("qk,qd->kd", d_scores, query_part, preferred_element_type=jnp.float32)
            * head_scale
        )
        return (d_query, d_key, d_value)

    d_query, d_key, d_value = lax.map(one_head, jnp.arange(HEADS))
    merged = [
        merge_heads(d_query, model_width),
        merge_heads(d_key, model_width),
        merge_heads(d_value, model_width),
    ]
    return jnp.concatenate(merged, axis=-1).astype(jnp.bfloat16)


def general_form(
    tokens,
    cond,
    segment_ids,
    ada_weight,
    ada_bias,
    qkv_weight,
    qv_bias,
    proj_weight,
    proj_bias,
    fc1_weight,
    fc1_bias,
    fc2_weight,
    fc2_bias,
    out_grad,
):
    row_count, seq_len, model_width = tokens.shape
    ff_width = fc1_weight.shape[1]
    stream = tokens.astype(jnp.float32)
    cond_float = cond.astype(jnp.float32)
    cond_act = (cond_float / (1.0 + jnp.exp(-cond_float))).astype(jnp.bfloat16)
    fsdp_at, dp_at = lax.axis_index("fsdp"), lax.axis_index("dp")
    dp_size = lax.axis_size("dp")
    slice_width, bias_width = ada_weight.shape[0], ada_bias.shape[0]
    act_all = lax.all_gather(cond_act, ("fsdp", "dp"), axis=0, tiled=True)
    act_mine = lax.dynamic_slice_in_dim(act_all, fsdp_at * slice_width, slice_width, 1)
    partial = jnp.dot(act_mine, ada_weight, preferred_element_type=jnp.float32)
    bias_row = lax.dynamic_update_slice_in_dim(
        jnp.zeros((6 * model_width,), jnp.float32),
        ada_bias.astype(jnp.float32),
        fsdp_at * bias_width,
        0,
    )
    partial = (partial + bias_row).reshape(-1, dp_size, row_count, 6 * model_width)
    partial = lax.dynamic_index_in_dim(partial, dp_at, 1, keepdims=False)
    modulation = lax.psum_scatter(
        partial.reshape(-1, 6 * model_width), "fsdp", scatter_dimension=0, tiled=True
    )
    pieces = [
        modulation[:, None, section * model_width : (section + 1) * model_width]
        for section in range(6)
    ]
    shift_one, scale_one, gate_one, shift_two, scale_two, gate_two = pieces
    qkv_full, qv_bias_full, proj_full, proj_bias_full = (
        lax.all_gather(qkv_weight, "fsdp", axis=0, tiled=True),
        lax.all_gather(qv_bias, "fsdp", axis=0, tiled=True),
        lax.all_gather(proj_weight, "fsdp", axis=0, tiled=True),
        lax.all_gather(proj_bias, "fsdp", axis=0, tiled=True),
    )
    normed_one, inv_one = normalize(stream)
    hidden_one = (normed_one * (1.0 + scale_one) + shift_one).astype(jnp.bfloat16)
    qv_float = qv_bias_full.astype(jnp.float32)
    qkv_bias = jnp.concatenate(
        [qv_float[:model_width], jnp.zeros((model_width,), jnp.float32), qv_float[model_width:]]
    )
    projected = (
        jnp.dot(hidden_one, qkv_full, preferred_element_type=jnp.float32) + qkv_bias
    ).astype(jnp.bfloat16)

    def row_forward(row_items):
        return attend_row(row_items[0], row_items[1], model_width)

    mixed_rows, log_total = lax.map(row_forward, (projected, segment_ids))
    branch_one = jnp.dot(
        mixed_rows, proj_full, preferred_element_type=jnp.float32
    ) + proj_bias_full.astype(jnp.float32)
    resid_one = stream + gate_one * branch_one
    fc1_full, fc1_bias_full, fc2_full, fc2_bias_full = (
        lax.all_gather(fc1_weight, "fsdp", axis=0, tiled=True),
        lax.all_gather(fc1_bias, "fsdp", axis=0, tiled=True),
        lax.all_gather(fc2_weight, "fsdp", axis=0, tiled=True),
        lax.all_gather(fc2_bias, "fsdp", axis=0, tiled=True),
    )
    normed_two, inv_two = normalize(resid_one)
    hidden_two = (normed_two * (1.0 + scale_two) + shift_two).astype(jnp.bfloat16)
    pre_act = jnp.dot(
        hidden_two, fc1_full, preferred_element_type=jnp.float32
    ) + fc1_bias_full.astype(jnp.float32)
    active = gelu_tanh(pre_act).astype(jnp.bfloat16)
    branch_two = jnp.dot(
        active, fc2_full, preferred_element_type=jnp.float32
    ) + fc2_bias_full.astype(jnp.float32)
    output = (resid_one + gate_two * branch_two).astype(jnp.bfloat16)
    d_out = out_grad.astype(jnp.float32)
    fc1_back, fc2_back = (
        lax.all_gather(fc1_weight, "fsdp", axis=0, tiled=True),
        lax.all_gather(fc2_weight, "fsdp", axis=0, tiled=True),
    )
    d_gate_two = jnp.sum(d_out * branch_two, axis=1)
    d_branch_two = (d_out * gate_two).astype(jnp.bfloat16)
    fc2_shard = lax.psum_scatter(
        jnp.einsum("rsf,rsd->fd", active, d_branch_two, preferred_element_type=jnp.float32).astype(
            jnp.bfloat16
        ),
        "fsdp",
        scatter_dimension=0,
        tiled=True,
    )
    grad_fc2_bias = jnp.sum(d_branch_two.astype(jnp.float32), axis=(0, 1))
    d_active = jnp.einsum("rsd,fd->rsf", d_branch_two, fc2_back, preferred_element_type=jnp.float32)
    d_pre = (d_active * gelu_slope(pre_act)).astype(jnp.bfloat16)
    grad_fc1_bias = jnp.sum(d_pre.astype(jnp.float32), axis=(0, 1))
    d_hidden_two = jnp.einsum("rsf,ef->rse", d_pre, fc1_back, preferred_element_type=jnp.float32)
    d_scale_two = jnp.sum(d_hidden_two * normed_two, axis=1)
    d_shift_two = jnp.sum(d_hidden_two, axis=1)
    d_resid = d_out + normalize_back(d_hidden_two * (1.0 + scale_two), normed_two, inv_two)
    qkv_back, proj_back = (
        lax.all_gather(qkv_weight, "fsdp", axis=0, tiled=True),
        lax.all_gather(proj_weight, "fsdp", axis=0, tiled=True),
    )
    d_gate_one = jnp.sum(d_resid * branch_one, axis=1)
    d_branch_one = (d_resid * gate_one).astype(jnp.bfloat16)
    grad_proj_bias = jnp.sum(d_branch_one.astype(jnp.float32), axis=(0, 1))
    d_mixed = jnp.einsum(
        "rsd,ed->rse", d_branch_one, proj_back, preferred_element_type=jnp.float32
    ).astype(jnp.bfloat16)

    def row_backward(row_items):
        return attend_back(row_items[0], row_items[1], row_items[2], row_items[3], model_width)

    d_projected = lax.map(row_backward, (projected, segment_ids, log_total, d_mixed))
    d_proj_float = d_projected.astype(jnp.float32)
    grad_qv_bias = jnp.concatenate(
        [
            jnp.sum(d_proj_float[..., :model_width], axis=(0, 1)),
            jnp.sum(d_proj_float[..., 2 * model_width :], axis=(0, 1)),
        ]
    )
    d_hidden_one = jnp.einsum(
        "rsf,ef->rse", d_projected, qkv_back, preferred_element_type=jnp.float32
    )
    d_scale_one = jnp.sum(d_hidden_one * normed_one, axis=1)
    d_shift_one = jnp.sum(d_hidden_one, axis=1)
    tokens_grad = (
        d_resid + normalize_back(d_hidden_one * (1.0 + scale_one), normed_one, inv_one)
    ).astype(jnp.bfloat16)
    d_modulation = jnp.concatenate(
        [d_shift_one, d_scale_one, d_gate_one, d_shift_two, d_scale_two, d_gate_two], axis=-1
    ).astype(jnp.bfloat16)
    d_mod_all = lax.all_gather(d_modulation, ("fsdp", "dp"), axis=0, tiled=True)
    grad_ada = jnp.einsum("rd,re->de", act_mine, d_mod_all, preferred_element_type=jnp.float32)
    grad_ada_bias = jnp.sum(
        lax.dynamic_slice_in_dim(d_mod_all, fsdp_at * bias_width, bias_width, 1).astype(jnp.float32),
        axis=0,
    )

    def owners(term):
        return lax.psum_scatter(
            term.astype(jnp.bfloat16), "fsdp", scatter_dimension=0, tiled=True
        )

    qkv_shard = owners(
        jnp.einsum("rse,rsf->ef", hidden_one, d_projected, preferred_element_type=jnp.float32)
    )
    proj_shard = owners(
        jnp.einsum("rse,rsd->ed", mixed_rows, d_branch_one, preferred_element_type=jnp.float32)
    )
    fc1_shard = owners(
        jnp.einsum("rse,rsf->ef", hidden_two, d_pre, preferred_element_type=jnp.float32)
    )
    bias_shards = (
        None,
        lax.psum_scatter(
            grad_qv_bias.astype(jnp.bfloat16), "fsdp", scatter_dimension=0, tiled=True
        ).astype(jnp.float32),
        lax.psum_scatter(
            grad_proj_bias.astype(jnp.bfloat16), "fsdp", scatter_dimension=0, tiled=True
        ).astype(jnp.float32),
        lax.psum_scatter(
            grad_fc1_bias.astype(jnp.bfloat16), "fsdp", scatter_dimension=0, tiled=True
        ).astype(jnp.float32),
        lax.psum_scatter(
            grad_fc2_bias.astype(jnp.bfloat16), "fsdp", scatter_dimension=0, tiled=True
        ).astype(jnp.float32),
    )
    summed = (
        grad_ada,
        grad_ada_bias,
        lax.psum(qkv_shard.astype(jnp.bfloat16), "dp").astype(jnp.float32),
        lax.psum(bias_shards[1].astype(jnp.bfloat16), "dp").astype(jnp.float32),
        lax.psum(proj_shard.astype(jnp.bfloat16), "dp").astype(jnp.float32),
        lax.psum(bias_shards[2].astype(jnp.bfloat16), "dp").astype(jnp.float32),
        lax.psum(fc1_shard.astype(jnp.bfloat16), "dp").astype(jnp.float32),
        lax.psum(bias_shards[3].astype(jnp.bfloat16), "dp").astype(jnp.float32),
        lax.psum(fc2_shard, "dp").astype(jnp.float32),
        lax.psum(bias_shards[4].astype(jnp.bfloat16), "dp").astype(jnp.float32),
    )
    return (
        output,
        tokens_grad,
        summed[0],
        summed[1],
        summed[2],
        summed[3],
        summed[4],
        summed[5],
        summed[6],
        summed[7],
        summed[8],
        summed[9],
    )


MESH_ID = pl.DeviceIdType.MESH
f32 = jnp.float32
bf16 = jnp.bfloat16

SEQ = 256
WIDTH = 1152
HIDDEN = 4608
PART = 1152
QKV = 864
PAD = 128
LOCAL = 4


def dot_nn(left, right):
    return lax.dot_general(left, right, (((1,), (0,)), ((), ())), preferred_element_type=f32)


def dot_nt(left, right):
    return lax.dot_general(left, right, (((1,), (1,)), ((), ())), preferred_element_type=f32)


def dot_tn(left, right):
    return lax.dot_general(left, right, (((0,), (0,)), ((), ())), preferred_element_type=f32)


def iota(shape, axis):
    return lax.broadcasted_iota(jnp.int32, shape, axis)


def whole_part(value, divisor):
    return jnp.floor((value + 0.5) * (1.0 / divisor))


class Ids:
    def __init__(self):
        self.used = 0

    def take(self, count):
        start = self.used
        self.used += count
        return start


IDS = Ids()
IDS.small_y, IDS.small_z, IDS.small_c = IDS.take(1), IDS.take(6), IDS.take(1)
IDS.small_x, IDS.small_d = IDS.take(1), IDS.take(1)
IDS.mod_c, IDS.mod_y, IDS.mod_z = IDS.take(1), IDS.take(1), IDS.take(3)
IDS.core = [IDS.take(1) for _ in range(3)]
IDS.z = [IDS.take(3) for _ in range(4)]
IDS.y = [IDS.take(4) for _ in range(4)]
IDS.pass_on = [IDS.take(5) for _ in range(4)]
IDS.h1, IDS.h2, IDS.d2, IDS.d1 = IDS.take(3), IDS.take(3), IDS.take(3), IDS.take(3)
IDS.r1, IDS.r2, IDS.r3, IDS.r4 = IDS.take(3), IDS.take(3), IDS.take(3), IDS.take(3)
IDS.gy = [IDS.take(4) for _ in range(4)]
IDS.gz = [IDS.take(3) for _ in range(4)]
IDS.gf = [IDS.take(3) for _ in range(4)]
IDS.end_y, IDS.end_z, IDS.end_x, IDS.end_c = IDS.take(1), IDS.take(6), IDS.take(1), IDS.take(1)
ID_COUNT = IDS.used

SCRATCH = (
    ((32, 8, 384), f32),
    ((16, 8, WIDTH), f32),
    ((8, 8, WIDTH), f32),
    ((4, 8, WIDTH), f32),
    ((3, 8, WIDTH), f32),
    ((8, WIDTH), f32),
    ((72, WIDTH), bf16),
    ((72, QKV), bf16),
    ((72, PART), bf16),
    ((72, WIDTH), bf16),
    ((WIDTH, QKV), bf16),
    ((WIDTH, PART), bf16),
    ((PART, WIDTH), bf16),
    ((4, 72, WIDTH), bf16),
    ((288, WIDTH), bf16),
    ((1024, WIDTH), bf16),
    ((1024, WIDTH), bf16),
    ((1024, WIDTH), bf16),
    ((1024, 12 * PAD), bf16),
    ((16, SEQ, SEQ), bf16),
    ((1024, 288), bf16),
    ((1024, PART), bf16),
    ((1024, PART), bf16),
    ((1024, QKV), bf16),
    ((3, SEQ, WIDTH), bf16),
    ((3, SEQ, WIDTH), bf16),
    ((SEQ, WIDTH), bf16),
    ((SEQ, WIDTH), bf16),
    ((SEQ, WIDTH), bf16),
    ((SEQ, WIDTH), f32),
    ((SEQ, WIDTH), f32),
    ((SEQ, WIDTH), f32),
    ((SEQ, WIDTH), f32),
    ((16, WIDTH), f32),
    ((8, WIDTH), f32),
    ((WIDTH, QKV), bf16),
    ((WIDTH, PART), bf16),
    ((PART, WIDTH), bf16),
    ((4, 72, WIDTH), bf16),
    ((4, 144, QKV), bf16),
    ((4, 144, PART), bf16),
    ((4, 144, WIDTH), bf16),
    ((4, 72, WIDTH), bf16),
    ((3, 144, QKV), bf16),
    ((3, 144, PART), bf16),
    ((3, 144, WIDTH), bf16),
    ((3, 72, WIDTH), bf16),
    ((72, QKV), bf16),
    ((72, PART), bf16),
    ((72, WIDTH), bf16),
    ((72, QKV), bf16),
    ((72, PART), bf16),
    ((72, WIDTH), bf16),
    ((4, 72, QKV), bf16),
    ((4, 72, PART), bf16),
    ((4, 72, WIDTH), bf16),
    ((72, WIDTH), bf16),
    ((32, 16, WIDTH), bf16),
)


def block_kernel(
    tok, og, small, ada, adab, wqkv, wproj, wfc1, wfc2, out,
    tgrad, oada, oqkv, oproj, ofc1, ofc2, osum, S, modp, modc,
    mody, modz, mod, own_fc2, xr_qkv, xr_fc1, xr_fc2, G_qkv,
    G_fc1, G_fc2, G_proj, W_proj, H1, H2, D2, qp, P, mixed,
    active, slope, dprj, rrA, rrB, sA, sB, sX, keep, own,
    b1, resid, acc, bias, g_qkv, g_fc1, g_fc2, g_proj, yr_qkv, yr_fc1,
    yr_fc2, yr_proj, zr_qkv, zr_fc1, zr_fc2, zr_proj, fa_qkv, fa_fc1, fa_fc2, fb_qkv,
    fb_fc1, fb_fc2, fr_qkv, fr_fc1, fr_fc2, p_out, E, snd, rcv, loc,
):
    xr_w, G_w = (xr_qkv, xr_fc1, xr_fc2), (G_qkv, G_fc1, G_fc2)
    yr_w, zr_w = (yr_qkv, yr_fc1, yr_fc2), (zr_qkv, zr_fc1, zr_fc2)
    fa_w, fb_w, fr_w = (fa_qkv, fa_fc1, fa_fc2), (fb_qkv, fb_fc1, fb_fc2), (fr_qkv, fr_fc1, fr_fc2)
    f = lax.axis_index("fsdp")
    x = lax.axis_index("dp")
    z = lax.div(f, 4)
    y = lax.rem(lax.div(f, 2), 2)
    c = lax.rem(f, 2)
    q = 2 * x + c
    qp_, qx_, qd_ = 2 * x + 1 - c, 2 * (1 - x) + c, 2 * (1 - x) + 1 - c

    def dev(zz, yy, cc, xx):
        return ((zz * 2 + yy) * 2 + cc, xx)

    mate, xnb, diag, ynb = dev(z, y, 1 - c, x), dev(z, y, c, 1 - x), dev(z, y, 1 - c, 1 - x), dev(z, 1 - y, c, x)

    def z_to(k):
        return lax.rem(z + k, 4)

    def z_from(k):
        return lax.rem(z + 4 - k, 4)

    def znb(k):
        return dev(z_to(k), y, c, x)

    def rc(src, dst, ident, to):
        return pltpu.make_async_remote_copy(
            src_ref=src, dst_ref=dst, send_sem=snd.at[ident], recv_sem=rcv.at[ident],
            device_id=to, device_id_type=MESH_ID,
        )

    pending = []

    def send(src, dst, ident, to):
        rc(src, dst, ident, to).start()
        pending.append((src, ident, to))

    def got(dst, ident):
        rc(dst, dst, ident, mate).wait_recv()

    def sent(src, ident):
        rc(src, src, ident, mate).wait_send()

    def settle(first):
        keep_on = []
        for item in pending:
            if item[1] in first:
                sent(item[0], item[1])
            else:
                keep_on.append(item)
        pending[:] = keep_on

    barrier = pltpu.get_barrier_semaphore()
    neighbours = [mate, xnb, diag, ynb, znb(1), znb(2), znb(3)]
    for to in neighbours:
        pl.semaphore_signal(barrier, inc=1, device_id=to, device_id_type=MESH_ID)
    pl.semaphore_wait(barrier, len(neighbours))


    def slot_of(cc, xx, yy, zz):
        return ((cc * 2 + xx) * 2 + yy) * 4 + zz

    my_slot = slot_of(c, x, y, z)
    send(small, S.at[my_slot], IDS.small_y, ynb)
    own_copy = pltpu.make_async_copy(wfc2.at[q], own_fc2, loc.at[0])
    own_copy.start()
    send(wfc2.at[qp_], xr_fc2, IDS.core[2], mate)

    def split_qkv():
        for at in range(4):
            fr_qkv[at] = jnp.concatenate(
                [wqkv[:, (4 * step + at) * 72 : (4 * step + at + 1) * 72] for step in range(12)], axis=1
            )
        send(fr_qkv.at[qp_], xr_qkv, IDS.core[0], mate)

    def split_fc1():
        for at in range(4):
            fr_fc1[at] = jnp.concatenate(
                [wfc1[:, (4 * step + at) * 72 : (4 * step + at + 1) * 72] for step in range(16)], axis=1
            )
        send(fr_fc1.at[qp_], xr_fc1, IDS.core[1], mate)

    split_qkv()
    S[my_slot] = small[...]
    acc[...] = jnp.zeros((16, WIDTH), f32)
    in_column = y == x
    proj_copy = pltpu.make_async_copy(wproj, G_proj.at[z], loc.at[1])

    def chip_rows(zz, yy):
        return pl.ds(pl.multiple_of((2 * zz + yy) * 144, 16), 144)

    def own_part(kind):
        return G_w[kind].at[chip_rows(z, y), :]

    def assemble(kind):
        got(xr_w[kind], IDS.core[kind])
        mine = (own_fc2[...] if kind == 2 else fr_w[kind][q]).astype(f32)
        other = xr_w[kind][...].astype(f32)
        low = jnp.where(c == 0, mine, other)
        high = jnp.where(c == 0, other, mine)
        G_w[kind][chip_rows(z, y), :] = jnp.concatenate([low, high], axis=0).astype(bf16)

    def own_y(kind):
        send(own_part(kind), own_part(kind), IDS.y[kind], ynb)

    inner = (z == 1) | (z == 2)
    relays = []

    def relay(wanted, part, source, ident, send_ident, to):
        @pl.when(wanted)
        def _():
            pltpu.make_async_remote_copy(
                src_ref=source, dst_ref=part, send_sem=snd.at[send_ident], recv_sem=rcv.at[ident],
                device_id=to, device_id_type=MESH_ID,
            ).start()

        relays.append((wanted, part, send_ident))

    def own_z(kind):
        part = own_part(kind)
        relay(z < 3, part, part, IDS.z[kind], IDS.pass_on[kind], znb(1))
        relay(z > 0, part, part, IDS.z[kind] + 2, IDS.pass_on[kind] + 1, znb(3))

    STEPS = (1, 3, 2)

    def near(j):
        middle = STEPS[j]
        return jnp.where(z == 0, 3 - j, jnp.where(z == 3, 1 + j, middle))

    def onward(k):
        return lax.rem(z + jnp.where(k <= z, 1, 3), 4), jnp.where(k <= z, k, k - 2)

    def forward(kind, j):
        k = near(j)
        part = G_w[kind].at[chip_rows(z_from(k), y), :]
        got(part, IDS.z[kind] + k - 1)
        where, at = onward(k)
        relay(inner, part, part, IDS.z[kind] + at, IDS.pass_on[kind] + 2 + j, dev(where, y, c, x))
        send(part, part, IDS.y[kind] + 1 + j, ynb)

    def arrived(kind):
        other = 1 - y
        got(G_w[kind].at[chip_rows(z, other), :], IDS.y[kind])
        for j in range(3):
            got(G_w[kind].at[chip_rows(z_from(near(j)), other), :], IDS.y[kind] + 1 + j)

    def proj_z():
        @pl.when(in_column)
        def _():
            proj_copy.start()

        part = G_proj.at[z]
        relay(in_column & (z < 3), part, wproj, IDS.z[3], IDS.pass_on[3], znb(1))
        relay(in_column & (z > 0), part, wproj, IDS.z[3] + 2, IDS.pass_on[3] + 1, znb(3))

    def proj_y():
        @pl.when(in_column)
        def _():
            rc(wproj, G_proj.at[z], IDS.y[3], ynb).start()

    def proj_forward(j):
        k = near(j)
        part = G_proj.at[z_from(k)]

        @pl.when(in_column)
        def _():
            got(part, IDS.z[3] + k - 1)
            rc(part, part, IDS.y[3] + 1 + j, ynb).start()

        where, at = onward(k)
        relay(in_column & inner, part, part, IDS.z[3] + at, IDS.pass_on[3] + 2 + j, dev(where, y, c, x))

    def proj_arrived():
        @pl.when(in_column)
        def _():
            proj_copy.wait()
            sent(wproj, IDS.y[3])
            for j in range(3):
                sent(G_proj.at[z_from(near(j))], IDS.y[3] + 1 + j)

        @pl.when(jnp.logical_not(in_column))
        def _():
            got(G_proj.at[z], IDS.y[3])
            for j in range(3):
                got(G_proj.at[z_from(near(j))], IDS.y[3] + 1 + j)

        W_proj[...] = jnp.concatenate(
            [G_proj[head].astype(f32) for head in range(LOCAL)], axis=0
        ).astype(bf16)

    got(S.at[slot_of(c, x, 1 - y, z)], IDS.small_y)
    for k in (2, 1, 3):
        for yy in range(2):
            part = S.at[slot_of(c, x, yy, z)]
            send(part, part, IDS.small_z + 2 * (k - 1) + yy, znb(k))
    assemble(0)
    own_y(0)
    own_z(0)
    for k in (1, 2, 3):
        for yy in range(2):
            got(S.at[slot_of(c, x, yy, z_from(k))], IDS.small_z + 2 * (k - 1) + yy)
    eight = lambda cc, xx: S.at[pl.ds((cc * 2 + xx) * 8, 8)]
    send(eight(c, x), eight(c, x), IDS.small_c, mate)
    send(eight(c, x), eight(c, x), IDS.small_x, xnb)

    def pick_columns(rows):
        total = None
        for piece in range(3):
            kk = iota((384, PAD), 0) + piece * 384
            jj = iota((384, PAD), 1)
            chosen = ((kk == 72 * f + jj) & (jj < 72)).astype(f32).astype(bf16)
            term = dot_nn(rows(piece), chosen)
            total = term if total is None else total + term
        return total.astype(bf16)

    got(eight(1 - c, x), IDS.small_c)
    act = pick_columns(
        lambda piece: jnp.concatenate(
            [S[pl.ds((cc * 2 + x) * 8, 8), piece, :] for cc in range(2)], axis=0
        ).astype(bf16)
    )[:, :72]
    for section in range(6):
        modp[:, section, :] = dot_nn(
            act, ada[:, section * WIDTH : (section + 1) * WIDTH]
        ) + adab[section : section + 1, :]
    for section in (6, 7):
        modp[:, section, :] = jnp.zeros((16, WIDTH), f32)
    theirs, ours = modp.at[pl.ds((1 - c) * 8, 8)], modp.at[pl.ds(c * 8, 8)]
    send(theirs, modc, IDS.mod_c, mate)
    split_fc1()
    got(modc, IDS.mod_c)
    for at in range(8):
        ours[at] += modc[at]
    send(modp.at[pl.ds(c * 8 + (1 - y) * 4, 4)], mody, IDS.mod_y, ynb)
    forward(0, 0)
    own_copy.wait()
    assemble(1)
    got(mody, IDS.mod_y)
    base = c * 8 + y * 4
    for at in range(4):
        modp[base + at] += mody[at]
    for k in (2, 1, 3):
        send(modp.at[base + z_to(k)], modz.at[k - 1], IDS.mod_z + k - 1, znb(k))
    forward(0, 1)
    proj_z()
    own_z(1)
    assemble(2)
    proj_y()
    own_y(1)
    got(eight(c, 1 - x), IDS.small_x)
    send(eight(c, 1 - x), eight(c, 1 - x), IDS.small_d, mate)

    def place(row, width, lane_of, owner_of):
        kk = iota((384, width), 1).astype(f32)
        jj = iota((384, width), 0).astype(f32)
        chosen = (jj == lane_of(kk)).astype(f32).astype(bf16)
        spread = dot_nn(row.astype(bf16), chosen)
        at = iota((16, width), 0)
        slot_f = ((lax.rem(at, 4) * 2 + lax.rem(lax.div(at, 4), 2)) * 2 + lax.div(at, 8)).astype(f32)
        mine = slot_f == owner_of(iota((16, width), 1).astype(f32))
        return jnp.sum(jnp.where(mine, spread, 0.0), axis=0, keepdims=True)

    def plane(piece):
        return jnp.concatenate([S[pl.ds((cc * 2 + x) * 8, 8), piece, :] for cc in range(2)], axis=0)

    def mod72(kk):
        return kk - 72.0 * whole_part(kk, 72)

    by72 = lambda kk: whole_part(kk, 72)
    qf, xf, cf = q.astype(f32), x.astype(f32), c.astype(f32)
    row3, row4 = plane(3), plane(4)
    bias[0:1, :] = place(row3, WIDTH, lambda kk: 144.0 + mod72(kk), by72)
    bias[1:2, :] = place(row3, WIDTH, lambda kk: 216.0 + mod72(kk), by72)
    bias[2:3, :] = place(row4, WIDTH, lambda kk: 72.0 * qf + mod72(kk), by72)

    def qkv_owner(kk):
        third = whole_part(kk, 288)
        head = whole_part(kk - 288.0 * third, 72)
        owner = 2.0 * head + xf + 4.0 * third
        return jnp.where((third == 1.0) | (third > 2.5), -1.0, owner)

    bias[3:4, :] = place(row3, WIDTH, lambda kk: 72.0 * cf + mod72(kk), qkv_owner)

    for k in (1, 2, 3):
        got(modz.at[k - 1], IDS.mod_z + k - 1)
    mod[...] = modp[base + z] + modz[0] + modz[1] + modz[2]

    def row_of(section):
        return mod[section : section + 1, :]

    def slot_rows(slot):
        return pl.ds(pl.multiple_of(slot * SEQ, SEQ), SEQ)

    TILE = 64

    def tiles(body):
        def step(at, carry):
            body(pl.multiple_of(at * TILE, TILE))
            return carry

        lax.fori_loop(0, SEQ // TILE, step, 0)


    def norm_one(at):
        normed, _ = normalize(tok[pl.ds(at, TILE), :].astype(f32))
        H1[pl.ds(pl.multiple_of(q * SEQ + at, TILE), TILE), :] = (
            normed * (1.0 + row_of(1)) + row_of(0)
        ).astype(bf16)

    tiles(norm_one)

    def spread_start(buf, ident):
        part = buf.at[slot_rows(q), :]
        send(part, part, ident, mate)
        send(part, part, ident + 1, xnb)

    def spread_mid(buf, ident):
        part = buf.at[slot_rows(qx_), :]
        got(part, ident + 1)
        send(part, part, ident + 2, mate)

    def spread_mate(buf, ident):
        got(buf.at[slot_rows(qp_), :], ident)

    def spread_end(buf, ident):
        got(buf.at[slot_rows(qd_), :], ident + 2)

    spread_start(H1, IDS.h1)
    settle(tuple(IDS.core))

    def add_row(at, value):
        acc[at : at + 1, :] += jnp.sum(value, axis=0, keepdims=True)

    def out_gate(at):
        low = (og[pl.ds(at, TILE), :].astype(f32) * row_of(5)).astype(bf16)
        D2[pl.ds(pl.multiple_of(q * SEQ + at, TILE), TILE), :] = low
        add_row(6, low.astype(f32))

    tiles(out_gate)
    spread_start(D2, IDS.d2)
    spread_mate(H1, IDS.h1)
    forward(0, 2)
    spread_mid(H1, IDS.h1)
    arrived(0)


    def project(slot):
        rows = slot_rows(slot)
        value = (dot_nn(H1[rows, :], G_qkv[...]) + bias[3:4, :QKV]).astype(bf16)
        blank = jnp.zeros((SEQ, PAD - HEAD_DIM), bf16)
        for at in range(12):
            qp[rows, at * PAD : (at + 1) * PAD] = jnp.concatenate(
                [value[:, at * HEAD_DIM : (at + 1) * HEAD_DIM], blank], axis=1
            )

    def attend(slot):
        rows = slot_rows(slot)
        where_seg = slot_of(lax.rem(slot, 2), lax.div(slot, 2), y, z)
        seg = S[where_seg, 5:6, :SEQ]
        seg_column = jnp.transpose(jnp.broadcast_to(seg, (8, SEQ)))[:, :1]
        same = seg_column == seg
        pieces = []
        for head in range(LOCAL):
            query = qp[rows, head * PAD : (head + 1) * PAD]
            key = qp[rows, (LOCAL + head) * PAD : (LOCAL + head + 1) * PAD]
            value = qp[rows, (2 * LOCAL + head) * PAD : (2 * LOCAL + head + 1) * PAD]
            scores = jnp.where(same, dot_nt(query, key) * HEAD_DIM ** (-0.5), masked_score)
            exp_scores = jnp.exp(scores - jnp.max(scores, axis=1, keepdims=True))
            probs = (exp_scores / jnp.sum(exp_scores, axis=1, keepdims=True)).astype(bf16)
            P[slot * LOCAL + head] = probs
            pieces.append(dot_nn(probs, value).astype(bf16)[:, :HEAD_DIM])
        mixed[rows, :] = jnp.concatenate(pieces, axis=1)

    def pair(body, group):
        def step(at, carry):
            body(2 * group + lax.rem(c + at, 2))
            return carry

        lax.fori_loop(0, 2, step, 0)

    got(eight(1 - c, 1 - x), IDS.small_d)
    proj_forward(0)
    pair(project, x)
    forward(1, 0)
    proj_forward(1)
    pair(attend, x)
    forward(1, 1)
    proj_forward(2)
    own_z(2)
    spread_end(H1, IDS.h1)
    pair(project, 1 - x)
    forward(1, 2)
    pair(attend, 1 - x)
    spread_mate(D2, IDS.d2)
    spread_mid(D2, IDS.d2)


    def reduce_first(partial, rr, ident):
        sA[...] = partial(qd_).astype(bf16)
        send(sA, rr.at[0], ident, mate)
        keep[...] = partial(qx_)
        sB[...] = partial(qp_).astype(bf16)

    def reduce_next(partial, rr, ident):
        got(rr.at[0], ident)
        sX[...] = (keep[...] + rr[0].astype(f32)).astype(bf16)
        send(sX, rr.at[2], ident + 2, xnb)
        send(sB, rr.at[1], ident + 1, mate)
        own[...] = partial(q)

    def reduce_last(rr, ident):
        got(rr.at[1], ident + 1)
        got(rr.at[2], ident + 2)
        settle((ident, ident + 1, ident + 2))

    def total_rows(rr, at):
        rows = pl.ds(at, TILE)
        return own[rows, :] + rr[1, rows, :].astype(f32) + rr[2, rows, :].astype(f32)

    proj_arrived()

    def part_one(slot):
        return dot_nn(mixed[slot_rows(slot), :], W_proj[...])

    reduce_first(part_one, rrA, IDS.r1)
    reduce_next(part_one, rrA, IDS.r1)
    own_y(2)
    forward(2, 0)
    reduce_last(rrA, IDS.r1)


    def norm_two(at):
        rows = pl.ds(at, TILE)
        branch = total_rows(rrA, at) + bias[0:1, :]
        b1[rows, :] = branch
        stream = tok[rows, :].astype(f32) + row_of(2) * branch
        resid[rows, :] = stream
        normed, _ = normalize(stream)
        H2[pl.ds(pl.multiple_of(q * SEQ + at, TILE), TILE), :] = (
            normed * (1.0 + row_of(4)) + row_of(3)
        ).astype(bf16)

    tiles(norm_two)
    spread_start(H2, IDS.h2)
    forward(2, 1)
    spread_end(D2, IDS.d2)
    spread_mate(H2, IDS.h2)
    spread_mid(H2, IDS.h2)
    arrived(1)

    CHUNK = 384

    def first_layer(slot):
        rows = slot_rows(slot)
        for at in range(0, PART, CHUNK):
            pre = dot_nn(H2[rows, :], G_fc1[:, at : at + CHUNK]) + bias[2:3, at : at + CHUNK]
            square = pre * pre
            bend = jnp.tanh(root_half * (pre + 0.044715 * square * pre))
            active[rows, at : at + CHUNK] = (0.5 * pre * (1.0 + bend)).astype(bf16)
            slope[rows, at : at + CHUNK] = (
                0.5 * (1.0 + bend)
                + 0.5 * pre * (1.0 - bend * bend) * root_half * (1.0 + 3.0 * 0.044715 * square)
            ).astype(bf16)

    pair(first_layer, x)
    forward(2, 2)
    spread_end(H2, IDS.h2)
    pair(first_layer, 1 - x)

    def cross(left, right, dest, width):
        def step(at, carry):
            part = pl.ds(pl.multiple_of(at * CHUNK, CHUNK), CHUNK)
            dest[part, :] = dot_tn(left[:, part], right[...]).astype(bf16)
            return carry

        lax.fori_loop(0, width // CHUNK, step, 0)

    cross(active, D2, g_fc2, PART)

    def grad_start(kind, grads, steps):
        for k in steps:
            send(
                grads.at[chip_rows(z_to(k), 1 - y), :], yr_w[kind].at[k], IDS.gy[kind] + k, ynb
            )

    def add_block(grads, rows_at, extra):
        def step(at, carry):
            rows = pl.ds(pl.multiple_of(rows_at + at * 48, 16), 48)
            grads[rows, :] = (
                grads[rows, :].astype(f32) + extra[pl.ds(pl.multiple_of(at * 48, 16), 48), :].astype(f32)
            ).astype(bf16)
            return carry

        lax.fori_loop(0, 3, step, 0)

    def grad_mid(kind, grads, k):
        zz = z_to(k)
        got(yr_w[kind].at[k], IDS.gy[kind] + k)
        add_block(grads, (2 * zz + y) * 144, yr_w[kind].at[k])
        send(
            grads.at[chip_rows(zz, y), :], zr_w[kind].at[k - 1], IDS.gz[kind] + k - 1, znb(k)
        )

    def grad_end(kind, grads):
        got(yr_w[kind].at[0], IDS.gy[kind])
        for k in (1, 2, 3):
            got(zr_w[kind].at[k - 1], IDS.gz[kind] + k - 1)
        width = grads.shape[1]
        A, B, fr = fa_w[kind], fb_w[kind], fr_w[kind]
        for at in range(0, width, CHUNK):
            cols = slice(at, min(at + CHUNK, width))
            total = grads[chip_rows(z, y), cols].astype(f32) + yr_w[kind][0, :, cols].astype(f32)
            for k in range(3):
                total = total + zr_w[kind][k, :, cols].astype(f32)
            low, high = total[:72], total[72:]
            mine = jnp.where(c == 0, low, high).astype(bf16)
            A[:, cols] = mine
            B[:, cols] = jnp.where(c == 0, high, low).astype(bf16)
            fr[q, :, cols] = mine
        send(B, fr.at[q], IDS.gf[kind], mate)
        send(A, fr.at[q], IDS.gf[kind] + 1, xnb)
        send(B, fr.at[q], IDS.gf[kind] + 2, diag)

    slots = [area.at[72 * at : 72 * (at + 1), :] for area in (resid, b1, keep, own) for at in range(3)]
    out_copies = []

    def leave(value, target):
        at = len(out_copies)
        if at >= len(slots):
            out_copies[at - len(slots)].wait()
        slots[at % len(slots)][...] = value
        copy = pltpu.make_async_copy(slots[at % len(slots)], target, loc.at[2 + at])
        copy.start()
        out_copies.append(copy)

    def columns_of(ref, piece):
        return ref.at[:, piece * WIDTH : (piece + 1) * WIDTH]

    def grad_out(kind):
        fr = fr_w[kind]
        for step, source in enumerate((qp_, qx_, qd_)):
            got(fr.at[source], IDS.gf[kind] + step)
        if kind == 2:
            for at in range(4):
                leave(fr[at].astype(f32), ofc2.at[at])
            return
        for piece in range(3 if kind == 0 else 4):
            leave(
                jnp.concatenate(
                    [
                        fr[at, :, (4 * piece + step) * 72 : (4 * piece + step + 1) * 72]
                        for step in range(4)
                        for at in range(4)
                    ],
                    axis=1,
                ).astype(f32),
                columns_of(oqkv if kind == 0 else ofc1, piece),
            )

    grad_start(2, g_fc2, (1, 3, 2, 0))
    arrived(2)

    def back_hidden(slot):
        rows = slot_rows(slot)
        for at in range(0, PART, CHUNK):
            low = (
                dot_nt(D2[rows, :], G_fc2[at : at + CHUNK, :])
                * slope[rows, at : at + CHUNK].astype(f32)
            ).astype(bf16)
            slope[rows, at : at + CHUNK] = low
            acc[8:9, at : at + CHUNK] += jnp.sum(low.astype(f32), axis=0, keepdims=True)

    pair(back_hidden, x)
    pair(back_hidden, 1 - x)
    d_pre = slope
    settle(tuple(IDS.d2 + step for step in range(3)))
    D1 = D2
    def part_three(slot):
        return dot_nt(d_pre[slot_rows(slot), :], G_fc1[...])

    reduce_first(part_three, rrA, IDS.r3)
    reduce_next(part_three, rrA, IDS.r3)
    cross(H2, d_pre, g_fc1, WIDTH)
    grad_start(1, g_fc1, (1, 3, 2, 0))
    grad_mid(2, g_fc2, 1)
    reduce_last(rrA, IDS.r3)

    def back_two(at):
        rows = pl.ds(at, TILE)
        d_hidden = total_rows(rrA, at)
        normed, inv = normalize(resid[rows, :])
        add_row(3, d_hidden)
        add_row(4, d_hidden * normed)
        d_resid = og[rows, :].astype(f32) + normalize_back(d_hidden * (1.0 + row_of(4)), normed, inv)
        add_row(2, d_resid * b1[rows, :])
        low = (d_resid * row_of(2)).astype(bf16)
        add_row(7, low.astype(f32))
        D1[pl.ds(pl.multiple_of(q * SEQ + at, TILE), TILE), :] = low
        b1[rows, :] = d_resid

    tiles(back_two)
    spread_start(D1, IDS.d1)

    def part_two(slot):
        return dot_nn(active[slot_rows(slot), :], G_fc2[...])

    reduce_first(part_two, rrB, IDS.r2)
    reduce_next(part_two, rrB, IDS.r2)

    def finish_forward(at):
        rows = pl.ds(at, TILE)
        branch = total_rows(rrB, at) + bias[1:2, :]
        rrB[0, rows, :] = (resid[rows, :] + row_of(5) * branch).astype(bf16)
        add_row(5, og[rows, :].astype(f32) * branch)

    grad_mid(2, g_fc2, 3)
    spread_mate(D1, IDS.d1)


    def attend_backward(slot):
        rows = slot_rows(slot)
        d_mix = dot_nt(D1[rows, :], W_proj[...]).astype(bf16)
        blank = jnp.zeros((SEQ, PAD - HEAD_DIM), bf16)
        scale = HEAD_DIM ** (-0.5)
        d_query, d_key, d_value = [], [], []
        for head in range(LOCAL):
            query = qp[rows, head * PAD : (head + 1) * PAD]
            key = qp[rows, (LOCAL + head) * PAD : (LOCAL + head + 1) * PAD]
            value = qp[rows, (2 * LOCAL + head) * PAD : (2 * LOCAL + head + 1) * PAD]
            d_head = jnp.concatenate([d_mix[:, head * HEAD_DIM : (head + 1) * HEAD_DIM], blank], axis=1)
            probs = P[slot * LOCAL + head]
            d_probs = dot_nt(d_head, value)
            d_value.append(dot_tn(probs, d_head).astype(bf16)[:, :HEAD_DIM])
            wide = probs.astype(f32)
            d_scores = (wide * (d_probs - jnp.sum(d_probs * wide, axis=1, keepdims=True))).astype(bf16)
            d_query.append((dot_nn(d_scores, key) * scale).astype(bf16)[:, :HEAD_DIM])
            d_key.append((dot_tn(d_scores, query) * scale).astype(bf16)[:, :HEAD_DIM])
        value = jnp.concatenate(d_query + d_key + d_value, axis=1)
        dprj[rows, :] = value
        acc[9:10, :QKV] += jnp.sum(value.astype(f32), axis=0, keepdims=True)

    pair(attend_backward, x)
    spread_mid(D1, IDS.d1)
    grad_mid(2, g_fc2, 2)
    grad_mid(1, g_fc1, 1)
    spread_end(D1, IDS.d1)
    pair(attend_backward, 1 - x)
    grad_mid(1, g_fc1, 3)
    cross(H1, dprj, g_qkv, WIDTH)
    grad_start(0, g_qkv, (1, 3, 2, 0))

    def part_four(slot):
        return dot_nt(dprj[slot_rows(slot), :], G_qkv[...])

    settle((IDS.r2, IDS.r2 + 1))
    reduce_first(part_four, rrA, IDS.r4)
    grad_mid(1, g_fc1, 2)
    reduce_last(rrB, IDS.r2)
    tiles(finish_forward)
    row_copies = [pltpu.make_async_copy(rrB.at[0], out, loc.at[20])]
    row_copies[0].start()
    reduce_next(part_four, rrA, IDS.r4)
    proj_grads = dot_tn(mixed[...], D1[...])
    for head in range(LOCAL):
        g_proj[head] = proj_grads[head * 72 : (head + 1) * 72].astype(bf16)
    grad_mid(0, g_qkv, 1)
    grad_end(2, g_fc2)
    grad_mid(0, g_qkv, 3)
    reduce_last(rrA, IDS.r4)

    def back_one(at):
        rows = pl.ds(at, TILE)
        d_hidden = total_rows(rrA, at)
        normed, inv = normalize(tok[rows, :].astype(f32))
        add_row(0, d_hidden)
        add_row(1, d_hidden * normed)
        sA[rows, :] = (
            b1[rows, :] + normalize_back(d_hidden * (1.0 + row_of(1)), normed, inv)
        ).astype(bf16)

    tiles(back_one)
    row_copies.append(pltpu.make_async_copy(sA, tgrad, loc.at[21]))
    row_copies[1].start()

    E[my_slot] = acc[...].astype(bf16)
    send(E.at[my_slot], E.at[my_slot], IDS.end_y, ynb)

    @pl.when(jnp.logical_not(in_column))
    def _():
        for k in range(4):
            rc(g_proj.at[z_to(k)], yr_proj.at[k], IDS.gy[3] + k, ynb).start()

    grad_mid(0, g_qkv, 2)
    grad_end(1, g_fc1)
    got(E.at[slot_of(c, x, 1 - y, z)], IDS.end_y)
    for k in (2, 1, 3):
        for yy in range(2):
            part = E.at[slot_of(c, x, yy, z)]
            send(part, part, IDS.end_z + 2 * (k - 1) + yy, znb(k))

    @pl.when(in_column)
    def _():
        for k in STEPS:
            zz = z_to(k)
            got(yr_proj.at[k], IDS.gy[3] + k)
            g_proj[zz] = (g_proj[zz].astype(f32) + yr_proj[k].astype(f32)).astype(bf16)
            rc(g_proj.at[zz], zr_proj.at[k - 1], IDS.gz[3] + k - 1, znb(k)).start()

    grad_out(2)
    for k in (1, 2, 3):
        for yy in range(2):
            got(E.at[slot_of(c, x, yy, z_from(k))], IDS.end_z + 2 * (k - 1) + yy)
    group = lambda cc, xx: E.at[pl.ds((cc * 2 + xx) * 8, 8)]
    send(group(c, x), group(c, x), IDS.end_x, xnb)
    grad_end(0, g_qkv)

    @pl.when(in_column)
    def _():
        got(yr_proj.at[0], IDS.gy[3])
        total = g_proj[z].astype(f32) + yr_proj[0].astype(f32)
        for k in (1, 2, 3):
            got(zr_proj.at[k - 1], IDS.gz[3] + k - 1)
            total = total + zr_proj[k - 1].astype(f32)
        p_out[...] = total.astype(bf16)
        rc(p_out, p_out, IDS.gf[3], xnb).start()

    grad_out(1)
    got(group(c, 1 - x), IDS.end_x)
    send(E.at[pl.ds(c * 16, 16)], E.at[pl.ds(c * 16, 16)], IDS.end_c, mate)

    @pl.when(jnp.logical_not(in_column))
    def _():
        got(p_out, IDS.gf[3])

    leave(p_out[...].astype(f32), oproj)
    got(E.at[pl.ds((1 - c) * 16, 16)], IDS.end_c)

    act_all = pick_columns(lambda piece: S[:, piece, :].astype(bf16))[:, :72]
    for section in range(6):
        rows = E[:, section, :]
        leave(dot_tn(act_all, rows), columns_of(oada, section))
        osum[section : section + 1, :] = jnp.sum(rows.astype(f32), axis=0, keepdims=True)
    for section in (6, 7):
        osum[section : section + 1, :] = jnp.sum(E[:, section, :].astype(f32), axis=0, keepdims=True)
    for section in (8, 9):
        for quarter in range(4):
            start = ((quarter % 2) * 2 + quarter // 2) * 8
            at = 8 + 4 * (section - 8) + quarter
            osum[at : at + 1, :] = jnp.sum(
                E[start : start + 8, section, :].astype(f32), axis=0, keepdims=True
            )
    grad_out(0)
    for copy in out_copies[-len(slots) :]:
        copy.wait()
    for copy in row_copies:
        copy.wait()
    for src, ident, _ in pending:
        sent(src, ident)
    for wanted, part, ident in relays:

        @pl.when(wanted)
        def _(part=part, ident=ident):
            sent(part, ident)


    @pl.when(in_column)
    def _():
        for k in (1, 2, 3):
            sent(p_out, IDS.gz[3] + k - 1)
        sent(p_out, IDS.gf[3])

    @pl.when(jnp.logical_not(in_column))
    def _():
        for k in range(4):
            sent(p_out, IDS.gy[3] + k)


def one_kernel(
    tokens,
    cond,
    segment_ids,
    ada_weight,
    ada_bias,
    qkv_weight,
    qv_bias,
    proj_weight,
    proj_bias,
    fc1_weight,
    fc1_bias,
    fc2_weight,
    fc2_bias,
    out_grad,
):
    fsdp_at = lax.axis_index("fsdp")
    cond_float = cond[0].astype(f32)
    cond_act = (cond_float / (1.0 + jnp.exp(-cond_float))).astype(bf16).astype(f32)
    blank = lambda count: jnp.zeros((count,), f32)
    small = jnp.concatenate(
        [
            cond_act,
            qv_bias.astype(f32),
            proj_bias.astype(f32),
            fc2_bias.astype(f32),
            blank(96),
            fc1_bias.astype(f32),
            blank(96),
            segment_ids[0].astype(f32),
            blank(128 + 768),
        ]
    ).reshape(8, 384)
    adab = lax.dynamic_update_slice_in_dim(
        blank(8 * WIDTH), ada_bias.astype(f32), fsdp_at * 432, 0
    ).reshape(8, WIDTH)
    wfc2 = fc2_weight.reshape(4, 72, WIDTH)
    vmem = pl.BlockSpec(memory_space=pltpu.VMEM)
    anywhere = pl.BlockSpec(memory_space=pl.ANY)
    outside = pl.BlockSpec(memory_space=pltpu.HBM)
    shape = jax.ShapeDtypeStruct
    scratch = [pltpu.VMEM(dims, kind) for dims, kind in SCRATCH]
    out, tgrad, oada, oqkv, oproj, ofc1, ofc2, osum = pl.pallas_call(
        block_kernel,
        out_shape=(
            shape((SEQ, WIDTH), bf16),
            shape((SEQ, WIDTH), bf16),
            shape((72, 6 * WIDTH), f32),
            shape((72, 3 * WIDTH), f32),
            shape((72, WIDTH), f32),
            shape((72, HIDDEN), f32),
            shape((4, 72, WIDTH), f32),
            shape((16, WIDTH), f32),
        ),
        in_specs=[vmem, vmem, vmem, vmem, vmem, vmem, anywhere, vmem, anywhere],
        out_specs=(outside,) * 7 + (vmem,),
        scratch_shapes=scratch
        + [
            pltpu.SemaphoreType.DMA((ID_COUNT,)),
            pltpu.SemaphoreType.DMA((ID_COUNT,)),
            pltpu.SemaphoreType.DMA((22,)),
        ],
        compiler_params=pltpu.CompilerParams(
            collective_id=0, has_side_effects=True, vmem_limit_bytes=67043328
        ),
        name="whole_block",
    )(tokens[0], out_grad[0], small, ada_weight, adab, qkv_weight, proj_weight, fc1_weight, wfc2)
    def mine(vector, count):
        return lax.dynamic_slice_in_dim(vector, fsdp_at * count, count, 0)

    by_head = osum[12:16, :QKV].reshape(4, 3, 4, 72).transpose(1, 2, 0, 3).reshape(3 * WIDTH)
    return (
        out[None],
        tgrad[None],
        oada,
        mine(osum[:6].reshape(-1), 432),
        oqkv,
        mine(jnp.concatenate([by_head[:WIDTH], by_head[2 * WIDTH :]]), 144),
        oproj,
        mine(osum[7], 72),
        ofc1,
        mine(osum[8:12].reshape(4, 16, 72).transpose(1, 0, 2).reshape(-1), 288),
        ofc2.reshape(288, WIDTH),
        mine(osum[6], 72),
    )


def solution(mesh):
    in_specs = (
        P(("fsdp", "dp"), None, None),
        P(("fsdp", "dp"), None),
        P(("fsdp", "dp"), None),
        P("fsdp", None),
        P("fsdp"),
        P("fsdp", None),
        P("fsdp"),
        P("fsdp", None),
        P("fsdp"),
        P("fsdp", None),
        P("fsdp"),
        P("fsdp", None),
        P("fsdp"),
        P(("fsdp", "dp"), None, None),
    )
    out_specs = (
        P(("fsdp", "dp"), None, None),
        P(("fsdp", "dp"), None, None),
        P("fsdp", None),
        P("fsdp"),
        P("fsdp", None),
        P("fsdp"),
        P("fsdp", None),
        P("fsdp"),
        P("fsdp", None),
        P("fsdp"),
        P("fsdp", None),
        P("fsdp"),
    )
    fits = (mesh.shape["fsdp"], mesh.shape["dp"]) == (16, 2)
    return jax.shard_map(
        one_kernel if fits else general_form, mesh=mesh, in_specs=in_specs, out_specs=out_specs, check_vma=False
    )
```

```python
import functools

import jax
import jax.numpy as jnp
from jax import lax
from jax.experimental import pallas as pl
from jax.experimental.pallas import tpu as pltpu
from jax.sharding import PartitionSpec as P

HEADS = 16
HEAD_DIM = 72


root_half = 0.7978845608028654
norm_eps = 1e-06
masked_score = -1e30


def gelu_tanh(stream):
    return (
        0.5 * stream * (1.0 + jnp.tanh(root_half * (stream + 0.044715 * stream * stream * stream)))
    )


def gelu_slope(stream):
    tanh_inner = jnp.tanh(root_half * (stream + 0.044715 * stream * stream * stream))
    return 0.5 * (1.0 + tanh_inner) + 0.5 * stream * (1.0 - tanh_inner * tanh_inner) * root_half * (
        1.0 + 3.0 * 0.044715 * stream * stream
    )


def normalize(stream):
    centre = jnp.mean(stream, axis=-1, keepdims=True)
    centred = stream - centre
    inv_std = lax.rsqrt(jnp.mean(centred * centred, axis=-1, keepdims=True) + norm_eps)
    return (centred * inv_std, inv_std)


def normalize_back(incoming, normed, inv_std):
    return inv_std * (
        incoming
        - jnp.mean(incoming, axis=-1, keepdims=True)
        - normed * jnp.mean(incoming * normed, axis=-1, keepdims=True)
    )


def head_scores(projected, same_doc, head_index, model_width):
    query_part = lax.dynamic_slice_in_dim(projected, head_index * HEAD_DIM, HEAD_DIM, 1)
    key_part = lax.dynamic_slice_in_dim(projected, model_width + head_index * HEAD_DIM, HEAD_DIM, 1)
    value_part = lax.dynamic_slice_in_dim(
        projected, 2 * model_width + head_index * HEAD_DIM, HEAD_DIM, 1
    )
    raw_scores = jnp.einsum(
        "qd,kd->qk", query_part, key_part, preferred_element_type=jnp.float32
    ) * HEAD_DIM ** (-0.5)
    return (jnp.where(same_doc, raw_scores, masked_score), query_part, key_part, value_part)


def merge_heads(stacked, model_width):
    return jnp.transpose(stacked, (1, 0, 2)).reshape(stacked.shape[1], model_width)


def attend_row(projected, segments_row, model_width):
    same_doc = segments_row[:, None] == segments_row[None, :]

    def one_head(head_index):
        scores, query_part, key_part, value_part = head_scores(
            projected, same_doc, head_index, model_width
        )
        top_score = jnp.max(scores, axis=-1, keepdims=True)
        exp_scores = jnp.exp(scores - top_score)
        denominator = jnp.sum(exp_scores, axis=-1, keepdims=True)
        probabilities = (exp_scores / denominator).astype(jnp.bfloat16)
        mixed_heads = jnp.dot(probabilities, value_part, preferred_element_type=jnp.float32)
        return (mixed_heads, (top_score + jnp.log(denominator))[:, 0])

    mixed_heads, log_total = lax.map(one_head, jnp.arange(HEADS))
    return (merge_heads(mixed_heads, model_width).astype(jnp.bfloat16), log_total)


def attend_back(projected, segments_row, log_total, d_mixed, model_width):
    same_doc = segments_row[:, None] == segments_row[None, :]
    head_scale = HEAD_DIM ** (-0.5)

    def one_head(head_index):
        scores, query_part, key_part, value_part = head_scores(
            projected, same_doc, head_index, model_width
        )
        d_head = lax.dynamic_slice_in_dim(d_mixed, head_index * HEAD_DIM, HEAD_DIM, 1)
        lse_row = lax.dynamic_index_in_dim(log_total, head_index, 0, keepdims=False)
        probabilities = jnp.exp(scores - lse_row[:, None])
        prob_low = probabilities.astype(jnp.bfloat16)
        d_probs = jnp.einsum("qd,kd->qk", d_head, value_part, preferred_element_type=jnp.float32)
        d_value = jnp.einsum("qk,qd->kd", prob_low, d_head, preferred_element_type=jnp.float32)
        d_scores = (
            probabilities * (d_probs - jnp.sum(d_probs * probabilities, axis=-1, keepdims=True))
        ).astype(jnp.bfloat16)
        d_query = (
            jnp.einsum("qk,kd->qd", d_scores, key_part, preferred_element_type=jnp.float32)
            * head_scale
        )
        d_key = (
            jnp.einsum("qk,qd->kd", d_scores, query_part, preferred_element_type=jnp.float32)
            * head_scale
        )
        return (d_query, d_key, d_value)

    d_query, d_key, d_value = lax.map(one_head, jnp.arange(HEADS))
    merged = [
        merge_heads(d_query, model_width),
        merge_heads(d_key, model_width),
        merge_heads(d_value, model_width),
    ]
    return jnp.concatenate(merged, axis=-1).astype(jnp.bfloat16)


def general_form(
    tokens,
    cond,
    segment_ids,
    ada_weight,
    ada_bias,
    qkv_weight,
    qv_bias,
    proj_weight,
    proj_bias,
    fc1_weight,
    fc1_bias,
    fc2_weight,
    fc2_bias,
    out_grad,
):
    row_count, seq_len, model_width = tokens.shape
    ff_width = fc1_weight.shape[1]
    stream = tokens.astype(jnp.float32)
    cond_float = cond.astype(jnp.float32)
    cond_act = (cond_float / (1.0 + jnp.exp(-cond_float))).astype(jnp.bfloat16)
    fsdp_at, dp_at = lax.axis_index("fsdp"), lax.axis_index("dp")
    dp_size = lax.axis_size("dp")
    slice_width, bias_width = ada_weight.shape[0], ada_bias.shape[0]
    act_all = lax.all_gather(cond_act, ("fsdp", "dp"), axis=0, tiled=True)
    act_mine = lax.dynamic_slice_in_dim(act_all, fsdp_at * slice_width, slice_width, 1)
    partial = jnp.dot(act_mine, ada_weight, preferred_element_type=jnp.float32)
    bias_row = lax.dynamic_update_slice_in_dim(
        jnp.zeros((6 * model_width,), jnp.float32),
        ada_bias.astype(jnp.float32),
        fsdp_at * bias_width,
        0,
    )
    partial = (partial + bias_row).reshape(-1, dp_size, row_count, 6 * model_width)
    partial = lax.dynamic_index_in_dim(partial, dp_at, 1, keepdims=False)
    modulation = lax.psum_scatter(
        partial.reshape(-1, 6 * model_width), "fsdp", scatter_dimension=0, tiled=True
    )
    pieces = [
        modulation[:, None, section * model_width : (section + 1) * model_width]
        for section in range(6)
    ]
    shift_one, scale_one, gate_one, shift_two, scale_two, gate_two = pieces
    qkv_full, qv_bias_full, proj_full, proj_bias_full = (
        lax.all_gather(qkv_weight, "fsdp", axis=0, tiled=True),
        lax.all_gather(qv_bias, "fsdp", axis=0, tiled=True),
        lax.all_gather(proj_weight, "fsdp", axis=0, tiled=True),
        lax.all_gather(proj_bias, "fsdp", axis=0, tiled=True),
    )
    normed_one, inv_one = normalize(stream)
    hidden_one = (normed_one * (1.0 + scale_one) + shift_one).astype(jnp.bfloat16)
    qv_float = qv_bias_full.astype(jnp.float32)
    qkv_bias = jnp.concatenate(
        [qv_float[:model_width], jnp.zeros((model_width,), jnp.float32), qv_float[model_width:]]
    )
    projected = (
        jnp.dot(hidden_one, qkv_full, preferred_element_type=jnp.float32) + qkv_bias
    ).astype(jnp.bfloat16)

    def row_forward(row_items):
        return attend_row(row_items[0], row_items[1], model_width)

    mixed_rows, log_total = lax.map(row_forward, (projected, segment_ids))
    branch_one = jnp.dot(
        mixed_rows, proj_full, preferred_element_type=jnp.float32
    ) + proj_bias_full.astype(jnp.float32)
    resid_one = stream + gate_one * branch_one
    fc1_full, fc1_bias_full, fc2_full, fc2_bias_full = (
        lax.all_gather(fc1_weight, "fsdp", axis=0, tiled=True),
        lax.all_gather(fc1_bias, "fsdp", axis=0, tiled=True),
        lax.all_gather(fc2_weight, "fsdp", axis=0, tiled=True),
        lax.all_gather(fc2_bias, "fsdp", axis=0, tiled=True),
    )
    normed_two, inv_two = normalize(resid_one)
    hidden_two = (normed_two * (1.0 + scale_two) + shift_two).astype(jnp.bfloat16)
    pre_act = jnp.dot(
        hidden_two, fc1_full, preferred_element_type=jnp.float32
    ) + fc1_bias_full.astype(jnp.float32)
    active = gelu_tanh(pre_act).astype(jnp.bfloat16)
    branch_two = jnp.dot(
        active, fc2_full, preferred_element_type=jnp.float32
    ) + fc2_bias_full.astype(jnp.float32)
    output = (resid_one + gate_two * branch_two).astype(jnp.bfloat16)
    d_out = out_grad.astype(jnp.float32)
    fc1_back, fc2_back = (
        lax.all_gather(fc1_weight, "fsdp", axis=0, tiled=True),
        lax.all_gather(fc2_weight, "fsdp", axis=0, tiled=True),
    )
    d_gate_two = jnp.sum(d_out * branch_two, axis=1)
    d_branch_two = (d_out * gate_two).astype(jnp.bfloat16)
    fc2_shard = lax.psum_scatter(
        jnp.einsum("rsf,rsd->fd", active, d_branch_two, preferred_element_type=jnp.float32).astype(
            jnp.bfloat16
        ),
        "fsdp",
        scatter_dimension=0,
        tiled=True,
    )
    grad_fc2_bias = jnp.sum(d_branch_two.astype(jnp.float32), axis=(0, 1))
    d_active = jnp.einsum("rsd,fd->rsf", d_branch_two, fc2_back, preferred_element_type=jnp.float32)
    d_pre = (d_active * gelu_slope(pre_act)).astype(jnp.bfloat16)
    grad_fc1_bias = jnp.sum(d_pre.astype(jnp.float32), axis=(0, 1))
    d_hidden_two = jnp.einsum("rsf,ef->rse", d_pre, fc1_back, preferred_element_type=jnp.float32)
    d_scale_two = jnp.sum(d_hidden_two * normed_two, axis=1)
    d_shift_two = jnp.sum(d_hidden_two, axis=1)
    d_resid = d_out + normalize_back(d_hidden_two * (1.0 + scale_two), normed_two, inv_two)
    qkv_back, proj_back = (
        lax.all_gather(qkv_weight, "fsdp", axis=0, tiled=True),
        lax.all_gather(proj_weight, "fsdp", axis=0, tiled=True),
    )
    d_gate_one = jnp.sum(d_resid * branch_one, axis=1)
    d_branch_one = (d_resid * gate_one).astype(jnp.bfloat16)
    grad_proj_bias = jnp.sum(d_branch_one.astype(jnp.float32), axis=(0, 1))
    d_mixed = jnp.einsum(
        "rsd,ed->rse", d_branch_one, proj_back, preferred_element_type=jnp.float32
    ).astype(jnp.bfloat16)

    def row_backward(row_items):
        return attend_back(row_items[0], row_items[1], row_items[2], row_items[3], model_width)

    d_projected = lax.map(row_backward, (projected, segment_ids, log_total, d_mixed))
    d_proj_float = d_projected.astype(jnp.float32)
    grad_qv_bias = jnp.concatenate(
        [
            jnp.sum(d_proj_float[..., :model_width], axis=(0, 1)),
            jnp.sum(d_proj_float[..., 2 * model_width :], axis=(0, 1)),
        ]
    )
    d_hidden_one = jnp.einsum(
        "rsf,ef->rse", d_projected, qkv_back, preferred_element_type=jnp.float32
    )
    d_scale_one = jnp.sum(d_hidden_one * normed_one, axis=1)
    d_shift_one = jnp.sum(d_hidden_one, axis=1)
    tokens_grad = (
        d_resid + normalize_back(d_hidden_one * (1.0 + scale_one), normed_one, inv_one)
    ).astype(jnp.bfloat16)
    d_modulation = jnp.concatenate(
        [d_shift_one, d_scale_one, d_gate_one, d_shift_two, d_scale_two, d_gate_two], axis=-1
    ).astype(jnp.bfloat16)
    d_mod_all = lax.all_gather(d_modulation, ("fsdp", "dp"), axis=0, tiled=True)
    grad_ada = jnp.einsum("rd,re->de", act_mine, d_mod_all, preferred_element_type=jnp.float32)
    grad_ada_bias = jnp.sum(
        lax.dynamic_slice_in_dim(d_mod_all, fsdp_at * bias_width, bias_width, 1).astype(jnp.float32),
        axis=0,
    )

    def owners(term):
        return lax.psum_scatter(
            term.astype(jnp.bfloat16), "fsdp", scatter_dimension=0, tiled=True
        )

    qkv_shard = owners(
        jnp.einsum("rse,rsf->ef", hidden_one, d_projected, preferred_element_type=jnp.float32)
    )
    proj_shard = owners(
        jnp.einsum("rse,rsd->ed", mixed_rows, d_branch_one, preferred_element_type=jnp.float32)
    )
    fc1_shard = owners(
        jnp.einsum("rse,rsf->ef", hidden_two, d_pre, preferred_element_type=jnp.float32)
    )
    bias_shards = (
        None,
        lax.psum_scatter(
            grad_qv_bias.astype(jnp.bfloat16), "fsdp", scatter_dimension=0, tiled=True
        ).astype(jnp.float32),
        lax.psum_scatter(
            grad_proj_bias.astype(jnp.bfloat16), "fsdp", scatter_dimension=0, tiled=True
        ).astype(jnp.float32),
        lax.psum_scatter(
            grad_fc1_bias.astype(jnp.bfloat16), "fsdp", scatter_dimension=0, tiled=True
        ).astype(jnp.float32),
        lax.psum_scatter(
            grad_fc2_bias.astype(jnp.bfloat16), "fsdp", scatter_dimension=0, tiled=True
        ).astype(jnp.float32),
    )
    summed = (
        grad_ada,
        grad_ada_bias,
        lax.psum(qkv_shard.astype(jnp.bfloat16), "dp").astype(jnp.float32),
        lax.psum(bias_shards[1].astype(jnp.bfloat16), "dp").astype(jnp.float32),
        lax.psum(proj_shard.astype(jnp.bfloat16), "dp").astype(jnp.float32),
        lax.psum(bias_shards[2].astype(jnp.bfloat16), "dp").astype(jnp.float32),
        lax.psum(fc1_shard.astype(jnp.bfloat16), "dp").astype(jnp.float32),
        lax.psum(bias_shards[3].astype(jnp.bfloat16), "dp").astype(jnp.float32),
        lax.psum(fc2_shard, "dp").astype(jnp.float32),
        lax.psum(bias_shards[4].astype(jnp.bfloat16), "dp").astype(jnp.float32),
    )
    return (
        output,
        tokens_grad,
        summed[0],
        summed[1],
        summed[2],
        summed[3],
        summed[4],
        summed[5],
        summed[6],
        summed[7],
        summed[8],
        summed[9],
    )


MESH_ID = pl.DeviceIdType.MESH
f32 = jnp.float32
bf16 = jnp.bfloat16

SEQ = 256
WIDTH = 1152
HIDDEN = 4608
PART = 1152
QKV = 864
PAD = 128
LOCAL = 4


def dot_nn(left, right):
    return lax.dot_general(left, right, (((1,), (0,)), ((), ())), preferred_element_type=f32)


def dot_nt(left, right):
    return lax.dot_general(left, right, (((1,), (1,)), ((), ())), preferred_element_type=f32)


def dot_tn(left, right):
    return lax.dot_general(left, right, (((0,), (0,)), ((), ())), preferred_element_type=f32)


def iota(shape, axis):
    return lax.broadcasted_iota(jnp.int32, shape, axis)


def whole_part(value, divisor):
    return jnp.floor((value + 0.5) * (1.0 / divisor))


class Ids:
    def __init__(self):
        self.used = 0

    def take(self, count):
        start = self.used
        self.used += count
        return start


IDS = Ids()
IDS.small_y, IDS.small_z, IDS.small_c = IDS.take(1), IDS.take(6), IDS.take(1)
IDS.small_x, IDS.small_d = IDS.take(1), IDS.take(1)
IDS.mod_c, IDS.mod_y, IDS.mod_z = IDS.take(1), IDS.take(1), IDS.take(3)
IDS.core = [IDS.take(1) for _ in range(3)]
IDS.z = [IDS.take(3) for _ in range(4)]
IDS.y = [IDS.take(4) for _ in range(4)]
IDS.pass_on = [IDS.take(5) for _ in range(4)]
IDS.h1, IDS.h2, IDS.d2, IDS.d1 = IDS.take(3), IDS.take(3), IDS.take(3), IDS.take(3)
IDS.r1, IDS.r2, IDS.r3, IDS.r4 = IDS.take(3), IDS.take(3), IDS.take(3), IDS.take(3)
IDS.gy = [IDS.take(4) for _ in range(4)]
IDS.gz = [IDS.take(3) for _ in range(4)]
IDS.gf = [IDS.take(3) for _ in range(4)]
IDS.end_y, IDS.end_z, IDS.end_x, IDS.end_c = IDS.take(1), IDS.take(6), IDS.take(1), IDS.take(1)
ID_COUNT = IDS.used

SCRATCH = (
    ((32, 8, 384), f32),
    ((16, 8, WIDTH), f32),
    ((8, 8, WIDTH), f32),
    ((4, 8, WIDTH), f32),
    ((3, 8, WIDTH), f32),
    ((8, WIDTH), f32),
    ((72, WIDTH), bf16),
    ((72, QKV), bf16),
    ((72, PART), bf16),
    ((72, WIDTH), bf16),
    ((WIDTH, QKV), bf16),
    ((WIDTH, PART), bf16),
    ((PART, WIDTH), bf16),
    ((4, 72, WIDTH), bf16),
    ((288, WIDTH), bf16),
    ((1024, WIDTH), bf16),
    ((1024, WIDTH), bf16),
    ((1024, WIDTH), bf16),
    ((1024, 12 * PAD), bf16),
    ((16, SEQ, SEQ), bf16),
    ((1024, 288), bf16),
    ((1024, PART), bf16),
    ((1024, PART), bf16),
    ((1024, QKV), bf16),
    ((3, SEQ, WIDTH), bf16),
    ((3, SEQ, WIDTH), bf16),
    ((SEQ, WIDTH), bf16),
    ((SEQ, WIDTH), bf16),
    ((SEQ, WIDTH), bf16),
    ((SEQ, WIDTH), f32),
    ((SEQ, WIDTH), f32),
    ((SEQ, WIDTH), f32),
    ((SEQ, WIDTH), f32),
    ((16, WIDTH), f32),
    ((8, WIDTH), f32),
    ((WIDTH, QKV), bf16),
    ((WIDTH, PART), bf16),
    ((PART, WIDTH), bf16),
    ((4, 72, WIDTH), bf16),
    ((4, 144, QKV), bf16),
    ((4, 144, PART), bf16),
    ((4, 144, WIDTH), bf16),
    ((4, 72, WIDTH), bf16),
    ((3, 144, QKV), bf16),
    ((3, 144, PART), bf16),
    ((3, 144, WIDTH), bf16),
    ((3, 72, WIDTH), bf16),
    ((72, QKV), bf16),
    ((72, PART), bf16),
    ((72, WIDTH), bf16),
    ((72, QKV), bf16),
    ((72, PART), bf16),
    ((72, WIDTH), bf16),
    ((4, 72, QKV), bf16),
    ((4, 72, PART), bf16),
    ((4, 72, WIDTH), bf16),
    ((72, WIDTH), bf16),
    ((32, 16, WIDTH), bf16),
)


def block_kernel(
    tok, og, small, ada, adab, wqkv, wproj, wfc1, wfc2, out,
    tgrad, oada, oqkv, oproj, ofc1, ofc2, osum, S, modp, modc,
    mody, modz, mod, own_fc2, xr_qkv, xr_fc1, xr_fc2, G_qkv,
    G_fc1, G_fc2, G_proj, W_proj, H1, H2, D2, qp, P, mixed,
    active, slope, dprj, rrA, rrB, sA, sB, sX, keep, own,
    b1, resid, acc, bias, g_qkv, g_fc1, g_fc2, g_proj, yr_qkv, yr_fc1,
    yr_fc2, yr_proj, zr_qkv, zr_fc1, zr_fc2, zr_proj, fa_qkv, fa_fc1, fa_fc2, fb_qkv,
    fb_fc1, fb_fc2, fr_qkv, fr_fc1, fr_fc2, p_out, E, snd, rcv, loc,
):
    xr_w, G_w = (xr_qkv, xr_fc1, xr_fc2), (G_qkv, G_fc1, G_fc2)
    yr_w, zr_w = (yr_qkv, yr_fc1, yr_fc2), (zr_qkv, zr_fc1, zr_fc2)
    fa_w, fb_w, fr_w = (fa_qkv, fa_fc1, fa_fc2), (fb_qkv, fb_fc1, fb_fc2), (fr_qkv, fr_fc1, fr_fc2)
    f = lax.axis_index("fsdp")
    x = lax.axis_index("dp")
    z = lax.div(f, 4)
    y = lax.rem(lax.div(f, 2), 2)
    c = lax.rem(f, 2)
    q = 2 * x + c
    qp_, qx_, qd_ = 2 * x + 1 - c, 2 * (1 - x) + c, 2 * (1 - x) + 1 - c

    def dev(zz, yy, cc, xx):
        return ((zz * 2 + yy) * 2 + cc, xx)

    mate, xnb, diag, ynb = dev(z, y, 1 - c, x), dev(z, y, c, 1 - x), dev(z, y, 1 - c, 1 - x), dev(z, 1 - y, c, x)

    def z_to(k):
        return lax.rem(z + k, 4)

    def z_from(k):
        return lax.rem(z + 4 - k, 4)

    def znb(k):
        return dev(z_to(k), y, c, x)

    def rc(src, dst, ident, to):
        return pltpu.make_async_remote_copy(
            src_ref=src, dst_ref=dst, send_sem=snd.at[ident], recv_sem=rcv.at[ident],
            device_id=to, device_id_type=MESH_ID,
        )

    pending = []

    def send(src, dst, ident, to):
        rc(src, dst, ident, to).start()
        pending.append((src, ident, to))

    def got(dst, ident):
        rc(dst, dst, ident, mate).wait_recv()

    def sent(src, ident):
        rc(src, src, ident, mate).wait_send()

    def settle(first):
        keep_on = []
        for item in pending:
            if item[1] in first:
                sent(item[0], item[1])
            else:
                keep_on.append(item)
        pending[:] = keep_on

    barrier = pltpu.get_barrier_semaphore()
    neighbours = [mate, xnb, diag, ynb, znb(1), znb(2), znb(3)]
    for to in neighbours:
        pl.semaphore_signal(barrier, inc=1, device_id=to, device_id_type=MESH_ID)
    pl.semaphore_wait(barrier, len(neighbours))


    def slot_of(cc, xx, yy, zz):
        return ((cc * 2 + xx) * 2 + yy) * 4 + zz

    my_slot = slot_of(c, x, y, z)
    send(small, S.at[my_slot], IDS.small_y, ynb)
    own_copy = pltpu.make_async_copy(wfc2.at[q], own_fc2, loc.at[0])
    own_copy.start()
    send(wfc2.at[qp_], xr_fc2, IDS.core[2], mate)

    def split_qkv():
        for at in range(4):
            fr_qkv[at] = jnp.concatenate(
                [wqkv[:, (4 * step + at) * 72 : (4 * step + at + 1) * 72] for step in range(12)], axis=1
            )
        send(fr_qkv.at[qp_], xr_qkv, IDS.core[0], mate)

    def split_fc1():
        for at in range(4):
            fr_fc1[at] = jnp.concatenate(
                [wfc1[:, (4 * step + at) * 72 : (4 * step + at + 1) * 72] for step in range(16)], axis=1
            )
        send(fr_fc1.at[qp_], xr_fc1, IDS.core[1], mate)

    split_qkv()
    S[my_slot] = small[...]
    acc[...] = jnp.zeros((16, WIDTH), f32)
    in_column = y == x
    proj_copy = pltpu.make_async_copy(wproj, G_proj.at[z], loc.at[1])

    def chip_rows(zz, yy):
        return pl.ds(pl.multiple_of((2 * zz + yy) * 144, 16), 144)

    def own_part(kind):
        return G_w[kind].at[chip_rows(z, y), :]

    def assemble(kind):
        got(xr_w[kind], IDS.core[kind])
        mine = (own_fc2[...] if kind == 2 else fr_w[kind][q]).astype(f32)
        other = xr_w[kind][...].astype(f32)
        low = jnp.where(c == 0, mine, other)
        high = jnp.where(c == 0, other, mine)
        G_w[kind][chip_rows(z, y), :] = jnp.concatenate([low, high], axis=0).astype(bf16)

    def own_y(kind):
        send(own_part(kind), own_part(kind), IDS.y[kind], ynb)

    inner = (z == 1) | (z == 2)
    relays = []

    def relay(wanted, part, source, ident, send_ident, to):
        @pl.when(wanted)
        def _():
            pltpu.make_async_remote_copy(
                src_ref=source, dst_ref=part, send_sem=snd.at[send_ident], recv_sem=rcv.at[ident],
                device_id=to, device_id_type=MESH_ID,
            ).start()

        relays.append((wanted, part, send_ident))

    def own_z(kind):
        part = own_part(kind)
        relay(z < 3, part, part, IDS.z[kind], IDS.pass_on[kind], znb(1))
        relay(z > 0, part, part, IDS.z[kind] + 2, IDS.pass_on[kind] + 1, znb(3))

    STEPS = (1, 3, 2)

    def near(j):
        middle = STEPS[j]
        return jnp.where(z == 0, 3 - j, jnp.where(z == 3, 1 + j, middle))

    def onward(k):
        return lax.rem(z + jnp.where(k <= z, 1, 3), 4), jnp.where(k <= z, k, k - 2)

    def forward(kind, j):
        k = near(j)
        part = G_w[kind].at[chip_rows(z_from(k), y), :]
        got(part, IDS.z[kind] + k - 1)
        where, at = onward(k)
        relay(inner, part, part, IDS.z[kind] + at, IDS.pass_on[kind] + 2 + j, dev(where, y, c, x))
        send(part, part, IDS.y[kind] + 1 + j, ynb)

    def arrived(kind):
        other = 1 - y
        got(G_w[kind].at[chip_rows(z, other), :], IDS.y[kind])
        for j in range(3):
            got(G_w[kind].at[chip_rows(z_from(near(j)), other), :], IDS.y[kind] + 1 + j)

    def proj_z():
        @pl.when(in_column)
        def _():
            proj_copy.start()

        part = G_proj.at[z]
        relay(in_column & (z < 3), part, wproj, IDS.z[3], IDS.pass_on[3], znb(1))
        relay(in_column & (z > 0), part, wproj, IDS.z[3] + 2, IDS.pass_on[3] + 1, znb(3))

    def proj_y():
        @pl.when(in_column)
        def _():
            rc(wproj, G_proj.at[z], IDS.y[3], ynb).start()

    def proj_forward(j):
        k = near(j)
        part = G_proj.at[z_from(k)]

        @pl.when(in_column)
        def _():
            got(part, IDS.z[3] + k - 1)
            rc(part, part, IDS.y[3] + 1 + j, ynb).start()

        where, at = onward(k)
        relay(in_column & inner, part, part, IDS.z[3] + at, IDS.pass_on[3] + 2 + j, dev(where, y, c, x))

    def proj_arrived():
        @pl.when(in_column)
        def _():
            proj_copy.wait()
            sent(wproj, IDS.y[3])
            for j in range(3):
                sent(G_proj.at[z_from(near(j))], IDS.y[3] + 1 + j)

        @pl.when(jnp.logical_not(in_column))
        def _():
            got(G_proj.at[z], IDS.y[3])
            for j in range(3):
                got(G_proj.at[z_from(near(j))], IDS.y[3] + 1 + j)

        W_proj[...] = jnp.concatenate(
            [G_proj[head].astype(f32) for head in range(LOCAL)], axis=0
        ).astype(bf16)

    got(S.at[slot_of(c, x, 1 - y, z)], IDS.small_y)
    for k in (2, 1, 3):
        for yy in range(2):
            part = S.at[slot_of(c, x, yy, z)]
            send(part, part, IDS.small_z + 2 * (k - 1) + yy, znb(k))
    assemble(0)
    own_y(0)
    own_z(0)
    for k in (1, 2, 3):
        for yy in range(2):
            got(S.at[slot_of(c, x, yy, z_from(k))], IDS.small_z + 2 * (k - 1) + yy)
    eight = lambda cc, xx: S.at[pl.ds((cc * 2 + xx) * 8, 8)]
    send(eight(c, x), eight(c, x), IDS.small_c, mate)
    send(eight(c, x), eight(c, x), IDS.small_x, xnb)

    def pick_columns(rows):
        total = None
        for piece in range(3):
            kk = iota((384, PAD), 0) + piece * 384
            jj = iota((384, PAD), 1)
            chosen = ((kk == 72 * f + jj) & (jj < 72)).astype(f32).astype(bf16)
            term = dot_nn(rows(piece), chosen)
            total = term if total is None else total + term
        return total.astype(bf16)

    got(eight(1 - c, x), IDS.small_c)
    act = pick_columns(
        lambda piece: jnp.concatenate(
            [S[pl.ds((cc * 2 + x) * 8, 8), piece, :] for cc in range(2)], axis=0
        ).astype(bf16)
    )[:, :72]
    for section in range(6):
        modp[:, section, :] = dot_nn(
            act, ada[:, section * WIDTH : (section + 1) * WIDTH]
        ) + adab[section : section + 1, :]
    for section in (6, 7):
        modp[:, section, :] = jnp.zeros((16, WIDTH), f32)
    theirs, ours = modp.at[pl.ds((1 - c) * 8, 8)], modp.at[pl.ds(c * 8, 8)]
    send(theirs, modc, IDS.mod_c, mate)
    split_fc1()
    got(modc, IDS.mod_c)
    for at in range(8):
        ours[at] += modc[at]
    send(modp.at[pl.ds(c * 8 + (1 - y) * 4, 4)], mody, IDS.mod_y, ynb)
    forward(0, 0)
    own_copy.wait()
    assemble(1)
    got(mody, IDS.mod_y)
    base = c * 8 + y * 4
    for at in range(4):
        modp[base + at] += mody[at]
    for k in (2, 1, 3):
        send(modp.at[base + z_to(k)], modz.at[k - 1], IDS.mod_z + k - 1, znb(k))
    forward(0, 1)
    proj_z()
    own_z(1)
    assemble(2)
    proj_y()
    own_y(1)
    got(eight(c, 1 - x), IDS.small_x)
    send(eight(c, 1 - x), eight(c, 1 - x), IDS.small_d, mate)

    def place(row, width, lane_of, owner_of):
        kk = iota((384, width), 1).astype(f32)
        jj = iota((384, width), 0).astype(f32)
        chosen = (jj == lane_of(kk)).astype(f32).astype(bf16)
        spread = dot_nn(row.astype(bf16), chosen)
        at = iota((16, width), 0)
        slot_f = ((lax.rem(at, 4) * 2 + lax.rem(lax.div(at, 4), 2)) * 2 + lax.div(at, 8)).astype(f32)
        mine = slot_f == owner_of(iota((16, width), 1).astype(f32))
        return jnp.sum(jnp.where(mine, spread, 0.0), axis=0, keepdims=True)

    def plane(piece):
        return jnp.concatenate([S[pl.ds((cc * 2 + x) * 8, 8), piece, :] for cc in range(2)], axis=0)

    def mod72(kk):
        return kk - 72.0 * whole_part(kk, 72)

    by72 = lambda kk: whole_part(kk, 72)
    qf, xf, cf = q.astype(f32), x.astype(f32), c.astype(f32)
    row3, row4 = plane(3), plane(4)
    bias[0:1, :] = place(row3, WIDTH, lambda kk: 144.0 + mod72(kk), by72)
    bias[1:2, :] = place(row3, WIDTH, lambda kk: 216.0 + mod72(kk), by72)
    bias[2:3, :] = place(row4, WIDTH, lambda kk: 72.0 * qf + mod72(kk), by72)

    def qkv_owner(kk):
        third = whole_part(kk, 288)
        head = whole_part(kk - 288.0 * third, 72)
        owner = 2.0 * head + xf + 4.0 * third
        return jnp.where((third == 1.0) | (third > 2.5), -1.0, owner)

    bias[3:4, :] = place(row3, WIDTH, lambda kk: 72.0 * cf + mod72(kk), qkv_owner)

    for k in (1, 2, 3):
        got(modz.at[k - 1], IDS.mod_z + k - 1)
    mod[...] = modp[base + z] + modz[0] + modz[1] + modz[2]

    def row_of(section):
        return mod[section : section + 1, :]

    def slot_rows(slot):
        return pl.ds(pl.multiple_of(slot * SEQ, SEQ), SEQ)

    TILE = 64

    def tiles(body):
        def step(at, carry):
            body(pl.multiple_of(at * TILE, TILE))
            return carry

        lax.fori_loop(0, SEQ // TILE, step, 0)


    def norm_one(at):
        normed, _ = normalize(tok[pl.ds(at, TILE), :].astype(f32))
        H1[pl.ds(pl.multiple_of(q * SEQ + at, TILE), TILE), :] = (
            normed * (1.0 + row_of(1)) + row_of(0)
        ).astype(bf16)

    tiles(norm_one)

    def spread_start(buf, ident):
        part = buf.at[slot_rows(q), :]
        send(part, part, ident, mate)
        send(part, part, ident + 1, xnb)

    def spread_mid(buf, ident):
        part = buf.at[slot_rows(qx_), :]
        got(part, ident + 1)
        send(part, part, ident + 2, mate)

    def spread_mate(buf, ident):
        got(buf.at[slot_rows(qp_), :], ident)

    def spread_end(buf, ident):
        got(buf.at[slot_rows(qd_), :], ident + 2)

    spread_start(H1, IDS.h1)
    settle(tuple(IDS.core))

    def add_row(at, value):
        acc[at : at + 1, :] += jnp.sum(value, axis=0, keepdims=True)

    def out_gate(at):
        low = (og[pl.ds(at, TILE), :].astype(f32) * row_of(5)).astype(bf16)
        D2[pl.ds(pl.multiple_of(q * SEQ + at, TILE), TILE), :] = low
        add_row(6, low.astype(f32))

    tiles(out_gate)
    spread_start(D2, IDS.d2)
    spread_mate(H1, IDS.h1)
    forward(0, 2)
    spread_mid(H1, IDS.h1)
    arrived(0)


    def project(slot):
        rows = slot_rows(slot)
        value = (dot_nn(H1[rows, :], G_qkv[...]) + bias[3:4, :QKV]).astype(bf16)
        blank = jnp.zeros((SEQ, PAD - HEAD_DIM), bf16)
        for at in range(12):
            qp[rows, at * PAD : (at + 1) * PAD] = jnp.concatenate(
                [value[:, at * HEAD_DIM : (at + 1) * HEAD_DIM], blank], axis=1
            )

    def attend(slot):
        rows = slot_rows(slot)
        where_seg = slot_of(lax.rem(slot, 2), lax.div(slot, 2), y, z)
        seg = S[where_seg, 5:6, :SEQ]
        seg_column = jnp.transpose(jnp.broadcast_to(seg, (8, SEQ)))[:, :1]
        same = seg_column == seg
        pieces = []
        for head in range(LOCAL):
            query = qp[rows, head * PAD : (head + 1) * PAD]
            key = qp[rows, (LOCAL + head) * PAD : (LOCAL + head + 1) * PAD]
            value = qp[rows, (2 * LOCAL + head) * PAD : (2 * LOCAL + head + 1) * PAD]
            scores = jnp.where(same, dot_nt(query, key) * HEAD_DIM ** (-0.5), masked_score)
            exp_scores = jnp.exp(scores - jnp.max(scores, axis=1, keepdims=True))
            probs = (exp_scores / jnp.sum(exp_scores, axis=1, keepdims=True)).astype(bf16)
            P[slot * LOCAL + head] = probs
            pieces.append(dot_nn(probs, value).astype(bf16)[:, :HEAD_DIM])
        mixed[rows, :] = jnp.concatenate(pieces, axis=1)

    def pair(body, group):
        def step(at, carry):
            body(2 * group + lax.rem(c + at, 2))
            return carry

        lax.fori_loop(0, 2, step, 0)

    got(eight(1 - c, 1 - x), IDS.small_d)
    proj_forward(0)
    pair(project, x)
    forward(1, 0)
    proj_forward(1)
    pair(attend, x)
    forward(1, 1)
    proj_forward(2)
    own_z(2)
    spread_end(H1, IDS.h1)
    pair(project, 1 - x)
    forward(1, 2)
    pair(attend, 1 - x)
    spread_mate(D2, IDS.d2)
    spread_mid(D2, IDS.d2)


    def reduce_first(partial, rr, ident):
        sA[...] = partial(qd_).astype(bf16)
        send(sA, rr.at[0], ident, mate)
        keep[...] = partial(qx_)
        sB[...] = partial(qp_).astype(bf16)

    def reduce_next(partial, rr, ident):
        got(rr.at[0], ident)
        sX[...] = (keep[...] + rr[0].astype(f32)).astype(bf16)
        send(sX, rr.at[2], ident + 2, xnb)
        send(sB, rr.at[1], ident + 1, mate)
        own[...] = partial(q)

    def reduce_last(rr, ident):
        got(rr.at[1], ident + 1)
        got(rr.at[2], ident + 2)
        settle((ident, ident + 1, ident + 2))

    def total_rows(rr, at):
        rows = pl.ds(at, TILE)
        return own[rows, :] + rr[1, rows, :].astype(f32) + rr[2, rows, :].astype(f32)

    proj_arrived()

    def part_one(slot):
        return dot_nn(mixed[slot_rows(slot), :], W_proj[...])

    reduce_first(part_one, rrA, IDS.r1)
    reduce_next(part_one, rrA, IDS.r1)
    own_y(2)
    forward(2, 0)
    reduce_last(rrA, IDS.r1)


    def norm_two(at):
        rows = pl.ds(at, TILE)
        branch = total_rows(rrA, at) + bias[0:1, :]
        b1[rows, :] = branch
        stream = tok[rows, :].astype(f32) + row_of(2) * branch
        resid[rows, :] = stream
        normed, _ = normalize(stream)
        H2[pl.ds(pl.multiple_of(q * SEQ + at, TILE), TILE), :] = (
            normed * (1.0 + row_of(4)) + row_of(3)
        ).astype(bf16)

    tiles(norm_two)
    spread_start(H2, IDS.h2)
    forward(2, 1)
    spread_end(D2, IDS.d2)
    spread_mate(H2, IDS.h2)
    spread_mid(H2, IDS.h2)
    arrived(1)

    CHUNK = 384

    def first_layer(slot):
        rows = slot_rows(slot)
        for at in range(0, PART, CHUNK):
            pre = dot_nn(H2[rows, :], G_fc1[:, at : at + CHUNK]) + bias[2:3, at : at + CHUNK]
            square = pre * pre
            bend = jnp.tanh(root_half * (pre + 0.044715 * square * pre))
            active[rows, at : at + CHUNK] = (0.5 * pre * (1.0 + bend)).astype(bf16)
            slope[rows, at : at + CHUNK] = (
                0.5 * (1.0 + bend)
                + 0.5 * pre * (1.0 - bend * bend) * root_half * (1.0 + 3.0 * 0.044715 * square)
            ).astype(bf16)

    pair(first_layer, x)
    forward(2, 2)
    spread_end(H2, IDS.h2)
    pair(first_layer, 1 - x)

    def cross(left, right, dest, width):
        def step(at, carry):
            part = pl.ds(pl.multiple_of(at * CHUNK, CHUNK), CHUNK)
            dest[part, :] = dot_tn(left[:, part], right[...]).astype(bf16)
            return carry

        lax.fori_loop(0, width // CHUNK, step, 0)

    cross(active, D2, g_fc2, PART)

    def grad_start(kind, grads, steps):
        for k in steps:
            send(
                grads.at[chip_rows(z_to(k), 1 - y), :], yr_w[kind].at[k], IDS.gy[kind] + k, ynb
            )

    def add_block(grads, rows_at, extra):
        def step(at, carry):
            rows = pl.ds(pl.multiple_of(rows_at + at * 48, 16), 48)
            grads[rows, :] = (
                grads[rows, :].astype(f32) + extra[pl.ds(pl.multiple_of(at * 48, 16), 48), :].astype(f32)
            ).astype(bf16)
            return carry

        lax.fori_loop(0, 3, step, 0)

    def grad_mid(kind, grads, k):
        zz = z_to(k)
        got(yr_w[kind].at[k], IDS.gy[kind] + k)
        add_block(grads, (2 * zz + y) * 144, yr_w[kind].at[k])
        send(
            grads.at[chip_rows(zz, y), :], zr_w[kind].at[k - 1], IDS.gz[kind] + k - 1, znb(k)
        )

    def grad_end(kind, grads):
        got(yr_w[kind].at[0], IDS.gy[kind])
        for k in (1, 2, 3):
            got(zr_w[kind].at[k - 1], IDS.gz[kind] + k - 1)
        width = grads.shape[1]
        A, B, fr = fa_w[kind], fb_w[kind], fr_w[kind]
        for at in range(0, width, CHUNK):
            cols = slice(at, min(at + CHUNK, width))
            total = grads[chip_rows(z, y), cols].astype(f32) + yr_w[kind][0, :, cols].astype(f32)
            for k in range(3):
                total = total + zr_w[kind][k, :, cols].astype(f32)
            low, high = total[:72], total[72:]
            mine = jnp.where(c == 0, low, high).astype(bf16)
            A[:, cols] = mine
            B[:, cols] = jnp.where(c == 0, high, low).astype(bf16)
            fr[q, :, cols] = mine
        send(B, fr.at[q], IDS.gf[kind], mate)
        send(A, fr.at[q], IDS.gf[kind] + 1, xnb)
        send(B, fr.at[q], IDS.gf[kind] + 2, diag)

    slots = [area.at[72 * at : 72 * (at + 1), :] for area in (resid, b1, keep, own) for at in range(3)]
    out_copies = []

    def leave(value, target):
        at = len(out_copies)
        if at >= len(slots):
            out_copies[at - len(slots)].wait()
        slots[at % len(slots)][...] = value
        copy = pltpu.make_async_copy(slots[at % len(slots)], target, loc.at[2 + at])
        copy.start()
        out_copies.append(copy)

    def columns_of(ref, piece):
        return ref.at[:, piece * WIDTH : (piece + 1) * WIDTH]

    def grad_out(kind):
        fr = fr_w[kind]
        for step, source in enumerate((qp_, qx_, qd_)):
            got(fr.at[source], IDS.gf[kind] + step)
        if kind == 2:
            for at in range(4):
                leave(fr[at].astype(f32), ofc2.at[at])
            return
        for piece in range(3 if kind == 0 else 4):
            leave(
                jnp.concatenate(
                    [
                        fr[at, :, (4 * piece + step) * 72 : (4 * piece + step + 1) * 72]
                        for step in range(4)
                        for at in range(4)
                    ],
                    axis=1,
                ).astype(f32),
                columns_of(oqkv if kind == 0 else ofc1, piece),
            )

    grad_start(2, g_fc2, (2, 1, 3, 0))
    arrived(2)

    def back_hidden(slot):
        rows = slot_rows(slot)
        for at in range(0, PART, CHUNK):
            low = (
                dot_nt(D2[rows, :], G_fc2[at : at + CHUNK, :])
                * slope[rows, at : at + CHUNK].astype(f32)
            ).astype(bf16)
            slope[rows, at : at + CHUNK] = low
            acc[8:9, at : at + CHUNK] += jnp.sum(low.astype(f32), axis=0, keepdims=True)

    pair(back_hidden, x)
    pair(back_hidden, 1 - x)
    d_pre = slope
    settle(tuple(IDS.d2 + step for step in range(3)))
    D1 = D2
    def part_three(slot):
        return dot_nt(d_pre[slot_rows(slot), :], G_fc1[...])

    reduce_first(part_three, rrA, IDS.r3)
    reduce_next(part_three, rrA, IDS.r3)
    cross(H2, d_pre, g_fc1, WIDTH)
    grad_start(1, g_fc1, (2, 1, 3, 0))
    grad_mid(2, g_fc2, 2)
    reduce_last(rrA, IDS.r3)

    def back_two(at):
        rows = pl.ds(at, TILE)
        d_hidden = total_rows(rrA, at)
        normed, inv = normalize(resid[rows, :])
        add_row(3, d_hidden)
        add_row(4, d_hidden * normed)
        d_resid = og[rows, :].astype(f32) + normalize_back(d_hidden * (1.0 + row_of(4)), normed, inv)
        add_row(2, d_resid * b1[rows, :])
        low = (d_resid * row_of(2)).astype(bf16)
        add_row(7, low.astype(f32))
        D1[pl.ds(pl.multiple_of(q * SEQ + at, TILE), TILE), :] = low
        b1[rows, :] = d_resid

    tiles(back_two)
    spread_start(D1, IDS.d1)

    def part_two(slot):
        return dot_nn(active[slot_rows(slot), :], G_fc2[...])

    reduce_first(part_two, rrB, IDS.r2)
    reduce_next(part_two, rrB, IDS.r2)

    def finish_forward(at):
        rows = pl.ds(at, TILE)
        branch = total_rows(rrB, at) + bias[1:2, :]
        rrB[0, rows, :] = (resid[rows, :] + row_of(5) * branch).astype(bf16)
        add_row(5, og[rows, :].astype(f32) * branch)

    grad_mid(2, g_fc2, 1)
    spread_mate(D1, IDS.d1)


    def attend_backward(slot):
        rows = slot_rows(slot)
        d_mix = dot_nt(D1[rows, :], W_proj[...]).astype(bf16)
        blank = jnp.zeros((SEQ, PAD - HEAD_DIM), bf16)
        scale = HEAD_DIM ** (-0.5)
        d_query, d_key, d_value = [], [], []
        for head in range(LOCAL):
            query = qp[rows, head * PAD : (head + 1) * PAD]
            key = qp[rows, (LOCAL + head) * PAD : (LOCAL + head + 1) * PAD]
            value = qp[rows, (2 * LOCAL + head) * PAD : (2 * LOCAL + head + 1) * PAD]
            d_head = jnp.concatenate([d_mix[:, head * HEAD_DIM : (head + 1) * HEAD_DIM], blank], axis=1)
            probs = P[slot * LOCAL + head]
            d_probs = dot_nt(d_head, value)
            d_value.append(dot_tn(probs, d_head).astype(bf16)[:, :HEAD_DIM])
            wide = probs.astype(f32)
            d_scores = (wide * (d_probs - jnp.sum(d_probs * wide, axis=1, keepdims=True))).astype(bf16)
            d_query.append((dot_nn(d_scores, key) * scale).astype(bf16)[:, :HEAD_DIM])
            d_key.append((dot_tn(d_scores, query) * scale).astype(bf16)[:, :HEAD_DIM])
        value = jnp.concatenate(d_query + d_key + d_value, axis=1)
        dprj[rows, :] = value
        acc[9:10, :QKV] += jnp.sum(value.astype(f32), axis=0, keepdims=True)

    pair(attend_backward, x)
    spread_mid(D1, IDS.d1)
    grad_mid(2, g_fc2, 3)
    grad_mid(1, g_fc1, 2)
    spread_end(D1, IDS.d1)
    pair(attend_backward, 1 - x)
    grad_mid(1, g_fc1, 1)
    cross(H1, dprj, g_qkv, WIDTH)
    grad_start(0, g_qkv, (2, 1, 3, 0))

    def part_four(slot):
        return dot_nt(dprj[slot_rows(slot), :], G_qkv[...])

    settle((IDS.r2, IDS.r2 + 1))
    reduce_first(part_four, rrA, IDS.r4)
    grad_mid(1, g_fc1, 3)
    reduce_last(rrB, IDS.r2)
    tiles(finish_forward)
    row_copies = [pltpu.make_async_copy(rrB.at[0], out, loc.at[20])]
    row_copies[0].start()
    reduce_next(part_four, rrA, IDS.r4)
    proj_grads = dot_tn(mixed[...], D1[...])
    for head in range(LOCAL):
        g_proj[head] = proj_grads[head * 72 : (head + 1) * 72].astype(bf16)
    grad_mid(0, g_qkv, 2)
    grad_end(2, g_fc2)
    grad_mid(0, g_qkv, 1)
    reduce_last(rrA, IDS.r4)

    def back_one(at):
        rows = pl.ds(at, TILE)
        d_hidden = total_rows(rrA, at)
        normed, inv = normalize(tok[rows, :].astype(f32))
        add_row(0, d_hidden)
        add_row(1, d_hidden * normed)
        sA[rows, :] = (
            b1[rows, :] + normalize_back(d_hidden * (1.0 + row_of(1)), normed, inv)
        ).astype(bf16)

    tiles(back_one)
    row_copies.append(pltpu.make_async_copy(sA, tgrad, loc.at[21]))
    row_copies[1].start()

    E[my_slot] = acc[...].astype(bf16)
    send(E.at[my_slot], E.at[my_slot], IDS.end_y, ynb)

    @pl.when(jnp.logical_not(in_column))
    def _():
        for k in range(4):
            rc(g_proj.at[z_to(k)], yr_proj.at[k], IDS.gy[3] + k, ynb).start()

    grad_mid(0, g_qkv, 3)
    grad_end(1, g_fc1)
    got(E.at[slot_of(c, x, 1 - y, z)], IDS.end_y)
    for k in (2, 1, 3):
        for yy in range(2):
            part = E.at[slot_of(c, x, yy, z)]
            send(part, part, IDS.end_z + 2 * (k - 1) + yy, znb(k))

    @pl.when(in_column)
    def _():
        for k in STEPS:
            zz = z_to(k)
            got(yr_proj.at[k], IDS.gy[3] + k)
            g_proj[zz] = (g_proj[zz].astype(f32) + yr_proj[k].astype(f32)).astype(bf16)
            rc(g_proj.at[zz], zr_proj.at[k - 1], IDS.gz[3] + k - 1, znb(k)).start()

    grad_out(2)
    for k in (1, 2, 3):
        for yy in range(2):
            got(E.at[slot_of(c, x, yy, z_from(k))], IDS.end_z + 2 * (k - 1) + yy)
    group = lambda cc, xx: E.at[pl.ds((cc * 2 + xx) * 8, 8)]
    send(group(c, x), group(c, x), IDS.end_x, xnb)
    grad_end(0, g_qkv)

    @pl.when(in_column)
    def _():
        got(yr_proj.at[0], IDS.gy[3])
        total = g_proj[z].astype(f32) + yr_proj[0].astype(f32)
        for k in (1, 2, 3):
            got(zr_proj.at[k - 1], IDS.gz[3] + k - 1)
            total = total + zr_proj[k - 1].astype(f32)
        p_out[...] = total.astype(bf16)
        rc(p_out, p_out, IDS.gf[3], xnb).start()

    grad_out(1)
    got(group(c, 1 - x), IDS.end_x)
    send(E.at[pl.ds(c * 16, 16)], E.at[pl.ds(c * 16, 16)], IDS.end_c, mate)

    @pl.when(jnp.logical_not(in_column))
    def _():
        got(p_out, IDS.gf[3])

    leave(p_out[...].astype(f32), oproj)
    got(E.at[pl.ds((1 - c) * 16, 16)], IDS.end_c)

    act_all = pick_columns(lambda piece: S[:, piece, :].astype(bf16))[:, :72]
    for section in range(6):
        rows = E[:, section, :]
        leave(dot_tn(act_all, rows), columns_of(oada, section))
        osum[section : section + 1, :] = jnp.sum(rows.astype(f32), axis=0, keepdims=True)
    for section in (6, 7):
        osum[section : section + 1, :] = jnp.sum(E[:, section, :].astype(f32), axis=0, keepdims=True)
    for section in (8, 9):
        for quarter in range(4):
            start = ((quarter % 2) * 2 + quarter // 2) * 8
            at = 8 + 4 * (section - 8) + quarter
            osum[at : at + 1, :] = jnp.sum(
                E[start : start + 8, section, :].astype(f32), axis=0, keepdims=True
            )
    grad_out(0)
    for copy in out_copies[-len(slots) :]:
        copy.wait()
    for copy in row_copies:
        copy.wait()
    for src, ident, _ in pending:
        sent(src, ident)
    for wanted, part, ident in relays:

        @pl.when(wanted)
        def _(part=part, ident=ident):
            sent(part, ident)


    @pl.when(in_column)
    def _():
        for k in (1, 2, 3):
            sent(p_out, IDS.gz[3] + k - 1)
        sent(p_out, IDS.gf[3])

    @pl.when(jnp.logical_not(in_column))
    def _():
        for k in range(4):
            sent(p_out, IDS.gy[3] + k)


def one_kernel(
    tokens,
    cond,
    segment_ids,
    ada_weight,
    ada_bias,
    qkv_weight,
    qv_bias,
    proj_weight,
    proj_bias,
    fc1_weight,
    fc1_bias,
    fc2_weight,
    fc2_bias,
    out_grad,
):
    fsdp_at = lax.axis_index("fsdp")
    cond_float = cond[0].astype(f32)
    cond_act = (cond_float / (1.0 + jnp.exp(-cond_float))).astype(bf16).astype(f32)
    blank = lambda count: jnp.zeros((count,), f32)
    small = jnp.concatenate(
        [
            cond_act,
            qv_bias.astype(f32),
            proj_bias.astype(f32),
            fc2_bias.astype(f32),
            blank(96),
            fc1_bias.astype(f32),
            blank(96),
            segment_ids[0].astype(f32),
            blank(128 + 768),
        ]
    ).reshape(8, 384)
    adab = lax.dynamic_update_slice_in_dim(
        blank(8 * WIDTH), ada_bias.astype(f32), fsdp_at * 432, 0
    ).reshape(8, WIDTH)
    wfc2 = fc2_weight.reshape(4, 72, WIDTH)
    vmem = pl.BlockSpec(memory_space=pltpu.VMEM)
    anywhere = pl.BlockSpec(memory_space=pl.ANY)
    outside = pl.BlockSpec(memory_space=pltpu.HBM)
    shape = jax.ShapeDtypeStruct
    scratch = [pltpu.VMEM(dims, kind) for dims, kind in SCRATCH]
    out, tgrad, oada, oqkv, oproj, ofc1, ofc2, osum = pl.pallas_call(
        block_kernel,
        out_shape=(
            shape((SEQ, WIDTH), bf16),
            shape((SEQ, WIDTH), bf16),
            shape((72, 6 * WIDTH), f32),
            shape((72, 3 * WIDTH), f32),
            shape((72, WIDTH), f32),
            shape((72, HIDDEN), f32),
            shape((4, 72, WIDTH), f32),
            shape((16, WIDTH), f32),
        ),
        in_specs=[vmem, vmem, vmem, vmem, vmem, vmem, anywhere, vmem, anywhere],
        out_specs=(outside,) * 7 + (vmem,),
        scratch_shapes=scratch
        + [
            pltpu.SemaphoreType.DMA((ID_COUNT,)),
            pltpu.SemaphoreType.DMA((ID_COUNT,)),
            pltpu.SemaphoreType.DMA((22,)),
        ],
        compiler_params=pltpu.CompilerParams(
            collective_id=0, has_side_effects=True, vmem_limit_bytes=67043328
        ),
        name="whole_block",
    )(tokens[0], out_grad[0], small, ada_weight, adab, qkv_weight, proj_weight, fc1_weight, wfc2)
    def mine(vector, count):
        return lax.dynamic_slice_in_dim(vector, fsdp_at * count, count, 0)

    by_head = osum[12:16, :QKV].reshape(4, 3, 4, 72).transpose(1, 2, 0, 3).reshape(3 * WIDTH)
    return (
        out[None],
        tgrad[None],
        oada,
        mine(osum[:6].reshape(-1), 432),
        oqkv,
        mine(jnp.concatenate([by_head[:WIDTH], by_head[2 * WIDTH :]]), 144),
        oproj,
        mine(osum[7], 72),
        ofc1,
        mine(osum[8:12].reshape(4, 16, 72).transpose(1, 0, 2).reshape(-1), 288),
        ofc2.reshape(288, WIDTH),
        mine(osum[6], 72),
    )


def solution(mesh):
    in_specs = (
        P(("fsdp", "dp"), None, None),
        P(("fsdp", "dp"), None),
        P(("fsdp", "dp"), None),
        P("fsdp", None),
        P("fsdp"),
        P("fsdp", None),
        P("fsdp"),
        P("fsdp", None),
        P("fsdp"),
        P("fsdp", None),
        P("fsdp"),
        P("fsdp", None),
        P("fsdp"),
        P(("fsdp", "dp"), None, None),
    )
    out_specs = (
        P(("fsdp", "dp"), None, None),
        P(("fsdp", "dp"), None, None),
        P("fsdp", None),
        P("fsdp"),
        P("fsdp", None),
        P("fsdp"),
        P("fsdp", None),
        P("fsdp"),
        P("fsdp", None),
        P("fsdp"),
        P("fsdp", None),
        P("fsdp"),
    )
    fits = (mesh.shape["fsdp"], mesh.shape["dp"]) == (16, 2)
    return jax.shard_map(
        one_kernel if fits else general_form, mesh=mesh, in_specs=in_specs, out_specs=out_specs, check_vma=False
    )
```
